512 devices in a mesh: section: 8 (over x, core), dp: 16 (over z), tensor: 4 (over y).
Axes of the slice: x: 4, y: 4, z: 16, core: 2. Of those that a mesh axis runs over, the one named last changes fastest.
Arguments:
- arrived: bfloat16 [16384, 8192], P(('section', 'dp'), 'tensor'), may hold values from -10 to 10
- cot_later: bfloat16 [16384, 8192], P(('section', 'dp'), 'tensor'), may hold values from -6 to 6
- q_base: bfloat16 [2, 16384, 8192], P(None, ('section', 'dp'), 'tensor'), may hold values from -121 to 121
- k_base: bfloat16 [2, 16384, 1024], P(None, ('section', 'dp'), 'tensor'), may hold values from -7 to 7
- v_base: bfloat16 [2, 16384, 1024], P(None, ('section', 'dp'), 'tensor'), may hold values from -6 to 6
- gains: float32 [16, 8192], P('section', 'tensor'), may hold values from 0.5 to 1.5
- parents: int32 [16384], P(('section', 'dp')), may hold values from -1 to 126, as said below
- a_query: bfloat16 [16, 8192, 128], P('section', ('tensor', 'dp')), may hold values from -0.0625 to 0.0625
- b_query: bfloat16 [16, 128, 8192], P('section', 'dp', 'tensor'), may hold values from -0.5 to 0.5
- a_out: bfloat16 [16, 8192, 128], P('section', ('tensor', 'dp')), may hold values from -0.0625 to 0.0625
- b_out: bfloat16 [16, 128, 8192], P('section', 'dp', 'tensor'), may hold values from -0.5 to 0.5
Outputs:
- section_out: bfloat16 [16384, 8192], P(('section', 'dp'), 'tensor')
- cot_send: bfloat16 [16384, 8192], P(('section', 'dp'), 'tensor')
- grad_a_query: float32 [16, 8192, 128], P('section', ('tensor', 'dp'))
- grad_b_query: float32 [16, 128, 8192], P('section', 'dp', 'tensor')
- grad_a_out: float32 [16, 8192, 128], P('section', ('tensor', 'dp'))
- grad_b_out: float32 [16, 128, 8192], P('section', 'dp', 'tensor')
The draws below stay inside these ranges and needn't reach their ends.
Inputs may be any that keep to these rules, and one draw needn't show every extreme that they name: `parents`: within each block of 128 tokens the first token's parent is -1 and every other token's parent is an earlier index of the same block, at most 12 before it.
All inputs are finite; a program needn't handle non-finite values.
Results may differ from the reference program's by a relative error of at most 0.04.
Values may be sent and summed in bfloat16 or wider, within the bound.
No kernel may reach another device: no remote copies, remote signals or barrier semaphores. Data moves between devices by JAX's collectives and lax.ppermute only.
A program may use at most 64 MiB of HBM per device.

```python
import jax
import jax.numpy as jnp
from jax import lax

D = 8192
HEADS = 64
KV_HEADS = 8
HEAD_DIM = 128
RANK = 128
SECTION_LAYERS = 2
TOK_DEV = 128
TOKENS = 16384
LAYERS_ALL = 16
N_SECTION = 8
N_DP = 16


def drawn_pair(key):
    groups = HEADS // KV_HEADS
    key_rows = jnp.clip(jax.random.normal(jax.random.fold_in(key, 31), (SECTION_LAYERS, TOKENS, KV_HEADS, HEAD_DIM), jnp.float32), -6.0, 6.0)
    query_rows = jnp.clip(jax.random.normal(jax.random.fold_in(key, 32), (SECTION_LAYERS, TOKENS, KV_HEADS, groups, HEAD_DIM), jnp.float32), -6.0, 6.0)
    return (query_rows.reshape(SECTION_LAYERS, TOKENS, -1), key_rows.reshape(SECTION_LAYERS, TOKENS, -1))


def draw_q_base(key, part):
    return drawn_pair(key)[0].astype(jnp.bfloat16)


def draw_k_base(key, part):
    return drawn_pair(key)[1].astype(jnp.bfloat16)


def draw_arrived(key, part):
    column = jnp.arange(D, dtype=jnp.float32) / (D - 1)
    spread = 0.5 * 2.5 ** column
    values = jnp.clip(jax.random.normal(jax.random.fold_in(key, 42), (TOKENS, D), jnp.float32), -6.0, 6.0)
    return (values * spread[None, :]).astype(jnp.bfloat16)


def draw_parents(key, part):
    position = jnp.arange(TOKENS, dtype=jnp.int32)
    local_index = position % TOK_DEV
    chooser = jax.random.randint(jax.random.fold_in(key, 21), (TOKENS,), 0, 8)
    longer = jax.random.randint(jax.random.fold_in(key, 22), (TOKENS,), 2, 13)
    jump_size = jnp.where(chooser < 6, 1, longer)
    jump_size = jnp.where(position % 61 == 7, 1, jump_size)
    jump_size = jnp.where(local_index == TOK_DEV - 1, 1, jump_size)
    jump_size = jnp.minimum(jump_size, local_index)
    return jnp.where(local_index == 0, -1, local_index - jump_size).astype(jnp.int32)


def levels(stream_key, shape, split, smallest, top_value):
    factor_of, own = 1.0, jax.random.fold_in(stream_key, 6)
    for dim, shards_of in split:
        steps = jnp.exp(jax.random.uniform(jax.random.fold_in(own, dim), (shards_of,), jnp.float32, smallest / len(split), top_value / len(split)))
        factor_of = factor_of * jnp.repeat(steps, shape[dim] // shards_of).reshape([-1 if axis == dim else 1 for axis in range(len(shape))])
    return factor_of


def bell_draw(rng, extent, deviation, bound, shards=(), kind=jnp.bfloat16):
    factor_of = levels(rng, extent, shards, -0.22, 0.18) if shards else 1.0
    drawn = jax.random.normal(rng, extent, jnp.float32) * deviation * factor_of
    return jnp.minimum(jnp.maximum(drawn, -bound), bound).astype(kind)


def setup_inputs(seed: int = 0) -> dict:
    splits = jax.random.split(jax.random.key(seed), 12)
    arrived = draw_arrived(jax.random.fold_in(splits[11], 71), 0)
    cot_later = bell_draw(splits[1], (TOKENS, D), 1.0, 6.0, ((0, 128), (1, 4)))
    q_base = draw_q_base(jax.random.fold_in(splits[11], 71), 0)
    k_base = draw_k_base(jax.random.fold_in(splits[11], 71), 0)
    v_base = bell_draw(splits[4], (SECTION_LAYERS, TOKENS, KV_HEADS * HEAD_DIM), 1.0, 6.0, ((1, 128), (2, 4)))
    gains = jnp.clip(0.5 + 1.0 * jax.random.uniform(splits[5], (LAYERS_ALL, D), jnp.float32) ** levels(splits[5], (LAYERS_ALL, D), ((0, 8), (1, 4)), -0.2, 0.2), 0.5, 1.5)
    parents = draw_parents(jax.random.fold_in(splits[11], 71), 0)
    a_query = bell_draw(splits[7], (LAYERS_ALL, D, RANK), D ** -0.5, 0.0625, ((0, 8), (1, 64)))
    b_query = bell_draw(splits[8], (LAYERS_ALL, RANK, HEADS * HEAD_DIM), RANK ** -0.5, 0.5, ((0, 8), (1, 16), (2, 4)))
    a_out = bell_draw(splits[9], (LAYERS_ALL, HEADS * HEAD_DIM, RANK), (HEADS * HEAD_DIM) ** -0.5, 0.0625, ((0, 8), (1, 64)))
    b_out = bell_draw(splits[10], (LAYERS_ALL, RANK, D), RANK ** -0.5, 0.5, ((0, 8), (1, 16), (2, 4)))
    return {"arrived": arrived, "cot_later": cot_later, "q_base": q_base, "k_base": k_base, "v_base": v_base, "gains": gains, "parents": parents, "a_query": a_query, "b_query": b_query, "a_out": a_out, "b_out": b_out}


EPSILON = 1e-05

def rounded(value):
    return lax.optimization_barrier(value.astype(jnp.bfloat16)).astype(jnp.float32)

def contract_rows(left, right):
    return lax.dot_general(left, right, (((0,), (0,)), ((), ())), preferred_element_type=jnp.float32)

def contract_cols(left, right):
    return lax.dot_general(left, right, (((1,), (1,)), ((), ())), preferred_element_type=jnp.float32)

def tree_mask(parent_links):
    token_count = parent_links.shape[0]
    position = jnp.arange(token_count, dtype=jnp.int32)
    linked = (position[:, None] == position[None, :]) | (parent_links[:, None] == position[None, :])
    reached = linked.astype(jnp.bfloat16)
    for doubling in range(max(1, (token_count - 1).bit_length())):
        reached = jnp.minimum(jnp.dot(reached, reached, preferred_element_type=jnp.float32), 1.0).astype(jnp.bfloat16)
    return reached > 0.5

def attend(queries, key_rows, value_rows, allowed):
    token_count = queries.shape[0]
    groups = key_rows.shape[1] // HEAD_DIM
    query_heads = queries.astype(jnp.float32).reshape(token_count, groups, -1, HEAD_DIM)
    key_heads = key_rows.astype(jnp.float32).reshape(token_count, groups, HEAD_DIM)
    value_heads = value_rows.astype(jnp.float32).reshape(token_count, groups, HEAD_DIM)
    scores = jnp.einsum('tgjd,ugd->gjtu', query_heads, key_heads) * HEAD_DIM ** (-0.5)
    scores = jnp.where(allowed[None, None], scores, -1e+30)
    highest = lax.optimization_barrier(jnp.max(scores, axis=-1, keepdims=True))
    weights = jnp.exp(scores - highest)
    probability = weights / lax.optimization_barrier(jnp.sum(weights, axis=-1, keepdims=True))
    mixed_out = jnp.einsum('gjtu,ugd->tgjd', rounded(probability), value_heads)
    return (probability, mixed_out.reshape(token_count, -1).astype(jnp.bfloat16))

def attend_back(back_mixed, probability, key_rows, value_rows):
    token_count = back_mixed.shape[0]
    groups = key_rows.shape[1] // HEAD_DIM
    back_heads = back_mixed.astype(jnp.float32).reshape(token_count, groups, -1, HEAD_DIM)
    key_heads = key_rows.astype(jnp.float32).reshape(token_count, groups, HEAD_DIM)
    value_heads = value_rows.astype(jnp.float32).reshape(token_count, groups, HEAD_DIM)
    back_prob = jnp.einsum('tgjd,ugd->gjtu', back_heads, value_heads)
    back_scores = probability * (back_prob - lax.optimization_barrier(jnp.sum(probability * back_prob, axis=-1, keepdims=True)))
    back_query = jnp.einsum('gjtu,ugd->tgjd', rounded(back_scores), key_heads) * HEAD_DIM ** (-0.5)
    return back_query.reshape(token_count, -1).astype(jnp.bfloat16)

def forward_layer(hidden, gain_row, adapter_set, query_base, key_rows, value_rows, allowed):
    down_query, up_query, down_output, up_output = adapter_set
    mean_square = lax.optimization_barrier(jnp.sum(hidden * hidden, axis=1)) / D
    scale_rows = lax.rsqrt(mean_square + EPSILON)
    unscaled = (hidden * gain_row[None, :]).astype(jnp.bfloat16)
    projected = jnp.dot(unscaled, down_query, preferred_element_type=jnp.float32)
    rank_query = (scale_rows[:, None] * projected).astype(jnp.bfloat16)
    normed = (hidden * scale_rows[:, None] * gain_row[None, :]).astype(jnp.bfloat16)
    queries = (query_base.astype(jnp.float32) + jnp.dot(rank_query, up_query, preferred_element_type=jnp.float32)).astype(jnp.bfloat16)
    probability, attended = attend(queries, key_rows, value_rows, allowed)
    rank_output = jnp.dot(attended, down_output, preferred_element_type=jnp.float32).astype(jnp.bfloat16)
    hidden_next = hidden + jnp.dot(rank_output, up_output, preferred_element_type=jnp.float32)
    return (hidden_next, (hidden, scale_rows, normed, projected, rank_query, probability, attended, rank_output))

def backward_layer(gradient, kept_values, gain_row, adapter_set, key_rows, value_rows):
    hidden, scale_rows, normed, projected, rank_query, probability, attended, rank_output = kept_values
    down_query, up_query, down_output, up_output = adapter_set
    grad_bf = gradient.astype(jnp.bfloat16)
    term_b_out = contract_rows(rank_output, grad_bf)
    back_rank_output = contract_cols(grad_bf, up_output).astype(jnp.bfloat16)
    term_a_out = contract_rows(attended, back_rank_output)
    back_attended = contract_cols(back_rank_output, down_output).astype(jnp.bfloat16)
    back_query = attend_back(back_attended, probability, key_rows, value_rows)
    term_b_query = contract_rows(rank_query, back_query)
    back_rank_query = contract_cols(back_query, up_query).astype(jnp.bfloat16)
    term_a_query = contract_rows(normed, back_rank_query)
    gained = gain_row[None, :] * contract_cols(back_rank_query, down_query)
    along_norm = lax.optimization_barrier(jnp.sum(back_rank_query.astype(jnp.float32) * projected, axis=1)) / D
    gradient_next = gradient + scale_rows[:, None] * gained - hidden * (scale_rows ** 3 * along_norm)[:, None]
    return (gradient_next, (term_a_query, term_b_query, term_a_out, term_b_out))

def reference(arrived, cot_later, q_base, k_base, v_base, gains, parents, a_query, b_query, a_out, b_out):
    block_shape = (N_SECTION, N_DP, TOK_DEV)
    section_inputs = jnp.roll(arrived.reshape(block_shape + (D,)), 1, axis=0)
    section_returns = jnp.roll(cot_later.reshape(block_shape + (D,)), -1, axis=0)
    query_blocks = q_base.reshape((SECTION_LAYERS,) + block_shape + (HEADS * HEAD_DIM,))
    key_blocks = k_base.reshape((SECTION_LAYERS,) + block_shape + (KV_HEADS * HEAD_DIM,))
    value_blocks = v_base.reshape((SECTION_LAYERS,) + block_shape + (KV_HEADS * HEAD_DIM,))
    parent_blocks = parents.reshape(block_shape)
    outputs_hidden = []
    outputs_back = []
    grad_lists = ([], [], [], [])
    for section_index in range(N_SECTION):
        first_layer = section_index * SECTION_LAYERS
        section_gains = gains[first_layer:first_layer + SECTION_LAYERS]
        adapter_sets = [(a_query[first_layer + layer_index], b_query[first_layer + layer_index], a_out[first_layer + layer_index], b_out[first_layer + layer_index]) for layer_index in range(SECTION_LAYERS)]

        def one_block(totals, pieces, section_gains=section_gains, adapter_sets=adapter_sets):
            section_input, cot_block, query_base, key_base, value_base, parent_links = pieces
            allowed = tree_mask(parent_links)
            hidden = section_input.astype(jnp.float32)
            kept_list = []
            for layer_index in range(SECTION_LAYERS):
                hidden, kept_values = forward_layer(hidden, section_gains[layer_index], adapter_sets[layer_index], query_base[layer_index], key_base[layer_index], value_base[layer_index], allowed)
                kept_list.append(kept_values)
            gradient = cot_block.astype(jnp.float32)
            partials = [None] * SECTION_LAYERS
            for layer_index in reversed(range(SECTION_LAYERS)):
                gradient, partials[layer_index] = backward_layer(gradient, kept_list[layer_index], section_gains[layer_index], adapter_sets[layer_index], key_base[layer_index], value_base[layer_index])
            new_totals = tuple((totals[member] + jnp.stack([rounded(partials[layer_index][member]) for layer_index in range(SECTION_LAYERS)]) for member in range(4)))
            return (new_totals, (hidden.astype(jnp.bfloat16), gradient.astype(jnp.bfloat16)))
        start_totals = (jnp.zeros((SECTION_LAYERS, D, RANK), jnp.float32), jnp.zeros((SECTION_LAYERS, RANK, HEADS * HEAD_DIM), jnp.float32), jnp.zeros((SECTION_LAYERS, HEADS * HEAD_DIM, RANK), jnp.float32), jnp.zeros((SECTION_LAYERS, RANK, D), jnp.float32))
        pieces = (section_inputs[section_index], section_returns[section_index], jnp.moveaxis(query_blocks[:, section_index], 0, 1), jnp.moveaxis(key_blocks[:, section_index], 0, 1), jnp.moveaxis(value_blocks[:, section_index], 0, 1), parent_blocks[section_index])
        totals, (block_hidden, block_back) = lax.scan(one_block, start_totals, pieces)
        outputs_hidden.append(block_hidden.reshape(N_DP * TOK_DEV, D))
        outputs_back.append(block_back.reshape(N_DP * TOK_DEV, D))
        for member in range(4):
            grad_lists[member].append(totals[member])
    return (jnp.concatenate(outputs_hidden, axis=0), jnp.concatenate(outputs_back, axis=0), jnp.concatenate(grad_lists[0], axis=0), jnp.concatenate(grad_lists[1], axis=0), jnp.concatenate(grad_lists[2], axis=0), jnp.concatenate(grad_lists[3], axis=0))
```

```python
import functools

import jax
import jax.numpy as jnp
from jax import lax
from jax.experimental import pallas as pl
from jax.experimental.pallas import tpu as pltpu
from jax.sharding import PartitionSpec as P

D = 8192
HEAD_DIM = 128
EPSILON = 1e-05
F32 = jnp.float32
BF16 = jnp.bfloat16
VMEM_LIMIT = 12 << 20
A_OUT0, B_OUT0, A_QUERY1, B_OUT1, B_QUERY1, A_OUT1 = range(6)


def from_behind(value, axis, steps):
    count = lax.axis_size(axis)
    pairs = [(source, (source + steps) % count) for source in range(count)]
    return lax.ppermute(value, axis, pairs)


def dot(left, right):
    return jnp.dot(left, right, preferred_element_type=F32)


def dot_rows(left, right):
    return lax.dot_general(left, right, (((0,), (0,)), ((), ())), preferred_element_type=F32)


def dot_cols(left, right):
    return lax.dot_general(left, right, (((1,), (1,)), ((), ())), preferred_element_type=F32)


def row_sum(value):
    return jnp.sum(value, axis=1, keepdims=True)


def kernel_call(body, out_shape, operands, flops=4e8):
    size = sum(x.size * x.dtype.itemsize for x in (*operands, *out_shape))
    return pl.pallas_call(
        body,
        out_shape=out_shape,
        in_specs=[pl.BlockSpec(memory_space=pltpu.VMEM)] * len(operands),
        out_specs=[pl.BlockSpec(memory_space=pltpu.VMEM)] * len(out_shape),
        compiler_params=pltpu.CompilerParams(vmem_limit_bytes=VMEM_LIMIT),
        cost_estimate=pl.CostEstimate(flops=int(flops), bytes_accessed=size, transcendentals=0),
    )(*operands)


def shape(dims, dtype):
    return jax.ShapeDtypeStruct(dims, dtype)


def pack_up(block):
    rows, width = block.shape
    return block.reshape(rows, width // 128, 128).transpose(1, 0, 2).reshape(-1, 128)


def unpack_up(block, rows):
    tiles = block.shape[0] // rows
    return block.reshape(tiles, rows, 128).transpose(1, 0, 2).reshape(rows, tiles * 128)


def read_down(stack_ref, member):
    value = stack_ref[:, member]
    return value.reshape(-1, 128)


def read_up(stack_ref, member):
    count, _, length, _ = stack_ref.shape
    rows = 128 // count
    columns = []
    for pair in range(length // (2 * rows)):
        slab = stack_ref[:, member, pair * 2 * rows : (pair + 1) * 2 * rows, :].astype(F32)
        for half in range(2):
            columns.append(
                slab[:, half * rows : (half + 1) * rows, :].reshape(128, 128).astype(BF16)
            )
    return jnp.concatenate(columns, axis=1)


def write_down(stack_ref, member, value):
    count = stack_ref.shape[0]
    stack_ref[:, member] = value.astype(BF16).reshape(count, -1, 128)


def write_up(stack_ref, member, value):
    count, _, length, _ = stack_ref.shape
    rows = 128 // count
    for pair in range(length // (2 * rows)):
        halves = [
            value[:, (2 * pair + half) * 128 : (2 * pair + half + 1) * 128].reshape(
                count, rows, 128
            )
            for half in range(2)
        ]
        stack_ref[:, member, pair * 2 * rows : (pair + 1) * 2 * rows, :] = jnp.concatenate(
            halves, axis=1
        ).astype(BF16)


def to_column(row):
    lane = lax.broadcasted_iota(jnp.int32, (128, 128), 1)
    line = lax.broadcasted_iota(jnp.int32, (128, 128), 0)
    return row_sum(jnp.where(lane == line, jnp.broadcast_to(row, (128, 128)), 0.0))


def mask_body(parent_ref, mask_ref):
    lane = lax.broadcasted_iota(jnp.int32, (128, 128), 1)
    line = lax.broadcasted_iota(jnp.int32, (128, 128), 0)
    linked = (lane == line) | (parent_ref[...] == lane)
    reached = jnp.where(linked, 1.0, 0.0).astype(BF16)
    for _ in range(7):
        reached = jnp.minimum(dot(reached, reached), 1.0).astype(BF16)
    mask_ref[...] = reached.astype(F32)


def first_body(hidden_ref, gain_ref, down_ref, sent_ref):
    hidden = hidden_ref[...].astype(F32)
    projected = dot((hidden * gain_ref[...]).astype(BF16), down_ref[...])
    ones = jnp.ones((8, hidden.shape[1]), F32)
    squares = lax.dot_general(
        ones,
        hidden * hidden,
        (((1,), (1,)), ((), ())),
        preferred_element_type=F32,
        precision=lax.Precision.HIGHEST,
    )
    for peer in range(sent_ref.shape[0]):
        sent_ref[peer, :128, :] = projected
        sent_ref[peer, 128:, :] = squares


def softmax_of(queries, keys, mask):
    scores = jnp.where(mask > 0.5, dot_cols(queries, keys) * HEAD_DIM ** (-0.5), -1e30)
    weights = jnp.exp(scores - jnp.max(scores, axis=1, keepdims=True))
    return weights / row_sum(weights)


def columns_of(index):
    return slice(index * HEAD_DIM, (index + 1) * HEAD_DIM)


def forward0_body(
    came_ref,
    up_ref,
    query_ref,
    key_ref,
    value_ref,
    mask_ref,
    attended_ref,
    probability_ref,
    rank_ref,
    small_ref,
):
    total = came_ref[0]
    for peer in range(1, came_ref.shape[0]):
        total = total + came_ref[peer]
    projected = total[:128]
    squares = to_column(total[128:129])
    scale = lax.rsqrt(squares / D + EPSILON)
    rank_query = (scale * projected).astype(BF16)
    rank_ref[...] = rank_query
    small_ref[0] = projected
    small_ref[1] = jnp.broadcast_to(scale, (128, 128))
    small_ref[2] = jnp.broadcast_to(squares, (128, 128))
    mask = mask_ref[...]
    heads = query_ref.shape[1] // HEAD_DIM
    groups = key_ref.shape[1] // HEAD_DIM
    for head in range(heads):
        at, shared = columns_of(head), columns_of(head // (heads // groups))
        queries = (query_ref[:, at].astype(F32) + dot(rank_query, up_ref[:, at])).astype(BF16)
        probability = softmax_of(queries, key_ref[:, shared], mask)
        probability_ref[head] = probability
        attended_ref[:, at] = dot(probability.astype(BF16), value_ref[:, shared]).astype(BF16)


def second_body(attended_ref, hidden_ref, cot_ref, gain_ref, stack_ref, sent_ref, kept_ref):
    hidden, gain = hidden_ref[...], gain_ref[...]
    up0 = read_up(stack_ref, B_OUT0)
    down1 = read_down(stack_ref, A_QUERY1)
    cot = cot_ref[...]
    sent_ref[:128, :] = dot(attended_ref[...], read_down(stack_ref, A_OUT0)).astype(BF16)
    sent_ref[128:256, :] = dot((hidden.astype(F32) * gain).astype(BF16), down1).astype(BF16)
    sent_ref[256:384, :] = dot((up0.astype(F32) * gain).astype(BF16), down1).astype(BF16)
    sent_ref[384:512, :] = dot_cols(cot, read_up(stack_ref, B_OUT1)).astype(BF16)
    sent_ref[512:640, :] = dot_cols(hidden, up0).astype(BF16)
    sent_ref[640:, :] = dot_cols(up0, up0).astype(BF16)
    kept_ref[...] = dot_cols(cot, up0).astype(BF16)


def layer1_body(
    came_ref,
    small0_ref,
    kept_ref,
    stack_ref,
    query_ref,
    key_ref,
    value_ref,
    mask_ref,
    sent_ref,
    attended_ref,
    back_query_ref,
    ranks_ref,
    small_ref,
):
    def total(start):
        value = came_ref[0, start : start + 128, :].astype(F32)
        for peer in range(1, came_ref.shape[0]):
            value = value + came_ref[peer, start : start + 128, :].astype(F32)
        return value

    rank_output0 = total(0).astype(BF16)
    wide0 = rank_output0.astype(F32)
    cross = total(256)
    projected = total(128) + dot(rank_output0, cross.astype(BF16))
    back_rank_output = total(384).astype(BF16)
    hidden_up = total(512)
    gram = total(640)
    gram_high = gram.astype(BF16)
    gram_low = (gram - gram_high.astype(F32)).astype(BF16)
    output_gram = dot(rank_output0, gram_high) + dot(rank_output0, gram_low)
    squares = small0_ref[2, :, :1] + row_sum(wide0 * (2.0 * hidden_up + output_gram))
    scale = lax.rsqrt(jnp.maximum(squares, 0.0) / D + EPSILON)
    rank_query = (scale * projected).astype(BF16)
    ranks_ref[0] = rank_output0
    ranks_ref[1] = rank_query
    ranks_ref[2] = back_rank_output
    small_ref[0] = projected
    small_ref[1] = jnp.broadcast_to(scale, (128, 128))
    small_ref[2] = cross
    small_ref[3] = hidden_up + output_gram
    mask = mask_ref[...]
    up_query = read_up(stack_ref, B_QUERY1)
    down_output = read_down(stack_ref, A_OUT1)
    heads = query_ref.shape[1] // HEAD_DIM
    groups = key_ref.shape[1] // HEAD_DIM
    for head in range(heads):
        at, shared = columns_of(head), columns_of(head // (heads // groups))
        keys, values = key_ref[:, shared], value_ref[:, shared]
        queries = (query_ref[:, at].astype(F32) + dot(rank_query, up_query[:, at])).astype(BF16)
        probability = softmax_of(queries, keys, mask)
        attended_ref[:, at] = dot(probability.astype(BF16), values).astype(BF16)
        back_query_ref[:, at] = score_back(
            dot_cols(back_rank_output, down_output[at, :]).astype(BF16), probability, keys, values
        )
    rank_output = dot(attended_ref[...], down_output).astype(BF16)
    back_rank = dot_cols(back_query_ref[...], up_query).astype(BF16)
    for peer in range(sent_ref.shape[0]):
        sent_ref[peer, :128, :] = rank_output
        sent_ref[peer, 128:256, :] = back_rank
        sent_ref[peer, 256:, :] = kept_ref[...]


def score_back(back_attended, probability, keys, values):
    back_probability = dot_cols(back_attended, values)
    back_scores = probability * (back_probability - row_sum(probability * back_probability))
    return (dot(back_scores.astype(BF16), keys) * HEAD_DIM ** (-0.5)).astype(BF16)


def middle_body(
    came_ref,
    ranks_ref,
    small_ref,
    hidden_ref,
    cot_ref,
    gain_ref,
    stack_ref,
    attended0_ref,
    attended1_ref,
    back_query_ref,
    out_ref,
    gradient_ref,
    back_rank_ref,
    terms_ref,
):
    def total(start):
        value = came_ref[0, start : start + 128, :].astype(F32)
        for peer in range(1, came_ref.shape[0]):
            value = value + came_ref[peer, start : start + 128, :].astype(F32)
        return value

    rank_output1 = total(0).astype(BF16)
    back_rank = total(128).astype(BF16)
    gain = gain_ref[...]
    rank_output0, rank_query = ranks_ref[0], ranks_ref[1]
    scale = small_ref[1, :, :1]
    along = row_sum(back_rank.astype(F32) * small_ref[0]) / D
    pull = scale * scale * scale * along
    back_output0 = (
        total(256) + scale * dot_cols(back_rank, small_ref[2].astype(BF16)) - pull * small_ref[3]
    ).astype(BF16)
    back_rank_ref[...] = back_output0
    write_down(terms_ref, A_OUT0, dot_rows(attended0_ref[...], back_output0))
    write_down(terms_ref, A_OUT1, dot_rows(attended1_ref[...], ranks_ref[2]))
    write_up(terms_ref, B_QUERY1, dot_rows(rank_query, back_query_ref[...]))
    cot = cot_ref[...]
    write_up(terms_ref, B_OUT1, dot_rows(rank_output1, cot))
    hidden = hidden_ref[...].astype(F32) + dot(rank_output0, read_up(stack_ref, B_OUT0))
    normed = (hidden * scale * gain).astype(BF16)
    write_down(terms_ref, A_QUERY1, dot_rows(normed, back_rank))
    gained = gain * dot_cols(back_rank, read_down(stack_ref, A_QUERY1))
    gradient = cot.astype(F32) + scale * gained - hidden * pull
    gradient_ref[...] = gradient
    write_up(terms_ref, B_OUT0, dot_rows(rank_output0, gradient.astype(BF16)))
    out_ref[...] = (hidden + dot(rank_output1, read_up(stack_ref, B_OUT1))).astype(BF16)


def backward0_body(
    back_rank_ref,
    stack_ref,
    probability_ref,
    key_ref,
    value_ref,
    up_ref,
    back_query_ref,
    sent_ref,
):
    back_output = back_rank_ref[...]
    down_output = read_down(stack_ref, A_OUT0)
    heads = probability_ref.shape[0]
    groups = key_ref.shape[1] // HEAD_DIM
    for head in range(heads):
        at, shared = columns_of(head), columns_of(head // (heads // groups))
        back_query_ref[:, at] = score_back(
            dot_cols(back_output, down_output[at, :]).astype(BF16),
            probability_ref[head],
            key_ref[:, shared],
            value_ref[:, shared],
        )
    back_rank = dot_cols(back_query_ref[...], up_ref[...]).astype(BF16)
    for peer in range(sent_ref.shape[0]):
        sent_ref[peer] = back_rank


def last_body(
    came_ref,
    small_ref,
    rank_ref,
    back_query_ref,
    hidden_ref,
    gradient_ref,
    gain_ref,
    down_ref,
    cot_ref,
    terms_ref,
):
    value = came_ref[0].astype(F32)
    for peer in range(1, came_ref.shape[0]):
        value = value + came_ref[peer].astype(F32)
    back_rank = value.astype(BF16)
    gain = gain_ref[...]
    scale = small_ref[1, :, :1]
    hidden = hidden_ref[...].astype(F32)
    write_down(terms_ref, 0, dot_rows((hidden * scale * gain).astype(BF16), back_rank))
    write_up(terms_ref, 1, dot_rows(rank_ref[...], back_query_ref[...]))
    along = row_sum(back_rank.astype(F32) * small_ref[0]) / D
    gained = gain * dot_cols(back_rank, down_ref[...])
    cot_ref[...] = (
        gradient_ref[...] + scale * gained - hidden * (scale * scale * scale * along)
    ).astype(BF16)


def swap(value, axis):
    return lax.all_to_all(value, axis, 0, 0, tiled=True)


def on_device(
    arrived, cot_later, q_base, k_base, v_base, gains, parents, a_query, b_query, a_out, b_out
):
    ways = lax.axis_size("tensor")
    count = lax.axis_size("dp")
    rows = b_query.shape[1]
    width = arrived.shape[1]
    heads = width // HEAD_DIM
    block = shape((128, width), BF16)
    hidden = from_behind(arrived, "section", 1)
    shard = jnp.stack(
        [a_out[0], pack_up(b_out[0]), a_query[1], pack_up(b_out[1]), pack_up(b_query[1]), a_out[1]]
    )
    stack = lax.all_gather(shard, "dp", axis=0, tiled=False)
    cot = from_behind(cot_later, "section", -1)
    down0 = lax.all_gather(a_query[0], "dp", axis=0, tiled=True)
    gain0, gain1 = gains[0:1], gains[1:2]

    (mask,) = kernel_call(mask_body, [shape((128, 128), F32)], (parents.reshape(128, 1),), 3e7)
    (sent,) = kernel_call(
        first_body, [shape((ways, 136, 128), F32)], (hidden, gain0, down0), 1e8
    )
    came = swap(sent, "tensor")
    up_block, _ = lax.optimization_barrier((b_query[0], sent))
    up0 = lax.all_gather(up_block, "dp", axis=0, tiled=True)
    attended0, probability, rank_query0, small0 = kernel_call(
        forward0_body,
        [
            block,
            shape((heads, 128, 128), F32),
            shape((128, 128), BF16),
            shape((3, 128, 128), F32),
        ],
        (came, up0, q_base[0], k_base[0], v_base[0], mask),
    )
    sent, kept = kernel_call(
        second_body,
        [shape((768, 128), BF16), shape((128, 128), BF16)],
        (attended0, hidden, cot, gain1, stack),
        5e8,
    )
    came = lax.all_gather(sent, "tensor", axis=0, tiled=False)
    sent, attended1, back_query1, ranks, small1 = kernel_call(
        layer1_body,
        [
            shape((ways, 384, 128), BF16),
            block,
            block,
            shape((3, 128, 128), BF16),
            shape((4, 128, 128), F32),
        ],
        (came, small0, kept, stack, q_base[1], k_base[1], v_base[1], mask),
        8e8,
    )
    came = swap(sent, "tensor")
    section_out, gradient, back_rank_output0, terms = kernel_call(
        middle_body,
        [block, shape((128, width), F32), shape((128, 128), BF16), shape(stack.shape, BF16)],
        (
            came, ranks, small1, hidden, cot, gain1, stack, attended0, attended1, back_query1,
        ),
        6e8,
    )
    reduced = lax.psum_scatter(terms, "dp", scatter_dimension=0, tiled=False)
    back_query0, sent = kernel_call(
        backward0_body,
        [block, shape((ways, 128, 128), BF16)],
        (back_rank_output0, stack, probability, k_base[0], v_base[0], up0),
    )
    came = swap(sent, "tensor")
    cot_send, last_terms = kernel_call(
        last_body,
        [block, shape((count, 2, stack.shape[2], 128), BF16)],
        (came, small0, rank_query0, back_query0, hidden, gradient, gain0, down0),
    )
    last = jnp.sum(swap(last_terms, "dp").astype(F32), axis=0)
    reduced = reduced.astype(F32)
    return (
        section_out,
        cot_send,
        jnp.stack([last[0], reduced[A_QUERY1]]),
        jnp.stack([unpack_up(last[1], rows), unpack_up(reduced[B_QUERY1], rows)]),
        jnp.stack([reduced[A_OUT0], reduced[A_OUT1]]),
        jnp.stack([unpack_up(reduced[B_OUT0], rows), unpack_up(reduced[B_OUT1], rows)]),
    )


def solution(mesh):
    in_specs = (
        P(("section", "dp"), "tensor"),
        P(("section", "dp"), "tensor"),
        P(None, ("section", "dp"), "tensor"),
        P(None, ("section", "dp"), "tensor"),
        P(None, ("section", "dp"), "tensor"),
        P("section", "tensor"),
        P(("section", "dp")),
        P("section", ("tensor", "dp"), None),
        P("section", "dp", "tensor"),
        P("section", ("tensor", "dp"), None),
        P("section", "dp", "tensor"),
    )
    out_specs = (
        P(("section", "dp"), "tensor"),
        P(("section", "dp"), "tensor"),
        P("section", ("tensor", "dp"), None),
        P("section", "dp", "tensor"),
        P("section", ("tensor", "dp"), None),
        P("section", "dp", "tensor"),
    )
    return jax.shard_map(
        on_device, mesh=mesh, in_specs=in_specs, out_specs=out_specs, check_vma=False
    )
```

```python
import jax
import jax.numpy as jnp
from jax import lax
from jax.experimental import pallas as pl
from jax.experimental.pallas import tpu as pltpu
from jax.sharding import PartitionSpec as P

D = 8192
HEAD_DIM = 128
HEADS_AT_ONCE = 4
EPSILON = 1e-05
F32 = jnp.float32
BF16 = jnp.bfloat16
VMEM_LIMIT = 58 << 20
ALL = slice(None)
A_OUT0, B_OUT0, A_QUERY1, B_OUT1, B_QUERY1, A_OUT1 = range(6)
TERM_A_QUERY, TERM_B_QUERY, TERM_A_OUT, TERM_B_OUT = 0, 2, 4, 6


def from_behind(value, axis, steps):
    count = lax.axis_size(axis)
    pairs = [(source, (source + steps) % count) for source in range(count)]
    return lax.ppermute(value, axis, pairs)


def dot(left, right):
    return jnp.dot(left, right, preferred_element_type=F32)


def dot_rows(left, right):
    return lax.dot_general(left, right, (((0,), (0,)), ((), ())), preferred_element_type=F32)


def dot_cols(left, right):
    return lax.dot_general(left, right, (((1,), (1,)), ((), ())), preferred_element_type=F32)


def row_sum(value):
    return jnp.sum(value, axis=1, keepdims=True)


def shape(dims, dtype):
    return jax.ShapeDtypeStruct(dims, dtype)


class Arriving:
    def __init__(self, copy, ref):
        self.copy, self.ref, self.waited = copy, ref, False
        self.shape = ref.shape

    def wait(self):
        if not self.waited:
            self.copy.wait()
            self.waited = True

    def __getitem__(self, at):
        self.wait()
        return self.ref[at]


class Leaving:
    def __init__(self, copy, ref):
        self.copy, self.ref, self.sent = copy, ref, False
        self.shape = ref.shape

    def send(self):
        if not self.sent:
            self.copy.start()
            self.sent = True

    def __setitem__(self, at, value):
        self.ref[at] = value

    def __getitem__(self, at):
        return self.ref[at]


def sliced(dims, at):
    at = at + (ALL,) * (len(dims) - len(at))
    result = []
    for size, entry in zip(dims, at, strict=True):
        if isinstance(entry, slice):
            result.append(len(range(*entry.indices(size))))
    return tuple(result)


def kernel_call(body, ins, outs, flops, alias=None):
    hbm, vmem = pl.BlockSpec(memory_space=pltpu.HBM), pl.BlockSpec(memory_space=pltpu.VMEM)
    scratch, in_count, out_count = [], len(ins), len(outs)
    for index, item in enumerate(ins):
        if isinstance(item, tuple) and index != alias:
            scratch += [pltpu.VMEM(sliced(item[0].shape, at), item[0].dtype) for at in item[1]]
    first_out = len(scratch)
    for item in outs:
        if isinstance(item, tuple):
            scratch += [pltpu.VMEM(sliced(item[0].shape, at), item[0].dtype) for at in item[1]]
    buffers = len(scratch)

    def run(*refs):
        in_refs, out_refs = refs[:in_count], refs[in_count : in_count + out_count]
        places = refs[in_count + out_count :]
        marks = places[buffers] if buffers else None
        used, given, arriving, leaving = 0, [], [], []
        for index, (ref, item) in enumerate(zip(in_refs, ins, strict=True)):
            if index == alias:
                continue
            if not isinstance(item, tuple):
                given.append(ref)
                continue
            for at in item[1]:
                copy = pltpu.make_async_copy(ref.at[at], places[used], marks.at[used])
                copy.start()
                arriving.append(Arriving(copy, places[used]))
                given.append(arriving[-1])
                used += 1
        assert used == first_out
        for ref, item in zip(out_refs, outs, strict=True):
            if not isinstance(item, tuple):
                given.append(ref)
                continue
            for at in item[1]:
                copy = pltpu.make_async_copy(places[used], ref.at[at], marks.at[used])
                leaving.append(Leaving(copy, places[used]))
                given.append(leaving[-1])
                used += 1
        body(*given)
        for item in leaving:
            item.send()
        for item in arriving:
            item.wait()
        for item in leaving:
            item.copy.wait()

    arrays = [item[0] if isinstance(item, tuple) else item for item in ins]
    shapes = [item[0] if isinstance(item, tuple) else item for item in outs]
    size = sum(x.size * x.dtype.itemsize for x in (*arrays, *shapes))
    return pl.pallas_call(
        run,
        out_shape=shapes,
        in_specs=[hbm if isinstance(item, tuple) else vmem for item in ins],
        out_specs=[hbm if isinstance(item, tuple) else vmem for item in outs],
        scratch_shapes=scratch + ([pltpu.SemaphoreType.DMA((buffers,))] if buffers else []),
        input_output_aliases={} if alias is None else {alias: 0},
        compiler_params=pltpu.CompilerParams(vmem_limit_bytes=VMEM_LIMIT),
        cost_estimate=pl.CostEstimate(flops=int(flops), bytes_accessed=size, transcendentals=0),
    )(*arrays)


def whole(value):
    return (value, [(ALL,) * len(value.shape)])


def read_down(ref):
    return ref[...].reshape(-1, 128)


def read_up(ref):
    count, length, _ = ref.shape
    rows = 128 // count
    columns = []
    for pair in range(length // (2 * rows)):
        slab = ref[:, pair * 2 * rows : (pair + 1) * 2 * rows, :].astype(F32)
        for half in range(2):
            columns.append(
                slab[:, half * rows : (half + 1) * rows, :].reshape(128, 128).astype(BF16)
            )
    return jnp.concatenate(columns, axis=1)


def write_down(ref, value):
    ref[...] = value.astype(BF16).reshape(ref.shape)


def write_up(ref, value):
    count, length, _ = ref.shape
    rows = 128 // count
    for pair in range(length // (2 * rows)):
        halves = [
            value[:, (2 * pair + half) * 128 : (2 * pair + half + 1) * 128].reshape(
                count, rows, 128
            )
            for half in range(2)
        ]
        ref[:, pair * 2 * rows : (pair + 1) * 2 * rows, :] = jnp.concatenate(
            halves, axis=1
        ).astype(BF16)


def pack_body(*refs):
    sources, ups, targets = refs[:3], refs[3:6], refs[6:12]
    for ref, place in zip(sources, (A_OUT0, A_QUERY1, A_OUT1), strict=True):
        targets[place][...] = ref[...]
    for ref, place in zip(ups, (B_OUT0, B_OUT1, B_QUERY1), strict=True):
        rows, width = ref.shape
        value = ref[...].astype(F32)
        for pair in range(width // 256):
            halves = [
                value[:, (2 * pair + half) * 128 : (2 * pair + half + 1) * 128]
                for half in range(2)
            ]
            targets[place][pair * 2 * rows : (pair + 1) * 2 * rows, :] = jnp.concatenate(
                halves, axis=0
            ).astype(BF16)


def unpack_body(came, a_query_ref, b_query_ref, a_out_ref, b_out_ref):
    for layer in range(2):
        for ref, place in ((a_query_ref, TERM_A_QUERY), (a_out_ref, TERM_A_OUT)):
            ref[layer] = came[place + layer].astype(F32)
        for ref, place in ((b_query_ref, TERM_B_QUERY), (b_out_ref, TERM_B_OUT)):
            rows, width = ref.shape[1:]
            value = came[place + layer].astype(F32)
            for tile in range(width // 128):
                ref[layer, :, tile * 128 : (tile + 1) * 128] = value[
                    tile * rows : (tile + 1) * rows
                ]


def first_body(hidden_ref, gain_ref, parent_ref, down_ref, sent_ref, bias_ref):
    lane = lax.broadcasted_iota(jnp.int32, (128, 128), 1)
    line = lax.broadcasted_iota(jnp.int32, (128, 128), 0)
    linked = (lane == line) | (jnp.broadcast_to(parent_ref[...], (128, 128)) == line)
    reached = jnp.where(linked, 1.0, 0.0).astype(BF16)
    for _ in range(7):
        reached = jnp.minimum(dot(reached, reached), 1.0).astype(BF16)
    bias_ref[...] = jnp.where(jnp.transpose(reached.astype(F32)) > 0.5, 0.0, -1e30)
    hidden = hidden_ref[...].astype(F32)
    projected = dot((hidden * gain_ref[...]).astype(BF16), down_ref[...])
    squares = lax.dot_general(
        jnp.ones((8, hidden.shape[1]), F32),
        hidden * hidden,
        (((1,), (1,)), ((), ())),
        preferred_element_type=F32,
        precision=lax.Precision.HIGHEST,
    )
    for peer in range(sent_ref.shape[0]):
        sent_ref[peer, :128, :] = projected
        sent_ref[peer, 128:, :] = squares


def to_column(row):
    lane = lax.broadcasted_iota(jnp.int32, (128, 128), 1)
    line = lax.broadcasted_iota(jnp.int32, (128, 128), 0)
    return row_sum(jnp.where(lane == line, jnp.broadcast_to(row, (128, 128)), 0.0))


def total(ref, start=0):
    value = ref[0, start : start + 128, :].astype(F32)
    for peer in range(1, ref.shape[0]):
        value = value + ref[peer, start : start + 128, :].astype(F32)
    return value


def head_blocks(query_ref, key_ref):
    heads = query_ref.shape[-1] // HEAD_DIM
    groups = key_ref.shape[-1] // HEAD_DIM
    share = heads // groups
    return [
        (head, slice((head // share) * HEAD_DIM, (head // share + 1) * HEAD_DIM))
        for head in range(0, heads, HEADS_AT_ONCE)
    ]


def stacked(value, head):
    return jnp.concatenate(
        [
            value[:, (head + k) * HEAD_DIM : (head + k + 1) * HEAD_DIM]
            for k in range(HEADS_AT_ONCE)
        ],
        axis=0,
    )


def spread(ref, head, value):
    for k in range(HEADS_AT_ONCE):
        ref[:, (head + k) * HEAD_DIM : (head + k + 1) * HEAD_DIM] = value[k * 128 : (k + 1) * 128]


def softmax_of(queries, keys, bias):
    scores = dot_cols(queries, keys) * HEAD_DIM ** (-0.5) + bias
    weights = jnp.exp(scores - jnp.max(scores, axis=1, keepdims=True))
    return weights * (1.0 / row_sum(weights))


def score_back(back_attended, probability, keys, values):
    back_probability = dot_cols(back_attended, values)
    back_scores = probability * (back_probability - row_sum(probability * back_probability))
    return (dot(back_scores.astype(BF16), keys) * HEAD_DIM ** (-0.5)).astype(BF16)


def forward0_body(
    came_ref, up_ref, bias_ref, query_ref, key_ref, value_ref, attended_ref, probability_ref,
    rank_ref, small_ref,
):
    projected = total(came_ref)
    squares = came_ref[0, 128:129, :]
    for peer in range(1, came_ref.shape[0]):
        squares = squares + came_ref[peer, 128:129, :]
    squares = to_column(squares)
    scale = lax.rsqrt(squares / D + EPSILON)
    rank_query = (scale * projected).astype(BF16)
    rank_ref[...] = rank_query
    small_ref[0] = projected
    small_ref[1] = jnp.broadcast_to(scale, (128, 128))
    small_ref[2] = jnp.broadcast_to(squares, (128, 128))
    rank_ref.send()
    small_ref.send()
    bias = jnp.concatenate([bias_ref[...]] * HEADS_AT_ONCE, axis=0)
    queries = (query_ref[...].astype(F32) + dot(rank_query, up_ref[...])).astype(BF16)
    for head, shared in head_blocks(query_ref, key_ref):
        probability = softmax_of(stacked(queries, head), key_ref[:, shared], bias)
        probability_ref[head * 128 : (head + HEADS_AT_ONCE) * 128, :] = probability
        spread(
            attended_ref, head, dot(probability.astype(BF16), value_ref[:, shared]).astype(BF16)
        )


def second_body(
    attended_ref, down_output_ref, hidden_ref, up0_ref, down1_ref, cot_ref, up1_ref, gain_ref,
    sent_ref, kept_ref,
):
    sent_ref[:128, :] = dot(attended_ref[...], read_down(down_output_ref)).astype(BF16)
    hidden, gain = hidden_ref[...], gain_ref[...]
    up0 = read_up(up0_ref)
    sent_ref[512:640, :] = dot_cols(hidden, up0).astype(BF16)
    sent_ref[640:, :] = dot_cols(up0, up0).astype(BF16)
    down1 = read_down(down1_ref)
    sent_ref[128:256, :] = dot((hidden.astype(F32) * gain).astype(BF16), down1).astype(BF16)
    sent_ref[256:384, :] = dot((up0.astype(F32) * gain).astype(BF16), down1).astype(BF16)
    cot = cot_ref[...]
    sent_ref[384:512, :] = dot_cols(cot, read_up(up1_ref)).astype(BF16)
    kept_ref[...] = dot_cols(cot, up0).astype(BF16)


def layer1_body(
    came_ref, small0_ref, query_ref, up_ref, key_ref, value_ref, bias_ref, down_ref, kept_ref,
    sent_ref, attended_ref, back_query_ref, ranks_ref, small_ref,
):
    rank_output0 = total(came_ref).astype(BF16)
    cross = total(came_ref, 256)
    projected = total(came_ref, 128) + dot(rank_output0, cross.astype(BF16))
    back_rank_output = total(came_ref, 384).astype(BF16)
    hidden_up = total(came_ref, 512)
    gram = total(came_ref, 640)
    gram_high = gram.astype(BF16)
    gram_low = (gram - gram_high.astype(F32)).astype(BF16)
    output_gram = dot(rank_output0, gram_high) + dot(rank_output0, gram_low)
    squares = small0_ref[2, :, :1] + row_sum(
        rank_output0.astype(F32) * (2.0 * hidden_up + output_gram)
    )
    scale = lax.rsqrt(jnp.maximum(squares, 0.0) / D + EPSILON)
    rank_query = (scale * projected).astype(BF16)
    ranks_ref[0] = rank_output0
    ranks_ref[1] = rank_query
    ranks_ref[2] = back_rank_output
    ranks_ref.send()
    small_ref[0] = projected
    small_ref[1] = jnp.broadcast_to(scale, (128, 128))
    small_ref[2] = cross
    small_ref[3] = hidden_up + output_gram
    small_ref.send()
    bias = jnp.concatenate([bias_ref[...]] * HEADS_AT_ONCE, axis=0)
    up_query = read_up(up_ref)
    queries = (query_ref[...].astype(F32) + dot(rank_query, up_query)).astype(BF16)
    down_output = read_down(down_ref)
    back_attended = dot_cols(back_rank_output, down_output).astype(BF16)
    for head, shared in head_blocks(query_ref, key_ref):
        keys, values = key_ref[:, shared], value_ref[:, shared]
        probability = softmax_of(stacked(queries, head), keys, bias)
        spread(attended_ref, head, dot(probability.astype(BF16), values).astype(BF16))
        spread(
            back_query_ref, head, score_back(stacked(back_attended, head), probability, keys, values)
        )
    attended_ref.send()
    back_query_ref.send()
    rank_output = dot(attended_ref[...], down_output).astype(BF16)
    back_rank = dot_cols(back_query_ref[...], up_query).astype(BF16)
    for peer in range(sent_ref.shape[0]):
        sent_ref[peer, :128, :] = rank_output
        sent_ref[peer, 128:256, :] = back_rank
        sent_ref[peer, 256:, :] = kept_ref[...]


def backward0_body(
    came_ref, small_ref, down_ref, key_ref, value_ref, probability_ref, up_ref,
    sent_ref, back_query_ref, ranks_ref, pull_ref,
):
    back_rank1 = total(came_ref, 128).astype(BF16)
    scale = small_ref[1, :, :1]
    along = row_sum(back_rank1.astype(F32) * small_ref[0]) / D
    pull = scale * scale * scale * along
    back_output = (
        total(came_ref, 256)
        + scale * dot_cols(back_rank1, small_ref[2].astype(BF16))
        - pull * small_ref[3]
    ).astype(BF16)
    ranks_ref[0] = total(came_ref).astype(BF16)
    ranks_ref[1] = back_rank1
    ranks_ref[2] = back_output
    ranks_ref.send()
    pull_ref[...] = jnp.broadcast_to(pull, (128, 128))
    pull_ref.send()
    back_attended = dot_cols(back_output, read_down(down_ref)).astype(BF16)
    for head, shared in head_blocks(back_query_ref, key_ref):
        spread(
            back_query_ref,
            head,
            score_back(
                stacked(back_attended, head),
                probability_ref[head * 128 : (head + HEADS_AT_ONCE) * 128, :],
                key_ref[:, shared],
                value_ref[:, shared],
            ),
        )
    back_query_ref.send()
    back_rank = dot_cols(back_query_ref[...], up_ref[...]).astype(BF16)
    for peer in range(sent_ref.shape[0]):
        sent_ref[peer] = back_rank


def terms_body(
    ranks1_ref, ranks2_ref, small_ref, pull_ref, gain_ref, cot_ref, hidden_ref, up0_ref, down1_ref,
    up1_ref, attended0_ref, attended1_ref, rank0_ref, back_query0_ref, back_query1_ref,
    a_query1, b_query0, b_query1, a_out0, a_out1, b_out0, b_out1, out_ref, gradient_ref,
):
    rank_output0, rank_query1, back_output1 = ranks1_ref[0], ranks1_ref[1], ranks1_ref[2]
    rank_output1, back_rank1, back_output0 = ranks2_ref[0], ranks2_ref[1], ranks2_ref[2]
    cot = cot_ref[...]
    write_up(b_out1, dot_rows(rank_output1, cot))
    b_out1.send()
    gain, scale, pull = gain_ref[...], small_ref[1, :, :1], pull_ref[:, :1]
    hidden = hidden_ref[...].astype(F32) + dot(rank_output0, read_up(up0_ref))
    write_down(a_query1, dot_rows((hidden * scale * gain).astype(BF16), back_rank1))
    a_query1.send()
    gained = gain * dot_cols(back_rank1, read_down(down1_ref))
    gradient = cot.astype(F32) + scale * gained - hidden * pull
    gradient_ref[...] = gradient
    gradient_ref.send()
    write_up(b_out0, dot_rows(rank_output0, gradient.astype(BF16)))
    b_out0.send()
    out_ref[...] = (hidden + dot(rank_output1, read_up(up1_ref))).astype(BF16)
    out_ref.send()
    write_down(a_out0, dot_rows(attended0_ref[...], back_output0))
    a_out0.send()
    write_down(a_out1, dot_rows(attended1_ref[...], back_output1))
    a_out1.send()
    write_up(b_query1, dot_rows(rank_query1, back_query1_ref[...]))
    b_query1.send()
    write_up(b_query0, dot_rows(rank0_ref[...], back_query0_ref[...]))


def last_term_body(came_ref, small_ref, gain_ref, hidden_ref, a_query0):
    normed = (hidden_ref[...].astype(F32) * small_ref[1, :, :1] * gain_ref[...]).astype(BF16)
    write_down(a_query0, dot_rows(normed, total(came_ref).astype(BF16)))


def cot_body(came_ref, small_ref, gain_ref, down_ref, hidden_ref, gradient_ref, cot_ref):
    back_rank = total(came_ref).astype(BF16)
    scale = small_ref[1, :, :1]
    along = row_sum(back_rank.astype(F32) * small_ref[0]) / D
    gained = gain_ref[...] * dot_cols(back_rank, down_ref[...])
    cot_ref[...] = (
        gradient_ref[...]
        + scale * gained
        - hidden_ref[...].astype(F32) * (scale * scale * scale * along)
    ).astype(BF16)


def swap(value, axis):
    return lax.all_to_all(value, axis, 0, 0, tiled=True)


def on_device(
    arrived, cot_later, q_base, k_base, v_base, gains, parents, a_query, b_query, a_out, b_out
):
    ways = lax.axis_size("tensor")
    count = lax.axis_size("dp")
    rows, width = b_query.shape[1], arrived.shape[1]
    length = rows * width // 128
    heads = width // HEAD_DIM
    block = whole(shape((128, width), BF16))
    layer0, layer1 = [(0,)], [(1,)]
    gain0, gain1 = (gains, [(slice(0, 1),)]), (gains, [(slice(1, 2),)])
    factor = [(ALL, member) for member in range(6)]

    (shard,) = kernel_call(
        pack_body,
        [
            (a_out, layer0), (a_query, layer1), (a_out, layer1),
            (b_out, layer0), (b_out, layer1), (b_query, layer1),
        ],
        [(shape((6, length, 128), BF16), [(member,) for member in range(6)])],
        0,
    )
    stack = lax.all_gather(shard, "dp", axis=0, tiled=False)
    hidden = from_behind(arrived, "section", 1)
    cot = from_behind(cot_later, "section", -1)
    down0 = lax.all_gather(a_query[0], "dp", axis=0, tiled=True)
    sent, bias = kernel_call(
        first_body,
        [whole(hidden), gain0, parents.reshape(1, 128), down0],
        [shape((ways, 136, 128), F32), shape((128, 128), F32)],
        1e8,
    )
    came = swap(sent, "tensor")
    up_block, _ = lax.optimization_barrier((b_query[0], sent))
    up0 = lax.all_gather(up_block, "dp", axis=0, tiled=True)
    attended0, probability, rank_query0, small0 = kernel_call(
        forward0_body,
        [came, up0, bias, (q_base, layer0), (k_base, layer0), (v_base, layer0)],
        [
            block,
            whole(shape((heads * 128, 128), F32)),
            whole(shape((128, 128), BF16)),
            whole(shape((3, 128, 128), F32)),
        ],
        4e8,
    )
    sent, kept = kernel_call(
        second_body,
        [
            whole(attended0), (stack, [factor[A_OUT0]]), whole(hidden),
            (stack, [factor[B_OUT0], factor[A_QUERY1]]), whole(cot), (stack, [factor[B_OUT1]]),
            gain1,
        ],
        [shape((768, 128), BF16), shape((128, 128), BF16)],
        5e8,
    )
    came = lax.all_gather(sent, "tensor", axis=0, tiled=False)
    sent, attended1, back_query1, ranks1, small1 = kernel_call(
        layer1_body,
        [
            came, whole(small0), (q_base, layer1), (stack, [factor[B_QUERY1]]), (k_base, layer1),
            (v_base, layer1), bias, (stack, [factor[A_OUT1]]), kept,
        ],
        [
            shape((ways, 384, 128), BF16),
            block,
            block,
            whole(shape((3, 128, 128), BF16)),
            whole(shape((4, 128, 128), F32)),
        ],
        8e8,
    )
    came = swap(sent, "tensor")
    sent, back_query0, ranks2, pull = kernel_call(
        backward0_body,
        [
            came, whole(small1), (stack, [factor[A_OUT0]]), (k_base, layer0), (v_base, layer0),
            whole(probability), whole(up0),
        ],
        [
            shape((ways, 128, 128), BF16),
            block,
            whole(shape((3, 128, 128), BF16)),
            whole(shape((128, 128), F32)),
        ],
        4e8,
    )
    came = swap(sent, "tensor")
    term_shape = shape((count, 8, length, 128), BF16)
    terms, section_out, gradient = kernel_call(
        terms_body,
        [
            whole(ranks1), whole(ranks2), whole(small1), whole(pull), gain1, whole(cot),
            whole(hidden), (stack, [factor[B_OUT0], factor[A_QUERY1], factor[B_OUT1]]),
            whole(attended0), whole(attended1), whole(rank_query0), whole(back_query0),
            whole(back_query1),
        ],
        [
            (
                term_shape,
                [
                    (ALL, member)
                    for member in (
                        TERM_A_QUERY + 1, TERM_B_QUERY, TERM_B_QUERY + 1, TERM_A_OUT,
                        TERM_A_OUT + 1, TERM_B_OUT, TERM_B_OUT + 1,
                    )
                ],
            ),
            block,
            whole(shape((128, width), F32)),
        ],
        1e9,
    )
    (terms,) = kernel_call(
        last_term_body,
        [came, whole(small0), gain0, whole(hidden), whole(terms)],
        [(term_shape, [(ALL, TERM_A_QUERY)])],
        1e8,
        alias=4,
    )
    reduced = lax.psum_scatter(terms, "dp", scatter_dimension=0, tiled=False)
    (cot_send,) = kernel_call(
        cot_body,
        [came, whole(small0), gain0, whole(down0), whole(hidden), whole(gradient)],
        [block],
        1e8,
    )
    grads = kernel_call(
        unpack_body,
        [whole(reduced)],
        [
            whole(shape((2, length, 128), F32)),
            whole(shape((2, rows, width), F32)),
            whole(shape((2, length, 128), F32)),
            whole(shape((2, rows, width), F32)),
        ],
        0,
    )
    return (section_out, cot_send, *grads)


def solution(mesh):
    in_specs = (
        P(("section", "dp"), "tensor"),
        P(("section", "dp"), "tensor"),
        P(None, ("section", "dp"), "tensor"),
        P(None, ("section", "dp"), "tensor"),
        P(None, ("section", "dp"), "tensor"),
        P("section", "tensor"),
        P(("section", "dp")),
        P("section", ("tensor", "dp"), None),
        P("section", "dp", "tensor"),
        P("section", ("tensor", "dp"), None),
        P("section", "dp", "tensor"),
    )
    out_specs = (
        P(("section", "dp"), "tensor"),
        P(("section", "dp"), "tensor"),
        P("section", ("tensor", "dp"), None),
        P("section", "dp", "tensor"),
        P("section", ("tensor", "dp"), None),
        P("section", "dp", "tensor"),
    )
    return jax.shard_map(
        on_device, mesh=mesh, in_specs=in_specs, out_specs=out_specs, check_vma=False
    )
```

```python
import jax
import jax.numpy as jnp
from jax import lax
from jax.experimental import pallas as pl
from jax.experimental.pallas import tpu as pltpu
from jax.sharding import PartitionSpec as P

D = 8192
HEAD_DIM = 128
HEADS_AT_ONCE = 4
EPSILON = 1e-05
F32 = jnp.float32
BF16 = jnp.bfloat16
VMEM_LIMIT = 58 << 20
ALL = slice(None)
A_OUT0, B_OUT0, A_QUERY1, B_OUT1, B_QUERY1, A_OUT1, B_QUERY0 = range(7)
TERM_A_QUERY, TERM_B_QUERY, TERM_A_OUT, TERM_B_OUT = 0, 2, 4, 6


def from_behind(value, axis, steps):
    count = lax.axis_size(axis)
    pairs = [(source, (source + steps) % count) for source in range(count)]
    return lax.ppermute(value, axis, pairs)


def dot(left, right):
    return jnp.dot(left, right, preferred_element_type=F32)


def dot_rows(left, right):
    return lax.dot_general(left, right, (((0,), (0,)), ((), ())), preferred_element_type=F32)


def dot_cols(left, right):
    return lax.dot_general(left, right, (((1,), (1,)), ((), ())), preferred_element_type=F32)


def row_sum(value):
    return jnp.sum(value, axis=1, keepdims=True)


def shape(dims, dtype):
    return jax.ShapeDtypeStruct(dims, dtype)


class Arriving:
    def __init__(self, copy, ref):
        self.copy, self.ref, self.waited = copy, ref, False
        self.shape = ref.shape

    def wait(self):
        if not self.waited:
            self.copy.wait()
            self.waited = True

    def __getitem__(self, at):
        self.wait()
        return self.ref[at]


class Leaving:
    def __init__(self, copies, ref):
        self.copies, self.ref, self.sent = copies, ref, False
        self.shape = ref.shape

    def send(self):
        if not self.sent:
            for copy in self.copies:
                copy.start()
            self.sent = True

    def __setitem__(self, at, value):
        self.ref[at] = value

    def __getitem__(self, at):
        return self.ref[at]


def sliced(dims, at):
    at = at + (ALL,) * (len(dims) - len(at))
    result = []
    for size, entry in zip(dims, at, strict=True):
        if isinstance(entry, slice):
            result.append(len(range(*entry.indices(size))))
    return tuple(result)


def kernel_call(body, ins, outs, flops, alias=None):
    hbm = pl.BlockSpec(memory_space=pltpu.HBM)
    scratch, marks_needed, in_count, out_count = [], 0, len(ins), len(outs)
    for index, (array, slices) in enumerate(ins):
        if index != alias:
            scratch += [pltpu.VMEM(sliced(array.shape, at), array.dtype) for at in slices]
            marks_needed += len(slices)
    for result, slices in outs:
        for at in slices:
            copies = at[0] if isinstance(at[0], tuple) else (at[0],)
            marks_needed += len(copies)
            scratch.append(
                pltpu.VMEM(sliced(result.shape, (copies[0], *at[1:])), result.dtype)
            )

    def run(*refs):
        in_refs, out_refs = refs[:in_count], refs[in_count : in_count + out_count]
        places, marks = refs[in_count + out_count : -1], refs[-1]
        used, mark, given, arriving, leaving = 0, 0, [], [], []
        for index, (ref, (_, slices)) in enumerate(zip(in_refs, ins, strict=True)):
            if index == alias:
                continue
            for at in slices:
                copy = pltpu.make_async_copy(ref.at[at], places[used], marks.at[mark])
                copy.start()
                arriving.append(Arriving(copy, places[used]))
                given.append(arriving[-1])
                used, mark = used + 1, mark + 1
        for ref, (_, slices) in zip(out_refs, outs, strict=True):
            for at in slices:
                copies = []
                for first in at[0] if isinstance(at[0], tuple) else (at[0],):
                    copies.append(
                        pltpu.make_async_copy(
                            places[used], ref.at[(first, *at[1:])], marks.at[mark]
                        )
                    )
                    mark += 1
                leaving.append(Leaving(copies, places[used]))
                given.append(leaving[-1])
                used += 1
        body(*given)
        for item in leaving:
            item.send()
        for item in arriving:
            item.wait()
        for item in leaving:
            for copy in item.copies:
                copy.wait()

    arrays, shapes = [array for array, _ in ins], [result for result, _ in outs]
    size = sum(x.size * x.dtype.itemsize for x in (*arrays, *shapes))
    return pl.pallas_call(
        run,
        out_shape=shapes,
        in_specs=[hbm] * in_count,
        out_specs=[hbm] * out_count,
        scratch_shapes=[*scratch, pltpu.SemaphoreType.DMA((marks_needed,))],
        input_output_aliases={} if alias is None else {alias: 0},
        compiler_params=pltpu.CompilerParams(vmem_limit_bytes=VMEM_LIMIT),
        cost_estimate=pl.CostEstimate(flops=int(flops), bytes_accessed=size, transcendentals=0),
    )(*arrays)


def whole(value):
    return (value, [(ALL,) * len(value.shape)])


def read_down(ref):
    return ref[...].reshape(-1, 128)


def read_up(ref):
    count, length, _ = ref.shape
    rows = 128 // count
    columns = []
    for pair in range(length // (2 * rows)):
        slab = ref[:, pair * 2 * rows : (pair + 1) * 2 * rows, :].astype(F32)
        for half in range(2):
            columns.append(
                slab[:, half * rows : (half + 1) * rows, :].reshape(128, 128).astype(BF16)
            )
    return jnp.concatenate(columns, axis=1)


def write_down(ref, value):
    value = value.astype(BF16)
    size = ref.shape[2] * ref.shape[1] // 128
    for place in range(ref.shape[0]):
        for part in range(size // 128):
            at = place * size + part * 128
            ref[place, part * 128 : (part + 1) * 128, :] = value[:, at : at + 128]


def write_up(ref, value):
    count, length, _ = ref.shape
    rows = 128 // count
    for pair in range(length // (2 * rows)):
        halves = [
            value[:, (2 * pair + half) * 128 : (2 * pair + half + 1) * 128].reshape(
                count, rows, 128
            )
            for half in range(2)
        ]
        ref[:, pair * 2 * rows : (pair + 1) * 2 * rows, :] = jnp.concatenate(
            halves, axis=1
        ).astype(BF16)


def pack_body(*refs):
    sources, ups, targets = refs[:3], refs[3:7], refs[7:14]
    for ref, place in zip(sources, (A_OUT0, A_QUERY1, A_OUT1), strict=True):
        targets[place][...] = ref[...]
    for ref, place in zip(ups, (B_OUT0, B_OUT1, B_QUERY1, B_QUERY0), strict=True):
        rows, width = ref.shape
        value = ref[...].astype(F32)
        for pair in range(width // 256):
            halves = [
                value[:, (2 * pair + half) * 128 : (2 * pair + half + 1) * 128]
                for half in range(2)
            ]
            targets[place][pair * 2 * rows : (pair + 1) * 2 * rows, :] = jnp.concatenate(
                halves, axis=0
            ).astype(BF16)


def unpack_body(came, a_query_ref, b_query_ref, a_out_ref, b_out_ref):
    for layer in range(2):
        for ref, place in ((a_query_ref, TERM_A_QUERY), (a_out_ref, TERM_A_OUT)):
            value = came[place + layer].astype(F32)
            for part in range(value.shape[0] // 128):
                at = slice(part * 128, (part + 1) * 128)
                ref[layer, at, :] = jnp.transpose(value[at])
        for ref, place in ((b_query_ref, TERM_B_QUERY), (b_out_ref, TERM_B_OUT)):
            rows, width = ref.shape[1:]
            value = came[place + layer].astype(F32)
            for tile in range(width // 128):
                ref[layer, :, tile * 128 : (tile + 1) * 128] = value[
                    tile * rows : (tile + 1) * rows
                ]


def first_body(hidden_ref, gain_ref, parent_ref, down_ref, sent_ref, bias_ref):
    lane = lax.broadcasted_iota(jnp.int32, (128, 128), 1)
    line = lax.broadcasted_iota(jnp.int32, (128, 128), 0)
    linked = (lane == line) | (jnp.broadcast_to(parent_ref[...], (128, 128)) == line)
    reached = jnp.where(linked, 1.0, 0.0).astype(BF16)
    for _ in range(7):
        reached = jnp.minimum(dot(reached, reached), 1.0).astype(BF16)
    bias_ref[...] = jnp.where(jnp.transpose(reached.astype(F32)) > 0.5, 0.0, -1e30)
    hidden = hidden_ref[...].astype(F32)
    projected = dot((hidden * gain_ref[...]).astype(BF16), down_ref[...])
    squares = lax.dot_general(
        jnp.ones((8, hidden.shape[1]), F32),
        hidden * hidden,
        (((1,), (1,)), ((), ())),
        preferred_element_type=F32,
        precision=lax.Precision.HIGHEST,
    )
    sent_ref[:128, :] = projected
    sent_ref[128:, :] = squares


def to_column(row):
    lane = lax.broadcasted_iota(jnp.int32, (128, 128), 1)
    line = lax.broadcasted_iota(jnp.int32, (128, 128), 0)
    return row_sum(jnp.where(lane == line, jnp.broadcast_to(row, (128, 128)), 0.0))


def total(ref, start=0):
    value = ref[0, start : start + 128, :].astype(F32)
    for peer in range(1, ref.shape[0]):
        value = value + ref[peer, start : start + 128, :].astype(F32)
    return value


def head_blocks(query_ref, key_ref):
    heads = query_ref.shape[-1] // HEAD_DIM
    groups = key_ref.shape[-1] // HEAD_DIM
    share = heads // groups
    return [
        (head, slice((head // share) * HEAD_DIM, (head // share + 1) * HEAD_DIM))
        for head in range(0, heads, HEADS_AT_ONCE)
    ]


def stacked(value, head):
    return jnp.concatenate(
        [
            value[:, (head + k) * HEAD_DIM : (head + k + 1) * HEAD_DIM]
            for k in range(HEADS_AT_ONCE)
        ],
        axis=0,
    )


def spread(ref, head, value):
    for k in range(HEADS_AT_ONCE):
        ref[:, (head + k) * HEAD_DIM : (head + k + 1) * HEAD_DIM] = value[k * 128 : (k + 1) * 128]


def softmax_of(queries, keys, bias):
    scores = dot_cols(queries, keys) * HEAD_DIM ** (-0.5) + bias
    weights = jnp.exp(scores - jnp.max(scores, axis=1, keepdims=True))
    return weights * (1.0 / row_sum(weights))


def score_back(back_attended, probability, keys, values):
    back_probability = dot_cols(back_attended, values)
    back_scores = probability * (back_probability - row_sum(probability * back_probability))
    return (dot(back_scores.astype(BF16), keys) * HEAD_DIM ** (-0.5)).astype(BF16)


def layer0_body(
    came_ref, query_ref, up_query_ref, key_ref, value_ref, bias_ref, hidden_ref, gain_ref,
    down_output_ref, up0_ref, down1_ref, up1_ref, cot_ref,
    sent_ref, attended_ref, probability_ref, rank_ref, small_ref, kept_ref,
):
    projected = total(came_ref)
    squares = came_ref[0, 128:129, :]
    for peer in range(1, came_ref.shape[0]):
        squares = squares + came_ref[peer, 128:129, :]
    squares = to_column(squares)
    scale = lax.rsqrt(squares / D + EPSILON)
    rank_query = (scale * projected).astype(BF16)
    rank_ref[...] = rank_query
    small_ref[0] = projected
    small_ref[1] = jnp.broadcast_to(scale, (128, 128))
    small_ref[2] = jnp.broadcast_to(squares, (128, 128))
    rank_ref.send()
    small_ref.send()
    bias = jnp.concatenate([bias_ref[...]] * HEADS_AT_ONCE, axis=0)
    queries = (query_ref[...].astype(F32) + dot(rank_query, read_up(up_query_ref))).astype(BF16)
    for head, shared in head_blocks(query_ref, key_ref):
        probability = softmax_of(stacked(queries, head), key_ref[:, shared], bias)
        probability_ref[head * 128 : (head + HEADS_AT_ONCE) * 128, :] = probability
        spread(
            attended_ref, head, dot(probability.astype(BF16), value_ref[:, shared]).astype(BF16)
        )
    probability_ref.send()
    attended_ref.send()
    hidden, gain = hidden_ref[...], gain_ref[...]
    up0, down1, cot = read_up(up0_ref), read_down(down1_ref), cot_ref[...]
    sent_ref[512:640, :] = dot_cols(hidden, up0).astype(BF16)
    sent_ref[640:, :] = dot_cols(up0, up0).astype(BF16)
    sent_ref[128:256, :] = dot((hidden.astype(F32) * gain).astype(BF16), down1).astype(BF16)
    sent_ref[256:384, :] = dot((up0.astype(F32) * gain).astype(BF16), down1).astype(BF16)
    sent_ref[384:512, :] = dot_cols(cot, read_up(up1_ref)).astype(BF16)
    sent_ref[:128, :] = dot(attended_ref[...], read_down(down_output_ref)).astype(BF16)
    sent_ref.send()
    kept_ref[...] = dot_cols(cot, up0).astype(BF16)


def layer1_body(
    came_ref, small0_ref, query_ref, up_ref, key_ref, value_ref, bias_ref, down_ref, kept_ref,
    sent_ref, attended_ref, back_query_ref, ranks_ref, small_ref,
):
    rank_output0 = total(came_ref).astype(BF16)
    cross = total(came_ref, 256)
    projected = total(came_ref, 128) + dot(rank_output0, cross.astype(BF16))
    back_rank_output = total(came_ref, 384).astype(BF16)
    hidden_up = total(came_ref, 512)
    gram = total(came_ref, 640)
    gram_high = gram.astype(BF16)
    gram_low = (gram - gram_high.astype(F32)).astype(BF16)
    output_gram = dot(rank_output0, gram_high) + dot(rank_output0, gram_low)
    squares = small0_ref[2, :, :1] + row_sum(
        rank_output0.astype(F32) * (2.0 * hidden_up + output_gram)
    )
    scale = lax.rsqrt(jnp.maximum(squares, 0.0) / D + EPSILON)
    rank_query = (scale * projected).astype(BF16)
    ranks_ref[0] = rank_output0
    ranks_ref[1] = rank_query
    ranks_ref[2] = back_rank_output
    ranks_ref.send()
    small_ref[0] = projected
    small_ref[1] = jnp.broadcast_to(scale, (128, 128))
    small_ref[2] = cross
    small_ref[3] = hidden_up + output_gram
    small_ref.send()
    bias = jnp.concatenate([bias_ref[...]] * HEADS_AT_ONCE, axis=0)
    up_query = read_up(up_ref)
    queries = (query_ref[...].astype(F32) + dot(rank_query, up_query)).astype(BF16)
    down_output = read_down(down_ref)
    back_attended = dot_cols(back_rank_output, down_output).astype(BF16)
    for head, shared in head_blocks(query_ref, key_ref):
        keys, values = key_ref[:, shared], value_ref[:, shared]
        probability = softmax_of(stacked(queries, head), keys, bias)
        spread(attended_ref, head, dot(probability.astype(BF16), values).astype(BF16))
        spread(
            back_query_ref, head, score_back(stacked(back_attended, head), probability, keys, values)
        )
    attended_ref.send()
    back_query_ref.send()
    rank_output = dot(attended_ref[...], down_output).astype(BF16)
    back_rank = dot_cols(back_query_ref[...], up_query).astype(BF16)
    sent_ref[:128, :] = rank_output
    sent_ref[128:256, :] = back_rank
    sent_ref[256:, :] = kept_ref[...]


def backward0_body(
    came_ref, small_ref, down_ref, key_ref, value_ref, probability_ref, up_ref,
    sent_ref, back_query_ref, ranks_ref, pull_ref,
):
    back_rank1 = total(came_ref, 128).astype(BF16)
    scale = small_ref[1, :, :1]
    along = row_sum(back_rank1.astype(F32) * small_ref[0]) / D
    pull = scale * scale * scale * along
    back_output = (
        total(came_ref, 256)
        + scale * dot_cols(back_rank1, small_ref[2].astype(BF16))
        - pull * small_ref[3]
    ).astype(BF16)
    ranks_ref[0] = total(came_ref).astype(BF16)
    ranks_ref[1] = back_rank1
    ranks_ref[2] = back_output
    ranks_ref.send()
    pull_ref[...] = jnp.broadcast_to(pull, (128, 128))
    pull_ref.send()
    back_attended = dot_cols(back_output, read_down(down_ref)).astype(BF16)
    for head, shared in head_blocks(back_query_ref, key_ref):
        spread(
            back_query_ref,
            head,
            score_back(
                stacked(back_attended, head),
                probability_ref[head * 128 : (head + HEADS_AT_ONCE) * 128, :],
                key_ref[:, shared],
                value_ref[:, shared],
            ),
        )
    back_query_ref.send()
    back_rank = dot_cols(back_query_ref[...], read_up(up_ref)).astype(BF16)
    sent_ref[...] = back_rank


def terms_body(
    ranks1_ref, ranks2_ref, small_ref, pull_ref, gain_ref, cot_ref, hidden_ref, up0_ref, down1_ref,
    up1_ref, attended0_ref, attended1_ref, rank0_ref, back_query0_ref, back_query1_ref,
    a_query1, b_query0, b_query1, a_out0, a_out1, b_out0, b_out1, out_ref, gradient_ref,
):
    rank_output0, rank_query1, back_output1 = ranks1_ref[0], ranks1_ref[1], ranks1_ref[2]
    rank_output1, back_rank1, back_output0 = ranks2_ref[0], ranks2_ref[1], ranks2_ref[2]
    cot = cot_ref[...]
    write_up(b_out1, dot_rows(rank_output1, cot))
    b_out1.send()
    gain, scale, pull = gain_ref[...], small_ref[1, :, :1], pull_ref[:, :1]
    hidden = hidden_ref[...].astype(F32) + dot(rank_output0, read_up(up0_ref))
    write_down(a_query1, dot_rows(back_rank1, (hidden * scale * gain).astype(BF16)))
    a_query1.send()
    gained = gain * dot_cols(back_rank1, read_down(down1_ref))
    gradient = cot.astype(F32) + scale * gained - hidden * pull
    gradient_ref[...] = gradient
    gradient_ref.send()
    write_up(b_out0, dot_rows(rank_output0, gradient.astype(BF16)))
    b_out0.send()
    out_ref[...] = (hidden + dot(rank_output1, read_up(up1_ref))).astype(BF16)
    out_ref.send()
    write_down(a_out0, dot_rows(back_output0, attended0_ref[...]))
    a_out0.send()
    write_down(a_out1, dot_rows(back_output1, attended1_ref[...]))
    a_out1.send()
    write_up(b_query1, dot_rows(rank_query1, back_query1_ref[...]))
    b_query1.send()
    write_up(b_query0, dot_rows(rank0_ref[...], back_query0_ref[...]))


def last_term_body(came_ref, small_ref, gain_ref, hidden_ref, a_query0):
    normed = (hidden_ref[...].astype(F32) * small_ref[1, :, :1] * gain_ref[...]).astype(BF16)
    write_down(a_query0, dot_rows(total(came_ref).astype(BF16), normed))


def cot_body(came_ref, small_ref, gain_ref, down_ref, hidden_ref, gradient_ref, cot_ref):
    back_rank = total(came_ref).astype(BF16)
    scale = small_ref[1, :, :1]
    along = row_sum(back_rank.astype(F32) * small_ref[0]) / D
    gained = gain_ref[...] * dot_cols(back_rank, down_ref[...])
    cot_ref[...] = (
        gradient_ref[...]
        + scale * gained
        - hidden_ref[...].astype(F32) * (scale * scale * scale * along)
    ).astype(BF16)


def swap(value, axis):
    return lax.all_to_all(value, axis, 0, 0, tiled=True)


def on_device(
    arrived, cot_later, q_base, k_base, v_base, gains, parents, a_query, b_query, a_out, b_out
):
    ways = lax.axis_size("tensor")
    count = lax.axis_size("dp")
    rows, width = b_query.shape[1], arrived.shape[1]
    length = rows * width // 128
    heads = width // HEAD_DIM
    block = whole(shape((128, width), BF16))
    ranks = whole(shape((3, 128, 128), BF16))
    layer0, layer1 = [(0,)], [(1,)]
    gain0, gain1 = (gains, [(slice(0, 1),)]), (gains, [(slice(1, 2),)])
    peers = [(tuple(range(ways)),)]

    (shard,) = kernel_call(
        pack_body,
        [
            (a_out, layer0), (a_query, layer1), (a_out, layer1),
            (b_out, layer0), (b_out, layer1), (b_query, layer1), (b_query, layer0),
        ],
        [(shape((7, length, 128), BF16), [(member,) for member in range(7)])],
        0,
    )
    stack = lax.all_gather(shard, "dp", axis=0, tiled=False)

    def factor(*members):
        return (stack, [(ALL, member) for member in members])

    hidden = from_behind(arrived, "section", 1)
    cot = from_behind(cot_later, "section", -1)
    down0 = lax.all_gather(a_query[0], "dp", axis=0, tiled=True)
    sent, bias = kernel_call(
        first_body,
        [whole(hidden), gain0, whole(parents.reshape(1, 128)), whole(down0)],
        [(shape((ways, 136, 128), F32), peers), whole(shape((128, 128), F32))],
        1e8,
    )
    came = swap(sent, "tensor")
    sent, attended0, probability, rank_query0, small0, kept = kernel_call(
        layer0_body,
        [
            whole(came), (q_base, layer0), factor(B_QUERY0), (k_base, layer0), (v_base, layer0),
            whole(bias), whole(hidden), gain1, factor(A_OUT0, B_OUT0, A_QUERY1, B_OUT1),
            whole(cot),
        ],
        [
            whole(shape((768, 128), BF16)),
            block,
            whole(shape((heads * 128, 128), F32)),
            whole(shape((128, 128), BF16)),
            whole(shape((3, 128, 128), F32)),
            whole(shape((128, 128), BF16)),
        ],
        9e8,
    )
    came = lax.all_gather(sent, "tensor", axis=0, tiled=False)
    sent, attended1, back_query1, ranks1, small1 = kernel_call(
        layer1_body,
        [
            whole(came), whole(small0), (q_base, layer1), factor(B_QUERY1), (k_base, layer1),
            (v_base, layer1), whole(bias), factor(A_OUT1), whole(kept),
        ],
        [
            (shape((ways, 384, 128), BF16), peers),
            block,
            block,
            ranks,
            whole(shape((4, 128, 128), F32)),
        ],
        8e8,
    )
    came = swap(sent, "tensor")
    sent, back_query0, ranks2, pull = kernel_call(
        backward0_body,
        [
            whole(came), whole(small1), factor(A_OUT0), (k_base, layer0), (v_base, layer0),
            whole(probability), factor(B_QUERY0),
        ],
        [
            (shape((ways, 128, 128), BF16), peers),
            block,
            ranks,
            whole(shape((128, 128), F32)),
        ],
        4e8,
    )
    came = swap(sent, "tensor")
    term_shape = shape((count, 8, length, 128), BF16)
    made_first = (
        TERM_A_QUERY + 1, TERM_B_QUERY, TERM_B_QUERY + 1, TERM_A_OUT, TERM_A_OUT + 1,
        TERM_B_OUT, TERM_B_OUT + 1,
    )
    terms, section_out, gradient = kernel_call(
        terms_body,
        [
            whole(ranks1), whole(ranks2), whole(small1), whole(pull), gain1, whole(cot),
            whole(hidden), factor(B_OUT0, A_QUERY1, B_OUT1), whole(attended0), whole(attended1),
            whole(rank_query0), whole(back_query0), whole(back_query1),
        ],
        [
            (term_shape, [(ALL, member) for member in made_first]),
            block,
            whole(shape((128, width), F32)),
        ],
        1e9,
    )
    (terms,) = kernel_call(
        last_term_body,
        [whole(came), whole(small0), gain0, whole(hidden), whole(terms)],
        [(term_shape, [(ALL, TERM_A_QUERY)])],
        1e8,
        alias=4,
    )
    reduced = lax.psum_scatter(terms, "dp", scatter_dimension=0, tiled=False)
    (cot_send,) = kernel_call(
        cot_body,
        [whole(came), whole(small0), gain0, whole(down0), whole(hidden), whole(gradient)],
        [block],
        1e8,
    )
    grads = kernel_call(
        unpack_body,
        [whole(reduced)],
        [
            whole(shape((2, length, 128), F32)),
            whole(shape((2, rows, width), F32)),
            whole(shape((2, length, 128), F32)),
            whole(shape((2, rows, width), F32)),
        ],
        0,
    )
    return (section_out, cot_send, *grads)


def solution(mesh):
    in_specs = (
        P(("section", "dp"), "tensor"),
        P(("section", "dp"), "tensor"),
        P(None, ("section", "dp"), "tensor"),
        P(None, ("section", "dp"), "tensor"),
        P(None, ("section", "dp"), "tensor"),
        P("section", "tensor"),
        P(("section", "dp")),
        P("section", ("tensor", "dp"), None),
        P("section", "dp", "tensor"),
        P("section", ("tensor", "dp"), None),
        P("section", "dp", "tensor"),
    )
    out_specs = (
        P(("section", "dp"), "tensor"),
        P(("section", "dp"), "tensor"),
        P("section", ("tensor", "dp"), None),
        P("section", "dp", "tensor"),
        P("section", ("tensor", "dp"), None),
        P("section", "dp", "tensor"),
    )
    return jax.shard_map(
        on_device, mesh=mesh, in_specs=in_specs, out_specs=out_specs, check_vma=False
    )
```

```python
import jax
import jax.numpy as jnp
from jax import lax
from jax.experimental import pallas as pl
from jax.experimental.pallas import tpu as pltpu
from jax.sharding import PartitionSpec as P

D = 8192
HEAD_DIM = 128
HEADS_AT_ONCE = 4
EPSILON = 1e-05
F32 = jnp.float32
BF16 = jnp.bfloat16
VMEM_LIMIT = 20 << 20
ALL = slice(None)
A_OUT0, B_OUT0, A_QUERY1, B_OUT1, B_QUERY1, A_OUT1, B_QUERY0 = range(7)
TERM_A_QUERY, TERM_B_QUERY, TERM_A_OUT, TERM_B_OUT = 0, 2, 4, 6


def from_behind(value, axis, steps):
    count = lax.axis_size(axis)
    pairs = [(source, (source + steps) % count) for source in range(count)]
    return lax.ppermute(value, axis, pairs)


def dot(left, right):
    return jnp.dot(left, right, preferred_element_type=F32)


def dot_rows(left, right):
    return lax.dot_general(left, right, (((0,), (0,)), ((), ())), preferred_element_type=F32)


def dot_cols(left, right):
    return lax.dot_general(left, right, (((1,), (1,)), ((), ())), preferred_element_type=F32)


def row_sum(value):
    return jnp.sum(value, axis=1, keepdims=True)


def shape(dims, dtype):
    return jax.ShapeDtypeStruct(dims, dtype)


class Arriving:
    def __init__(self, copy, ref):
        self.copy, self.ref, self.waited = copy, ref, False
        self.shape = ref.shape

    def wait(self):
        if not self.waited:
            self.copy.wait()
            self.waited = True

    def __getitem__(self, at):
        self.wait()
        return self.ref[at]


class Leaving:
    def __init__(self, copies, ref):
        self.copies, self.ref, self.sent = copies, ref, False
        self.shape = ref.shape

    def send(self):
        if not self.sent:
            for copy in self.copies:
                copy.start()
            self.sent = True

    def __setitem__(self, at, value):
        self.ref[at] = value

    def __getitem__(self, at):
        return self.ref[at]


class Staying:
    def __init__(self, ref):
        self.ref = ref
        self.shape = ref.shape

    def send(self):
        pass

    def __setitem__(self, at, value):
        self.ref[at] = value

    def __getitem__(self, at):
        return self.ref[at]


def sliced(dims, at):
    at = at + (ALL,) * (len(dims) - len(at))
    result = []
    for size, entry in zip(dims, at, strict=True):
        if isinstance(entry, slice):
            result.append(len(range(*entry.indices(size))))
    return tuple(result)


class Near:
    def __init__(self, array, *slices):
        self.array, self.slices = array, slices


def kernel_call(body, ins, outs, flops, alias=None):
    hbm, vmem = pl.BlockSpec(memory_space=pltpu.HBM), pl.BlockSpec(memory_space=pltpu.VMEM)
    scratch, marks_needed, in_count, out_count = [], 0, len(ins), len(outs)
    for index, item in enumerate(ins):
        if index != alias and not isinstance(item, Near):
            scratch += [pltpu.VMEM(sliced(item[0].shape, at), item[0].dtype) for at in item[1]]
            marks_needed += len(item[1])
    for item in outs:
        if not isinstance(item, Near):
            for at in item[1]:
                copies = at[0] if isinstance(at[0], tuple) else (at[0],)
                marks_needed += len(copies)
                scratch.append(
                    pltpu.VMEM(sliced(item[0].shape, (copies[0], *at[1:])), item[0].dtype)
                )

    def run(*refs):
        in_refs, out_refs = refs[:in_count], refs[in_count : in_count + out_count]
        places, marks = refs[in_count + out_count : -1], refs[-1]
        used, mark, given, arriving, leaving = 0, 0, [], [], []
        for index, (ref, item) in enumerate(zip(in_refs, ins, strict=True)):
            if index == alias:
                continue
            if isinstance(item, Near):
                given += [ref.at[at] for at in item.slices] if item.slices else [ref]
                continue
            for at in item[1]:
                copy = pltpu.make_async_copy(ref.at[at], places[used], marks.at[mark])
                copy.start()
                arriving.append(Arriving(copy, places[used]))
                given.append(arriving[-1])
                used, mark = used + 1, mark + 1
        for ref, item in zip(out_refs, outs, strict=True):
            if isinstance(item, Near):
                given.append(Staying(ref))
                continue
            for at in item[1]:
                copies = []
                for first in at[0] if isinstance(at[0], tuple) else (at[0],):
                    copies.append(
                        pltpu.make_async_copy(
                            places[used], ref.at[(first, *at[1:])], marks.at[mark]
                        )
                    )
                    mark += 1
                leaving.append(Leaving(copies, places[used]))
                given.append(leaving[-1])
                used += 1
        body(*given)
        for item in leaving:
            item.send()
        for item in arriving:
            item.wait()
        for item in leaving:
            for copy in item.copies:
                copy.wait()

    arrays = [item.array if isinstance(item, Near) else item[0] for item in ins]
    shapes = [item.array if isinstance(item, Near) else item[0] for item in outs]
    size = sum(x.size * x.dtype.itemsize for x in (*arrays, *shapes))
    return pl.pallas_call(
        run,
        out_shape=[
            result if isinstance(item, Near) else pltpu.HBM(result.shape, result.dtype)
            for result, item in zip(shapes, outs, strict=True)
        ],
        in_specs=[vmem if isinstance(item, Near) else hbm for item in ins],
        out_specs=[vmem if isinstance(item, Near) else hbm for item in outs],
        scratch_shapes=[*scratch, pltpu.SemaphoreType.DMA((max(marks_needed, 1),))],
        input_output_aliases={} if alias is None else {alias: 0},
        compiler_params=pltpu.CompilerParams(vmem_limit_bytes=VMEM_LIMIT),
        cost_estimate=pl.CostEstimate(flops=int(flops), bytes_accessed=size, transcendentals=0),
    )(
        *(
            array
            if isinstance(item, Near)
            else pltpu.with_memory_space_constraint(array, pltpu.HBM)
            for array, item in zip(arrays, ins, strict=True)
        )
    )


def whole(value):
    return (value, [(ALL,) * len(value.shape)])


def read_down(ref):
    return ref[...].reshape(-1, 128)


def read_up(ref):
    count, length, _ = ref.shape
    rows = 128 // count
    columns = []
    for pair in range(length // (2 * rows)):
        slab = ref[:, pair * 2 * rows : (pair + 1) * 2 * rows, :].astype(F32)
        for half in range(2):
            columns.append(
                slab[:, half * rows : (half + 1) * rows, :].reshape(128, 128).astype(BF16)
            )
    return jnp.concatenate(columns, axis=1)


def write_down(ref, value):
    value = value.astype(BF16)
    size = ref.shape[2] * ref.shape[1] // 128
    for place in range(ref.shape[0]):
        for part in range(size // 128):
            at = place * size + part * 128
            ref[place, part * 128 : (part + 1) * 128, :] = value[:, at : at + 128]


def write_up(ref, value):
    count, length, _ = ref.shape
    rows = 128 // count
    for pair in range(length // (2 * rows)):
        halves = [
            value[:, (2 * pair + half) * 128 : (2 * pair + half + 1) * 128].reshape(
                count, rows, 128
            )
            for half in range(2)
        ]
        ref[:, pair * 2 * rows : (pair + 1) * 2 * rows, :] = jnp.concatenate(
            halves, axis=1
        ).astype(BF16)


def pack_body(*refs):
    sources, ups, targets = refs[:3], refs[3:7], refs[7:14]
    for ref, place in zip(sources, (A_OUT0, A_QUERY1, A_OUT1), strict=True):
        targets[place][...] = ref[...]
    for ref, place in zip(ups, (B_OUT0, B_OUT1, B_QUERY1, B_QUERY0), strict=True):
        rows, width = ref.shape
        value = ref[...].astype(F32)
        for pair in range(width // 256):
            halves = [
                value[:, (2 * pair + half) * 128 : (2 * pair + half + 1) * 128]
                for half in range(2)
            ]
            targets[place][pair * 2 * rows : (pair + 1) * 2 * rows, :] = jnp.concatenate(
                halves, axis=0
            ).astype(BF16)


def unpack_body(came, a_query_ref, b_query_ref, a_out_ref, b_out_ref):
    for layer in range(2):
        for ref, place in ((a_query_ref, TERM_A_QUERY), (a_out_ref, TERM_A_OUT)):
            value = came[place + layer].astype(F32)
            for part in range(value.shape[0] // 128):
                at = slice(part * 128, (part + 1) * 128)
                ref[layer, at, :] = jnp.transpose(value[at])
        for ref, place in ((b_query_ref, TERM_B_QUERY), (b_out_ref, TERM_B_OUT)):
            rows, width = ref.shape[1:]
            value = came[place + layer].astype(F32)
            for tile in range(width // 128):
                ref[layer, :, tile * 128 : (tile + 1) * 128] = value[
                    tile * rows : (tile + 1) * rows
                ]


def first_body(hidden_ref, gain_ref, parent_ref, down_ref, sent_ref, bias_ref):
    lane = lax.broadcasted_iota(jnp.int32, (128, 128), 1)
    line = lax.broadcasted_iota(jnp.int32, (128, 128), 0)
    linked = (lane == line) | (jnp.broadcast_to(parent_ref[...], (128, 128)) == line)
    reached = jnp.where(linked, 1.0, 0.0).astype(BF16)
    for _ in range(7):
        reached = jnp.minimum(dot(reached, reached), 1.0).astype(BF16)
    bias_ref[...] = jnp.where(jnp.transpose(reached.astype(F32)) > 0.5, 0.0, -1e30)
    hidden = hidden_ref[...].astype(F32)
    projected = dot((hidden * gain_ref[...]).astype(BF16), down_ref[...])
    squares = lax.dot_general(
        jnp.ones((8, hidden.shape[1]), F32),
        hidden * hidden,
        (((1,), (1,)), ((), ())),
        preferred_element_type=F32,
        precision=lax.Precision.HIGHEST,
    )
    sent_ref[:128, :] = projected
    sent_ref[128:, :] = squares


def to_column(row):
    lane = lax.broadcasted_iota(jnp.int32, (128, 128), 1)
    line = lax.broadcasted_iota(jnp.int32, (128, 128), 0)
    return row_sum(jnp.where(lane == line, jnp.broadcast_to(row, (128, 128)), 0.0))


def total(ref, start=0):
    value = ref[0, start : start + 128, :].astype(F32)
    for peer in range(1, ref.shape[0]):
        value = value + ref[peer, start : start + 128, :].astype(F32)
    return value


def head_blocks(query_ref, key_ref):
    heads = query_ref.shape[-1] // HEAD_DIM
    groups = key_ref.shape[-1] // HEAD_DIM
    share = heads // groups
    return [
        (head, slice((head // share) * HEAD_DIM, (head // share + 1) * HEAD_DIM))
        for head in range(0, heads, HEADS_AT_ONCE)
    ]


def stacked(value, head):
    return jnp.concatenate(
        [
            value[:, (head + k) * HEAD_DIM : (head + k + 1) * HEAD_DIM]
            for k in range(HEADS_AT_ONCE)
        ],
        axis=0,
    )


def spread(ref, head, value):
    for k in range(HEADS_AT_ONCE):
        ref[:, (head + k) * HEAD_DIM : (head + k + 1) * HEAD_DIM] = value[k * 128 : (k + 1) * 128]


def softmax_of(queries, keys, bias):
    scores = dot_cols(queries, keys) * HEAD_DIM ** (-0.5) + bias
    weights = jnp.exp(scores - jnp.max(scores, axis=1, keepdims=True))
    return weights * (1.0 / row_sum(weights))


def score_back(back_attended, probability, keys, values):
    back_probability = dot_cols(back_attended, values)
    back_scores = probability * (back_probability - row_sum(probability * back_probability))
    return (dot(back_scores.astype(BF16), keys) * HEAD_DIM ** (-0.5)).astype(BF16)


def layer0_body(
    came_ref, query_ref, up_query_ref, key_ref, value_ref, bias_ref, hidden_ref, gain_ref,
    down_output_ref, up0_ref, down1_ref, up1_ref, cot_ref,
    sent_ref, attended_ref, probability_ref, rank_ref, small_ref, kept_ref, far_small_ref,
):
    projected = total(came_ref)
    squares = came_ref[0, 128:129, :]
    for peer in range(1, came_ref.shape[0]):
        squares = squares + came_ref[peer, 128:129, :]
    squares = to_column(squares)
    scale = lax.rsqrt(squares / D + EPSILON)
    rank_query = (scale * projected).astype(BF16)
    rank_ref[...] = rank_query
    small_ref[0] = projected
    small_ref[1] = jnp.broadcast_to(scale, (128, 128))
    small_ref[2] = jnp.broadcast_to(squares, (128, 128))
    far_small_ref[0] = projected
    far_small_ref[1] = jnp.broadcast_to(scale, (128, 128))
    rank_ref.send()
    far_small_ref.send()
    bias = jnp.concatenate([bias_ref[...]] * HEADS_AT_ONCE, axis=0)
    queries = (query_ref[...].astype(F32) + dot(rank_query, read_up(up_query_ref))).astype(BF16)
    for head, shared in head_blocks(query_ref, key_ref):
        probability = softmax_of(stacked(queries, head), key_ref[:, shared], bias)
        probability_ref[head * 128 : (head + HEADS_AT_ONCE) * 128, :] = probability
        spread(
            attended_ref, head, dot(probability.astype(BF16), value_ref[:, shared]).astype(BF16)
        )
    probability_ref.send()
    attended_ref.send()
    hidden, gain = hidden_ref[...], gain_ref[...]
    up0, down1, cot = read_up(up0_ref), read_down(down1_ref), cot_ref[...]
    sent_ref[512:640, :] = dot_cols(hidden, up0).astype(BF16)
    sent_ref[640:, :] = dot_cols(up0, up0).astype(BF16)
    sent_ref[128:256, :] = dot((hidden.astype(F32) * gain).astype(BF16), down1).astype(BF16)
    sent_ref[256:384, :] = dot((up0.astype(F32) * gain).astype(BF16), down1).astype(BF16)
    sent_ref[384:512, :] = dot_cols(cot, read_up(up1_ref)).astype(BF16)
    sent_ref[:128, :] = dot(attended_ref[...], read_down(down_output_ref)).astype(BF16)
    sent_ref.send()
    kept_ref[...] = dot_cols(cot, up0).astype(BF16)


def layer1_body(
    came_ref, small0_ref, query_ref, up_ref, key_ref, value_ref, bias_ref, down_ref, kept_ref,
    sent_ref, attended_ref, back_query_ref, ranks_ref, small_ref,
):
    rank_output0 = total(came_ref).astype(BF16)
    cross = total(came_ref, 256)
    projected = total(came_ref, 128) + dot(rank_output0, cross.astype(BF16))
    back_rank_output = total(came_ref, 384).astype(BF16)
    hidden_up = total(came_ref, 512)
    gram = total(came_ref, 640)
    gram_high = gram.astype(BF16)
    gram_low = (gram - gram_high.astype(F32)).astype(BF16)
    output_gram = dot(rank_output0, gram_high) + dot(rank_output0, gram_low)
    squares = small0_ref[2, :, :1] + row_sum(
        rank_output0.astype(F32) * (2.0 * hidden_up + output_gram)
    )
    scale = lax.rsqrt(jnp.maximum(squares, 0.0) / D + EPSILON)
    rank_query = (scale * projected).astype(BF16)
    ranks_ref[0] = rank_output0
    ranks_ref[1] = rank_query
    ranks_ref[2] = back_rank_output
    ranks_ref.send()
    small_ref[0] = projected
    small_ref[1] = jnp.broadcast_to(scale, (128, 128))
    small_ref[2] = cross
    small_ref[3] = hidden_up + output_gram
    small_ref.send()
    bias = jnp.concatenate([bias_ref[...]] * HEADS_AT_ONCE, axis=0)
    up_query = read_up(up_ref)
    queries = (query_ref[...].astype(F32) + dot(rank_query, up_query)).astype(BF16)
    down_output = read_down(down_ref)
    back_attended = dot_cols(back_rank_output, down_output).astype(BF16)
    for head, shared in head_blocks(query_ref, key_ref):
        keys, values = key_ref[:, shared], value_ref[:, shared]
        probability = softmax_of(stacked(queries, head), keys, bias)
        spread(attended_ref, head, dot(probability.astype(BF16), values).astype(BF16))
        spread(
            back_query_ref, head, score_back(stacked(back_attended, head), probability, keys, values)
        )
    attended_ref.send()
    back_query_ref.send()
    rank_output = dot(attended_ref[...], down_output).astype(BF16)
    back_rank = dot_cols(back_query_ref[...], up_query).astype(BF16)
    kept = kept_ref[...]
    for peer in range(sent_ref.shape[0]):
        sent_ref[peer, :128, :] = rank_output
        sent_ref[peer, 128:256, :] = back_rank
        sent_ref[peer, 256:, :] = kept


def backward0_body(
    came_ref, small_ref, down_ref, key_ref, value_ref, probability_ref, up_ref,
    sent_ref, back_query_ref, ranks_ref, pull_ref,
):
    back_rank1 = total(came_ref, 128).astype(BF16)
    scale = small_ref[1, :, :1]
    along = row_sum(back_rank1.astype(F32) * small_ref[0]) / D
    pull = scale * scale * scale * along
    back_output = (
        total(came_ref, 256)
        + scale * dot_cols(back_rank1, small_ref[2].astype(BF16))
        - pull * small_ref[3]
    ).astype(BF16)
    ranks_ref[0] = total(came_ref).astype(BF16)
    ranks_ref[1] = back_rank1
    ranks_ref[2] = back_output
    ranks_ref.send()
    pull_ref[...] = jnp.broadcast_to(pull, (128, 128))
    pull_ref.send()
    back_attended = dot_cols(back_output, read_down(down_ref)).astype(BF16)
    for head, shared in head_blocks(back_query_ref, key_ref):
        spread(
            back_query_ref,
            head,
            score_back(
                stacked(back_attended, head),
                probability_ref[head * 128 : (head + HEADS_AT_ONCE) * 128, :],
                key_ref[:, shared],
                value_ref[:, shared],
            ),
        )
    back_query_ref.send()
    back_rank = dot_cols(back_query_ref[...], read_up(up_ref)).astype(BF16)
    sent_ref[...] = back_rank


def terms_body(
    ranks1_ref, ranks2_ref, small_ref, pull_ref, gain_ref, cot_ref, hidden_ref, up0_ref, down1_ref,
    up1_ref, attended0_ref, attended1_ref, rank0_ref, back_query0_ref, back_query1_ref,
    a_query1, b_query0, b_query1, a_out0, a_out1, b_out0, b_out1, out_ref, gradient_ref,
):
    rank_output0, rank_query1, back_output1 = ranks1_ref[0], ranks1_ref[1], ranks1_ref[2]
    rank_output1, back_rank1, back_output0 = ranks2_ref[0], ranks2_ref[1], ranks2_ref[2]
    cot = cot_ref[...]
    write_up(b_out1, dot_rows(rank_output1, cot))
    b_out1.send()
    gain, scale, pull = gain_ref[...], small_ref[1, :, :1], pull_ref[:, :1]
    hidden = hidden_ref[...].astype(F32) + dot(rank_output0, read_up(up0_ref))
    write_down(a_query1, dot_rows(back_rank1, (hidden * scale * gain).astype(BF16)))
    a_query1.send()
    gained = gain * dot_cols(back_rank1, read_down(down1_ref))
    gradient = cot.astype(F32) + scale * gained - hidden * pull
    gradient_ref[...] = gradient
    gradient_ref.send()
    write_up(b_out0, dot_rows(rank_output0, gradient.astype(BF16)))
    b_out0.send()
    out_ref[...] = (hidden + dot(rank_output1, read_up(up1_ref))).astype(BF16)
    out_ref.send()
    write_down(a_out0, dot_rows(back_output0, attended0_ref[...]))
    a_out0.send()
    write_down(a_out1, dot_rows(back_output1, attended1_ref[...]))
    a_out1.send()
    write_up(b_query1, dot_rows(rank_query1, back_query1_ref[...]))
    b_query1.send()
    write_up(b_query0, dot_rows(rank0_ref[...], back_query0_ref[...]))


def last_term_body(came_ref, small_ref, gain_ref, hidden_ref, a_query0, back_rank_ref):
    back_rank = total(came_ref).astype(BF16)
    back_rank_ref[...] = back_rank
    back_rank_ref.send()
    normed = (hidden_ref[...].astype(F32) * small_ref[1, :, :1] * gain_ref[...]).astype(BF16)
    write_down(a_query0, dot_rows(back_rank, normed))


def cot_body(back_rank_ref, small_ref, gain_ref, down_ref, hidden_ref, gradient_ref, cot_ref):
    back_rank = back_rank_ref[...]
    scale = small_ref[1, :, :1]
    along = row_sum(back_rank.astype(F32) * small_ref[0]) / D
    gained = gain_ref[...] * dot_cols(back_rank, down_ref[...])
    cot_ref[...] = (
        gradient_ref[...]
        + scale * gained
        - hidden_ref[...].astype(F32) * (scale * scale * scale * along)
    ).astype(BF16)


def swap(value, axis):
    return lax.all_to_all(value, axis, 0, 0, tiled=True)


def on_device(
    arrived, cot_later, q_base, k_base, v_base, gains, parents, a_query, b_query, a_out, b_out
):
    ways = lax.axis_size("tensor")
    count = lax.axis_size("dp")
    rows, width = b_query.shape[1], arrived.shape[1]
    length = rows * width // 128
    heads = width // HEAD_DIM
    block = whole(shape((128, width), BF16))
    layer0, layer1 = [(0,)], [(1,)]
    gain0, gain1 = (gains, [(slice(0, 1),)]), (gains, [(slice(1, 2),)])
    peers = [(tuple(range(ways)),)]

    (shard,) = kernel_call(
        pack_body,
        [
            (a_out, layer0), (a_query, layer1), (a_out, layer1),
            (b_out, layer0), (b_out, layer1), (b_query, layer1), (b_query, layer0),
        ],
        [(shape((7, length, 128), BF16), [(member,) for member in range(7)])],
        0,
    )
    stack = lax.all_gather(shard, "dp", axis=0, tiled=False)

    def factor(*members):
        return (stack, [(ALL, member) for member in members])

    hidden = from_behind(arrived, "section", 1)
    cot = from_behind(cot_later, "section", -1)
    down0 = lax.all_gather(a_query[0], "dp", axis=0, tiled=True)
    sent, bias = kernel_call(
        first_body,
        [whole(hidden), gain0, whole(parents.reshape(1, 128)), whole(down0)],
        [(shape((ways, 136, 128), F32), peers), whole(shape((128, 128), F32))],
        1e8,
    )
    came = swap(sent, "tensor")
    sent, attended0, probability, rank_query0, small0, kept, far_small0 = kernel_call(
        layer0_body,
        [
            whole(came), (q_base, layer0), factor(B_QUERY0), (k_base, layer0), (v_base, layer0),
            whole(bias), whole(hidden), gain1, factor(A_OUT0, B_OUT0, A_QUERY1, B_OUT1),
            whole(cot),
        ],
        [
            Near(shape((768, 128), BF16)),
            Near(block[0]),
            Near(shape((heads * 128, 128), F32)),
            Near(shape((128, 128), BF16)),
            Near(shape((3, 128, 128), F32)),
            Near(shape((128, 128), BF16)),
            whole(shape((2, 128, 128), F32)),
        ],
        9e8,
    )
    came = lax.all_gather(sent, "tensor", axis=0, tiled=False)

    def near_factor(*members):
        return Near(stack, *[(ALL, member) for member in members])

    near_gain0, near_gain1 = Near(gains, (slice(0, 1),)), Near(gains, (slice(1, 2),))
    sent, attended1, back_query1, ranks1, small1 = kernel_call(
        layer1_body,
        [
            Near(came), Near(small0), Near(q_base, (1,)), near_factor(B_QUERY1),
            Near(k_base, (1,)), Near(v_base, (1,)), Near(bias), near_factor(A_OUT1), Near(kept),
        ],
        [
            Near(shape((ways, 384, 128), BF16)),
            Near(block[0]),
            Near(block[0]),
            Near(shape((3, 128, 128), BF16)),
            Near(shape((4, 128, 128), F32)),
        ],
        8e8,
    )
    came = swap(sent, "tensor")
    sent, back_query0, ranks2, pull = kernel_call(
        backward0_body,
        [
            Near(came), Near(small1), near_factor(A_OUT0), Near(k_base, (0,)), Near(v_base, (0,)),
            Near(probability), near_factor(B_QUERY0),
        ],
        [
            (shape((ways, 128, 128), BF16), peers),
            block,
            Near(shape((3, 128, 128), BF16)),
            Near(shape((128, 128), F32)),
        ],
        4e8,
    )
    came = swap(sent, "tensor")
    term_shape = shape((count, 8, length, 128), BF16)
    made_first = (
        TERM_A_QUERY + 1, TERM_B_QUERY, TERM_B_QUERY + 1, TERM_A_OUT, TERM_A_OUT + 1,
        TERM_B_OUT, TERM_B_OUT + 1,
    )
    terms, section_out, gradient = kernel_call(
        terms_body,
        [
            Near(ranks1), Near(ranks2), Near(small1), Near(pull), near_gain1, Near(cot),
            Near(hidden), factor(B_OUT0, A_QUERY1, B_OUT1), Near(attended0), Near(attended1),
            Near(rank_query0), whole(back_query0), Near(back_query1),
        ],
        [
            (term_shape, [(ALL, member) for member in made_first]),
            block,
            whole(shape((128, width), F32)),
        ],
        1e9,
    )
    terms, back_rank0 = kernel_call(
        last_term_body,
        [Near(came), Near(small0), near_gain0, Near(hidden), whole(terms)],
        [(term_shape, [(ALL, TERM_A_QUERY)]), whole(shape((128, 128), BF16))],
        1e8,
        alias=4,
    )
    reduced = lax.psum_scatter(terms, "dp", scatter_dimension=0, tiled=False)
    (cot_send,) = kernel_call(
        cot_body,
        [
            whole(back_rank0), whole(far_small0), gain0, whole(down0), whole(hidden),
            whole(gradient),
        ],
        [block],
        1e8,
    )
    grads = kernel_call(
        unpack_body,
        [whole(reduced)],
        [
            whole(shape((2, length, 128), F32)),
            whole(shape((2, rows, width), F32)),
            whole(shape((2, length, 128), F32)),
            whole(shape((2, rows, width), F32)),
        ],
        0,
    )
    return (section_out, cot_send, *grads)


def solution(mesh):
    in_specs = (
        P(("section", "dp"), "tensor"),
        P(("section", "dp"), "tensor"),
        P(None, ("section", "dp"), "tensor"),
        P(None, ("section", "dp"), "tensor"),
        P(None, ("section", "dp"), "tensor"),
        P("section", "tensor"),
        P(("section", "dp")),
        P("section", ("tensor", "dp"), None),
        P("section", "dp", "tensor"),
        P("section", ("tensor", "dp"), None),
        P("section", "dp", "tensor"),
    )
    out_specs = (
        P(("section", "dp"), "tensor"),
        P(("section", "dp"), "tensor"),
        P("section", ("tensor", "dp"), None),
        P("section", "dp", "tensor"),
        P("section", ("tensor", "dp"), None),
        P("section", "dp", "tensor"),
    )
    return jax.shard_map(
        on_device, mesh=mesh, in_specs=in_specs, out_specs=out_specs, check_vma=False
    )
```

```python
import jax
import jax.numpy as jnp
from jax import lax
from jax.experimental import pallas as pl
from jax.experimental.pallas import tpu as pltpu
from jax.sharding import PartitionSpec as P

D = 8192
HEAD_DIM = 128
HEADS_AT_ONCE = 4
EPSILON = 1e-05
F32 = jnp.float32
BF16 = jnp.bfloat16
VMEM_LIMIT = 20 << 20
ALL = slice(None)
(A_QUERY0, A_QUERY1, A_OUT0, A_OUT1, B_QUERY0, B_QUERY1, B_OUT0, B_OUT1) = range(8)
PROJECTED0, PROJECTED1, CROSS, BACK_OUTPUT1, HIDDEN_UP, GRAM, BACK_OUTPUT0, SQUARES = range(
    0, 1024, 128
)
SCALE_UP = 65536.0
TERM_A_QUERY, TERM_B_QUERY, TERM_A_OUT, TERM_B_OUT = 0, 2, 4, 6


def from_behind(value, axis, steps):
    count = lax.axis_size(axis)
    pairs = [(source, (source + steps) % count) for source in range(count)]
    return lax.ppermute(value, axis, pairs)


def dot(left, right):
    return jnp.dot(left, right, preferred_element_type=F32)


def dot_rows(left, right):
    return lax.dot_general(left, right, (((0,), (0,)), ((), ())), preferred_element_type=F32)


def dot_cols(left, right):
    return lax.dot_general(left, right, (((1,), (1,)), ((), ())), preferred_element_type=F32)


def row_sum(value):
    return jnp.sum(value, axis=1, keepdims=True)


def shape(dims, dtype):
    return jax.ShapeDtypeStruct(dims, dtype)


class Arriving:
    def __init__(self, copy, ref):
        self.copy, self.ref, self.waited = copy, ref, False
        self.shape = ref.shape

    def wait(self):
        if not self.waited:
            self.copy.wait()
            self.waited = True

    def __getitem__(self, at):
        self.wait()
        return self.ref[at]


class Leaving:
    def __init__(self, copies, ref):
        self.copies, self.ref, self.sent = copies, ref, False
        self.shape = ref.shape

    def send(self):
        if not self.sent:
            for copy in self.copies:
                copy.start()
            self.sent = True

    def __setitem__(self, at, value):
        self.ref[at] = value

    def __getitem__(self, at):
        return self.ref[at]


class Staying:
    def __init__(self, ref):
        self.ref = ref
        self.shape = ref.shape

    def send(self):
        pass

    def __setitem__(self, at, value):
        self.ref[at] = value

    def __getitem__(self, at):
        return self.ref[at]


def sliced(dims, at):
    at = at + (ALL,) * (len(dims) - len(at))
    result = []
    for size, entry in zip(dims, at, strict=True):
        if isinstance(entry, slice):
            result.append(len(range(*entry.indices(size))))
    return tuple(result)


class Near:
    def __init__(self, array, *slices):
        self.array, self.slices = array, slices


def kernel_call(body, ins, outs, flops, alias=None):
    hbm, vmem = pl.BlockSpec(memory_space=pltpu.HBM), pl.BlockSpec(memory_space=pltpu.VMEM)
    scratch, marks_needed, in_count, out_count = [], 0, len(ins), len(outs)
    for index, item in enumerate(ins):
        if index != alias and not isinstance(item, Near):
            scratch += [pltpu.VMEM(sliced(item[0].shape, at), item[0].dtype) for at in item[1]]
            marks_needed += len(item[1])
    for item in outs:
        if not isinstance(item, Near):
            for at in item[1]:
                copies = at[0] if isinstance(at[0], tuple) else (at[0],)
                marks_needed += len(copies)
                scratch.append(
                    pltpu.VMEM(sliced(item[0].shape, (copies[0], *at[1:])), item[0].dtype)
                )

    def run(*refs):
        in_refs, out_refs = refs[:in_count], refs[in_count : in_count + out_count]
        places, marks = refs[in_count + out_count : -1], refs[-1]
        used, mark, given, arriving, leaving = 0, 0, [], [], []
        for index, (ref, item) in enumerate(zip(in_refs, ins, strict=True)):
            if index == alias:
                continue
            if isinstance(item, Near):
                given += [ref.at[at] for at in item.slices] if item.slices else [ref]
                continue
            for at in item[1]:
                copy = pltpu.make_async_copy(ref.at[at], places[used], marks.at[mark])
                copy.start()
                arriving.append(Arriving(copy, places[used]))
                given.append(arriving[-1])
                used, mark = used + 1, mark + 1
        for ref, item in zip(out_refs, outs, strict=True):
            if isinstance(item, Near):
                given += [Staying(ref.at[at]) for at in item.slices] or [Staying(ref)]
                continue
            for at in item[1]:
                copies = []
                for first in at[0] if isinstance(at[0], tuple) else (at[0],):
                    copies.append(
                        pltpu.make_async_copy(
                            places[used], ref.at[(first, *at[1:])], marks.at[mark]
                        )
                    )
                    mark += 1
                leaving.append(Leaving(copies, places[used]))
                given.append(leaving[-1])
                used += 1
        body(*given)
        for item in leaving:
            item.send()
        for item in arriving:
            item.wait()
        for item in leaving:
            for copy in item.copies:
                copy.wait()

    arrays = [item.array if isinstance(item, Near) else item[0] for item in ins]
    shapes = [item.array if isinstance(item, Near) else item[0] for item in outs]
    size = sum(x.size * x.dtype.itemsize for x in (*arrays, *shapes))
    return pl.pallas_call(
        run,
        out_shape=[
            result if isinstance(item, Near) else pltpu.HBM(result.shape, result.dtype)
            for result, item in zip(shapes, outs, strict=True)
        ],
        in_specs=[vmem if isinstance(item, Near) else hbm for item in ins],
        out_specs=[vmem if isinstance(item, Near) else hbm for item in outs],
        scratch_shapes=[*scratch, pltpu.SemaphoreType.DMA((max(marks_needed, 1),))],
        input_output_aliases={} if alias is None else {alias: 0},
        compiler_params=pltpu.CompilerParams(vmem_limit_bytes=VMEM_LIMIT),
        cost_estimate=pl.CostEstimate(flops=int(flops), bytes_accessed=size, transcendentals=0),
    )(
        *(
            array
            if isinstance(item, Near)
            else pltpu.with_memory_space_constraint(array, pltpu.HBM)
            for array, item in zip(arrays, ins, strict=True)
        )
    )


def whole(value):
    return (value, [(ALL,) * len(value.shape)])


def read_down(ref):
    return ref[...].reshape(-1, 128)


def read_up(ref):
    count, length, _ = ref.shape
    rows = 128 // count
    columns = []
    for pair in range(length // (2 * rows)):
        slab = ref[:, pair * 2 * rows : (pair + 1) * 2 * rows, :].astype(F32)
        for half in range(2):
            columns.append(
                slab[:, half * rows : (half + 1) * rows, :].reshape(128, 128).astype(BF16)
            )
    return jnp.concatenate(columns, axis=1)


def write_down(ref, value):
    value = value.astype(BF16)
    size = ref.shape[2] * ref.shape[1] // 128
    for place in range(ref.shape[0]):
        for part in range(size // 128):
            at = place * size + part * 128
            ref[place, part * 128 : (part + 1) * 128, :] = value[:, at : at + 128]


def write_up(ref, value):
    count, length, _ = ref.shape
    rows = 128 // count
    for pair in range(length // (2 * rows)):
        halves = [
            value[:, (2 * pair + half) * 128 : (2 * pair + half + 1) * 128].reshape(
                count, rows, 128
            )
            for half in range(2)
        ]
        ref[:, pair * 2 * rows : (pair + 1) * 2 * rows, :] = jnp.concatenate(
            halves, axis=1
        ).astype(BF16)


def pack_body(parent_ref, *refs):
    downs, ups, targets, bias_ref = refs[:4], refs[4:8], refs[8:16], refs[16]
    lane = lax.broadcasted_iota(jnp.int32, (128, 128), 1)
    line = lax.broadcasted_iota(jnp.int32, (128, 128), 0)
    linked = (lane == line) | (jnp.broadcast_to(parent_ref[...], (128, 128)) == line)
    reached = jnp.where(linked, 1.0, 0.0).astype(BF16)
    for _ in range(7):
        reached = jnp.minimum(dot(reached, reached), 1.0).astype(BF16)
    bias_ref[...] = jnp.where(jnp.transpose(reached.astype(F32)) > 0.5, 0.0, -1e30)
    for ref, target in zip(downs, targets[:4], strict=True):
        target[...] = ref[...]
    for ref, target in zip(ups, targets[4:], strict=True):
        rows, width = ref.shape
        value = ref[...].astype(F32)
        for pair in range(width // 256):
            halves = [
                value[:, (2 * pair + half) * 128 : (2 * pair + half + 1) * 128]
                for half in range(2)
            ]
            target[pair * 2 * rows : (pair + 1) * 2 * rows, :] = jnp.concatenate(
                halves, axis=0
            ).astype(BF16)


def unpack_body(came, a_query_ref, b_query_ref, a_out_ref, b_out_ref):
    for layer in range(2):
        for ref, place in ((a_query_ref, TERM_A_QUERY), (a_out_ref, TERM_A_OUT)):
            value = came[place + layer].astype(F32)
            for part in range(value.shape[0] // 128):
                at = slice(part * 128, (part + 1) * 128)
                ref[layer, at, :] = jnp.transpose(value[at])
        for ref, place in ((b_query_ref, TERM_B_QUERY), (b_out_ref, TERM_B_OUT)):
            rows, width = ref.shape[1:]
            value = came[place + layer].astype(F32)
            for tile in range(width // 128):
                ref[layer, :, tile * 128 : (tile + 1) * 128] = value[
                    tile * rows : (tile + 1) * rows
                ]


def first_body(
    hidden_ref, cot_ref, gain0_ref, gain1_ref, down0_ref, down1_ref, up0_ref, up1_ref, sent_ref
):
    def send(start, value):
        value = value.astype(BF16)
        for peer in range(sent_ref.shape[0]):
            sent_ref[peer, start : start + value.shape[0], :] = value

    hidden, gain1 = hidden_ref[...], gain1_ref[...]
    wide = hidden.astype(F32)
    down1, up0, cot = read_down(down1_ref), read_up(up0_ref), cot_ref[...]
    send(PROJECTED0, dot((wide * gain0_ref[...]).astype(BF16), read_down(down0_ref)))
    send(PROJECTED1, dot((wide * gain1).astype(BF16), down1))
    send(CROSS, dot((up0.astype(F32) * gain1).astype(BF16), down1))
    send(BACK_OUTPUT1, dot_cols(cot, read_up(up1_ref)))
    send(HIDDEN_UP, dot_cols(hidden, up0))
    send(GRAM, dot_cols(up0, up0))
    send(BACK_OUTPUT0, dot_cols(cot, up0))
    squares = lax.dot_general(
        jnp.ones((16, hidden.shape[1]), F32),
        wide * wide,
        (((1,), (1,)), ((), ())),
        preferred_element_type=F32,
        precision=lax.Precision.HIGHEST,
    )
    high = squares.astype(BF16)
    rest = squares - high.astype(F32)
    middle = rest.astype(BF16)
    send(SQUARES, high)
    send(SQUARES + 16, middle)
    send(SQUARES + 32, rest - middle.astype(F32))


def to_column(row):
    lane = lax.broadcasted_iota(jnp.int32, (128, 128), 1)
    line = lax.broadcasted_iota(jnp.int32, (128, 128), 0)
    return row_sum(jnp.where(lane == line, jnp.broadcast_to(row, (128, 128)), 0.0))


def total(ref, start=0, rows=128):
    value = ref[0, start : start + rows, :].astype(F32)
    for peer in range(1, ref.shape[0]):
        value = value + ref[peer, start : start + rows, :].astype(F32)
    return value


def head_blocks(query_ref, key_ref):
    heads = query_ref.shape[-1] // HEAD_DIM
    groups = key_ref.shape[-1] // HEAD_DIM
    share = heads // groups
    return [
        (head, slice((head // share) * HEAD_DIM, (head // share + 1) * HEAD_DIM))
        for head in range(0, heads, HEADS_AT_ONCE)
    ]


def stacked(value, head):
    return jnp.concatenate(
        [
            value[:, (head + k) * HEAD_DIM : (head + k + 1) * HEAD_DIM]
            for k in range(HEADS_AT_ONCE)
        ],
        axis=0,
    )


def spread(ref, head, value):
    for k in range(HEADS_AT_ONCE):
        ref[:, (head + k) * HEAD_DIM : (head + k + 1) * HEAD_DIM] = value[k * 128 : (k + 1) * 128]


def softmax_of(queries, keys, bias):
    scores = dot_cols(queries, keys) * HEAD_DIM ** (-0.5) + bias
    weights = jnp.exp(scores - jnp.max(scores, axis=1, keepdims=True))
    return weights * (1.0 / row_sum(weights))


def score_back(back_attended, probability, keys, values):
    back_probability = dot_cols(back_attended, values)
    back_scores = probability * (back_probability - row_sum(probability * back_probability))
    return (dot(back_scores.astype(BF16), keys) * HEAD_DIM ** (-0.5)).astype(BF16)


def layer0_body(
    came_ref, query_ref, up_query_ref, key_ref, value_ref, bias_ref, down_output_ref,
    sent_ref, attended_ref, probability_ref, rank_ref, small_ref, far_small_ref,
):
    projected = total(came_ref, PROJECTED0)
    squares = to_column(
        (
            total(came_ref, SQUARES, 16)
            + total(came_ref, SQUARES + 16, 16)
            + total(came_ref, SQUARES + 32, 16)
        )[:1]
    )
    scale = lax.rsqrt(squares / D + EPSILON)
    rank_query = (scale * projected).astype(BF16)
    rank_ref[...] = rank_query
    small_ref[0] = projected
    small_ref[1] = jnp.broadcast_to(scale, (128, 128))
    small_ref[2] = jnp.broadcast_to(squares, (128, 128))
    far_small_ref[0] = projected
    far_small_ref[1] = jnp.broadcast_to(scale, (128, 128))
    rank_ref.send()
    far_small_ref.send()
    bias = jnp.concatenate([bias_ref[...]] * HEADS_AT_ONCE, axis=0)
    queries = (query_ref[...].astype(F32) + dot(rank_query, read_up(up_query_ref))).astype(BF16)
    for head, shared in head_blocks(query_ref, key_ref):
        probability = softmax_of(stacked(queries, head), key_ref[:, shared], bias)
        probability_ref[head * 128 : (head + HEADS_AT_ONCE) * 128, :] = probability
        spread(
            attended_ref, head, dot(probability.astype(BF16), value_ref[:, shared]).astype(BF16)
        )
    probability_ref.send()
    attended_ref.send()
    rank_output = dot(attended_ref[...], read_down(down_output_ref)).astype(BF16)
    for peer in range(sent_ref.shape[0]):
        sent_ref[peer] = rank_output


def layer1_body(
    came_ref, first_ref, small0_ref, query_ref, up_ref, key_ref, value_ref, bias_ref, down_ref,
    sent_ref, attended_ref, back_query_ref, ranks_ref, small_ref, scale_ref,
):
    rank_output0 = total(came_ref).astype(BF16)
    cross = total(first_ref, CROSS)
    projected = total(first_ref, PROJECTED1) + dot(rank_output0, cross.astype(BF16))
    back_rank_output = total(first_ref, BACK_OUTPUT1).astype(BF16)
    hidden_up = total(first_ref, HIDDEN_UP)
    gram = total(first_ref, GRAM)
    gram_high = gram.astype(BF16)
    gram_low = (gram - gram_high.astype(F32)).astype(BF16)
    output_gram = dot(rank_output0, gram_high) + dot(rank_output0, gram_low)
    squares = small0_ref[2, :, :1] + row_sum(
        rank_output0.astype(F32) * (2.0 * hidden_up + output_gram)
    )
    scale = lax.rsqrt(jnp.maximum(squares, 0.0) / D + EPSILON)
    rank_query = (scale * projected).astype(BF16)
    ranks_ref[0] = rank_output0
    ranks_ref[1] = rank_query
    ranks_ref[2] = back_rank_output
    ranks_ref.send()
    small_ref[0] = projected
    small_ref[1] = jnp.broadcast_to(scale, (128, 128))
    small_ref[2] = cross
    small_ref[3] = hidden_up + output_gram
    scale_ref[...] = jnp.broadcast_to(scale, (128, 128))
    scale_ref.send()
    bias = jnp.concatenate([bias_ref[...]] * HEADS_AT_ONCE, axis=0)
    up_query = read_up(up_ref)
    queries = (query_ref[...].astype(F32) + dot(rank_query, up_query)).astype(BF16)
    down_output = read_down(down_ref)
    back_attended = dot_cols(back_rank_output, down_output).astype(BF16)
    for head, shared in head_blocks(query_ref, key_ref):
        keys, values = key_ref[:, shared], value_ref[:, shared]
        probability = softmax_of(stacked(queries, head), keys, bias)
        spread(attended_ref, head, dot(probability.astype(BF16), values).astype(BF16))
        spread(
            back_query_ref, head, score_back(stacked(back_attended, head), probability, keys, values)
        )
    attended_ref.send()
    back_query_ref.send()
    rank_output = dot(attended_ref[...], down_output).astype(BF16)
    back_rank = dot_cols(back_query_ref[...], up_query).astype(BF16)
    for peer in range(sent_ref.shape[0]):
        sent_ref[peer, :128, :] = rank_output
        sent_ref[peer, 128:, :] = back_rank


def backward0_body(
    came_ref, first_ref, small_ref, down_ref, key_ref, value_ref, probability_ref, up_ref,
    sent_ref, back_query_ref, ranks_ref, pull_ref,
):
    back_rank1 = total(came_ref, 128).astype(BF16)
    scale = small_ref[1, :, :1]
    along = row_sum(back_rank1.astype(F32) * small_ref[0]) / D
    pull = scale * scale * scale * along
    back_output = (
        total(first_ref, BACK_OUTPUT0)
        + scale * dot_cols(back_rank1, small_ref[2].astype(BF16))
        - pull * small_ref[3]
    ).astype(BF16)
    ranks_ref[0] = total(came_ref).astype(BF16)
    ranks_ref[1] = back_rank1
    ranks_ref[2] = back_output
    ranks_ref.send()
    pull_ref[...] = jnp.broadcast_to(pull, (128, 128))
    pull_ref.send()
    back_attended = dot_cols(back_output, read_down(down_ref)).astype(BF16)
    for head, shared in head_blocks(back_query_ref, key_ref):
        spread(
            back_query_ref,
            head,
            score_back(
                stacked(back_attended, head),
                probability_ref[head * 128 : (head + HEADS_AT_ONCE) * 128, :],
                key_ref[:, shared],
                value_ref[:, shared],
            ),
        )
    back_query_ref.send()
    back_rank = dot_cols(back_query_ref[...], read_up(up_ref)).astype(BF16)
    sent_ref[...] = back_rank


def terms_body(
    ranks1_ref, ranks2_ref, scale_ref, pull_ref, gain_ref, cot_ref, hidden_ref, up0_ref, down1_ref,
    up1_ref, attended0_ref, attended1_ref, rank0_ref, back_query0_ref, back_query1_ref, small0_ref,
    gain0_ref, a_query1, b_query0, b_query1, a_out0, a_out1, b_out0, b_out1, out_ref, gradient_ref,
    normed0_ref,
):
    rank_output0, rank_query1, back_output1 = ranks1_ref[0], ranks1_ref[1], ranks1_ref[2]
    rank_output1, back_rank1, back_output0 = ranks2_ref[0], ranks2_ref[1], ranks2_ref[2]
    cot = cot_ref[...]
    write_up(b_out1, dot_rows(rank_output1, cot))
    b_out1.send()
    gain, scale, pull = gain_ref[...], scale_ref[:, :1], pull_ref[:, :1]
    hidden = hidden_ref[...].astype(F32)
    normed0_ref[...] = (hidden * small0_ref[1, :, :1] * gain0_ref[...]).astype(BF16)
    hidden = hidden + dot(rank_output0, read_up(up0_ref))
    write_down(a_query1, dot_rows(back_rank1, (hidden * scale * gain).astype(BF16)))
    a_query1.send()
    gained = gain * dot_cols(back_rank1, read_down(down1_ref))
    gradient = cot.astype(F32) + scale * gained - hidden * pull
    gradient_ref[...] = gradient
    gradient_ref.send()
    write_up(b_out0, dot_rows(rank_output0, gradient.astype(BF16)))
    b_out0.send()
    out_ref[...] = (hidden + dot(rank_output1, read_up(up1_ref))).astype(BF16)
    out_ref.send()
    write_down(a_out0, dot_rows(back_output0, attended0_ref[...]))
    a_out0.send()
    write_down(a_out1, dot_rows(back_output1, attended1_ref[...]))
    a_out1.send()
    write_up(b_query1, dot_rows(rank_query1, back_query1_ref[...]))
    b_query1.send()
    write_up(b_query0, dot_rows(rank0_ref[...], back_query0_ref[...]))


def last_term_body(came_ref, normed_ref, a_query0, back_rank_ref):
    back_rank = total(came_ref).astype(BF16)
    back_rank_ref[...] = back_rank
    back_rank_ref.send()
    write_down(a_query0, dot_rows(back_rank, normed_ref[...]))


def cot_body(back_rank_ref, small_ref, gain_ref, down_ref, hidden_ref, gradient_ref, cot_ref):
    back_rank = back_rank_ref[...]
    scale = small_ref[1, :, :1]
    along = row_sum(back_rank.astype(F32) * small_ref[0]) / D
    gained = gain_ref[...] * dot_cols(back_rank, read_down(down_ref))
    cot_ref[...] = (
        gradient_ref[...]
        + scale * gained
        - hidden_ref[...].astype(F32) * (scale * scale * scale * along)
    ).astype(BF16)


def swap(value, axis):
    return lax.all_to_all(value, axis, 0, 0, tiled=True)


def on_device(
    arrived, cot_later, q_base, k_base, v_base, gains, parents, a_query, b_query, a_out, b_out
):
    ways = lax.axis_size("tensor")
    count = lax.axis_size("dp")
    rows, width = b_query.shape[1], arrived.shape[1]
    length = rows * width // 128
    heads = width // HEAD_DIM
    block = whole(shape((128, width), BF16))
    layer0, layer1 = [(0,)], [(1,)]
    gain0, gain1 = (gains, [(slice(0, 1),)]), (gains, [(slice(1, 2),)])
    peers = [(tuple(range(ways)),)]

    shard, bias = kernel_call(
        pack_body,
        [
            whole(parents.reshape(1, 128)),
            *[(array, [(0,), (1,)]) for array in (a_query, a_out, b_query, b_out)],
        ],
        [
            Near(shape((8, length, 128), BF16), *[(member,) for member in range(8)]),
            whole(shape((128, 128), F32)),
        ],
        0,
    )
    shard = (shard.astype(F32) * SCALE_UP).astype(jnp.float16)
    stack = lax.all_gather(shard, "dp", axis=0, tiled=False)
    stack = (stack.astype(F32) * (1.0 / SCALE_UP)).astype(BF16)

    def factor(*members):
        return (stack, [(ALL, member) for member in members])

    def near_factor(*members):
        return Near(stack, *[(ALL, member) for member in members])

    hidden = from_behind(arrived, "section", 1)
    cot = from_behind(cot_later, "section", -1)
    near_gain0, near_gain1 = Near(gains, (slice(0, 1),)), Near(gains, (slice(1, 2),))
    (sent,) = kernel_call(
        first_body,
        [
            Near(hidden), Near(cot), near_gain0, near_gain1,
            near_factor(A_QUERY0, A_QUERY1, B_OUT0, B_OUT1),
        ],
        [Near(shape((ways, SQUARES + 48, 128), BF16))],
        6e8,
    )
    first = swap(sent, "tensor")
    sent, attended0, probability, rank_query0, small0, far_small0 = kernel_call(
        layer0_body,
        [
            Near(first), Near(q_base, (0,)), near_factor(B_QUERY0), Near(k_base, (0,)),
            Near(v_base, (0,)), Near(bias), near_factor(A_OUT0),
        ],
        [
            Near(shape((ways, 128, 128), BF16)),
            block,
            Near(shape((heads * 128, 128), F32)),
            whole(shape((128, 128), BF16)),
            Near(shape((3, 128, 128), F32)),
            whole(shape((2, 128, 128), F32)),
        ],
        9e8,
    )
    came = swap(sent, "tensor")
    sent, attended1, back_query1, ranks1, small1, scale1 = kernel_call(
        layer1_body,
        [
            Near(came), Near(first), Near(small0), Near(q_base, (1,)), near_factor(B_QUERY1),
            Near(k_base, (1,)), Near(v_base, (1,)), Near(bias), near_factor(A_OUT1),
        ],
        [
            Near(shape((ways, 256, 128), BF16)),
            block,
            block,
            whole(shape((3, 128, 128), BF16)),
            Near(shape((4, 128, 128), F32)),
            whole(shape((128, 128), F32)),
        ],
        8e8,
    )
    came = swap(sent, "tensor")
    sent, back_query0, ranks2, pull = kernel_call(
        backward0_body,
        [
            Near(came), Near(first), Near(small1), near_factor(A_OUT0), Near(k_base, (0,)),
            Near(v_base, (0,)), Near(probability), near_factor(B_QUERY0),
        ],
        [
            (shape((ways, 128, 128), BF16), peers),
            block,
            whole(shape((3, 128, 128), BF16)),
            whole(shape((128, 128), F32)),
        ],
        4e8,
    )
    came = swap(sent, "tensor")
    term_shape = shape((count, 8, length, 128), BF16)
    made_first = (
        TERM_A_QUERY + 1, TERM_B_QUERY, TERM_B_QUERY + 1, TERM_A_OUT, TERM_A_OUT + 1,
        TERM_B_OUT, TERM_B_OUT + 1,
    )
    terms, section_out, gradient, normed0 = kernel_call(
        terms_body,
        [
            whole(ranks1), whole(ranks2), whole(scale1), whole(pull), gain1, whole(cot),
            whole(hidden), factor(B_OUT0, A_QUERY1, B_OUT1), whole(attended0), whole(attended1),
            whole(rank_query0), whole(back_query0), whole(back_query1), whole(far_small0), gain0,
        ],
        [
            (term_shape, [(ALL, member) for member in made_first]),
            block,
            whole(shape((128, width), F32)),
            Near(block[0]),
        ],
        1e9,
    )
    terms, back_rank0 = kernel_call(
        last_term_body,
        [Near(came), Near(normed0), whole(terms)],
        [(term_shape, [(ALL, TERM_A_QUERY)]), whole(shape((128, 128), BF16))],
        1e8,
        alias=2,
    )
    reduced = lax.psum_scatter(terms, "dp", scatter_dimension=0, tiled=False)
    (cot_send,) = kernel_call(
        cot_body,
        [
            whole(back_rank0), whole(far_small0), gain0, factor(A_QUERY0), whole(hidden),
            whole(gradient),
        ],
        [block],
        1e8,
    )
    grads = kernel_call(
        unpack_body,
        [whole(reduced)],
        [
            whole(shape((2, length, 128), F32)),
            whole(shape((2, rows, width), F32)),
            whole(shape((2, length, 128), F32)),
            whole(shape((2, rows, width), F32)),
        ],
        0,
    )
    return (section_out, cot_send, *grads)


def solution(mesh):
    in_specs = (
        P(("section", "dp"), "tensor"),
        P(("section", "dp"), "tensor"),
        P(None, ("section", "dp"), "tensor"),
        P(None, ("section", "dp"), "tensor"),
        P(None, ("section", "dp"), "tensor"),
        P("section", "tensor"),
        P(("section", "dp")),
        P("section", ("tensor", "dp"), None),
        P("section", "dp", "tensor"),
        P("section", ("tensor", "dp"), None),
        P("section", "dp", "tensor"),
    )
    out_specs = (
        P(("section", "dp"), "tensor"),
        P(("section", "dp"), "tensor"),
        P("section", ("tensor", "dp"), None),
        P("section", "dp", "tensor"),
        P("section", ("tensor", "dp"), None),
        P("section", "dp", "tensor"),
    )
    return jax.shard_map(
        on_device, mesh=mesh, in_specs=in_specs, out_specs=out_specs, check_vma=False
    )
```

```python
import jax
import jax.numpy as jnp
from jax import lax
from jax.experimental import pallas as pl
from jax.experimental.pallas import tpu as pltpu
from jax.sharding import PartitionSpec as P

D = 8192
HEAD_DIM = 128
HEADS_AT_ONCE = 4
EPSILON = 1e-05
F32 = jnp.float32
BF16 = jnp.bfloat16
VMEM_LIMIT = 20 << 20
ALL = slice(None)
(A_QUERY0, A_QUERY1, A_OUT0, A_OUT1, B_QUERY0, B_QUERY1, B_OUT0, B_OUT1) = range(8)
PROJECTED0, PROJECTED1, CROSS, BACK_OUTPUT1, HIDDEN_UP, GRAM, BACK_OUTPUT0, SQUARES = range(
    0, 1024, 128
)
SCALE_UP = 65536.0
TERM_A_QUERY, TERM_B_QUERY, TERM_A_OUT, TERM_B_OUT = 0, 2, 4, 6


def from_behind(value, axis, steps):
    count = lax.axis_size(axis)
    pairs = [(source, (source + steps) % count) for source in range(count)]
    return lax.ppermute(value, axis, pairs)


def dot(left, right):
    return jnp.dot(left, right, preferred_element_type=F32)


def dot_rows(left, right):
    return lax.dot_general(left, right, (((0,), (0,)), ((), ())), preferred_element_type=F32)


def dot_cols(left, right):
    return lax.dot_general(left, right, (((1,), (1,)), ((), ())), preferred_element_type=F32)


def row_sum(value):
    return jnp.sum(value, axis=1, keepdims=True)


def shape(dims, dtype):
    return jax.ShapeDtypeStruct(dims, dtype)


class Arriving:
    def __init__(self, copy, ref):
        self.copy, self.ref, self.waited = copy, ref, False
        self.shape = ref.shape

    def wait(self):
        if not self.waited:
            self.copy.wait()
            self.waited = True

    def __getitem__(self, at):
        self.wait()
        return self.ref[at]


class Leaving:
    def __init__(self, copies, ref):
        self.copies, self.ref, self.sent = copies, ref, False
        self.shape = ref.shape

    def send(self):
        if not self.sent:
            for copy in self.copies:
                copy.start()
            self.sent = True

    def __setitem__(self, at, value):
        self.ref[at] = value

    def __getitem__(self, at):
        return self.ref[at]


class Staying:
    def __init__(self, ref):
        self.ref = ref
        self.shape = ref.shape

    def send(self):
        pass

    def __setitem__(self, at, value):
        self.ref[at] = value

    def __getitem__(self, at):
        return self.ref[at]


def sliced(dims, at):
    at = at + (ALL,) * (len(dims) - len(at))
    result = []
    for size, entry in zip(dims, at, strict=True):
        if isinstance(entry, slice):
            result.append(len(range(*entry.indices(size))))
    return tuple(result)


class Near:
    def __init__(self, array, *slices):
        self.array, self.slices = array, slices


def kernel_call(body, ins, outs, flops, alias=None):
    hbm, vmem = pl.BlockSpec(memory_space=pltpu.HBM), pl.BlockSpec(memory_space=pltpu.VMEM)
    scratch, marks_needed, in_count, out_count = [], 0, len(ins), len(outs)
    for index, item in enumerate(ins):
        if index != alias and not isinstance(item, Near):
            scratch += [pltpu.VMEM(sliced(item[0].shape, at), item[0].dtype) for at in item[1]]
            marks_needed += len(item[1])
    for item in outs:
        if not isinstance(item, Near):
            for at in item[1]:
                copies = at[0] if isinstance(at[0], tuple) else (at[0],)
                marks_needed += len(copies)
                scratch.append(
                    pltpu.VMEM(sliced(item[0].shape, (copies[0], *at[1:])), item[0].dtype)
                )

    def run(*refs):
        in_refs, out_refs = refs[:in_count], refs[in_count : in_count + out_count]
        places, marks = refs[in_count + out_count : -1], refs[-1]
        used, mark, given, arriving, leaving = 0, 0, [], [], []
        for index, (ref, item) in enumerate(zip(in_refs, ins, strict=True)):
            if index == alias:
                continue
            if isinstance(item, Near):
                given += [ref.at[at] for at in item.slices] if item.slices else [ref]
                continue
            for at in item[1]:
                copy = pltpu.make_async_copy(ref.at[at], places[used], marks.at[mark])
                copy.start()
                arriving.append(Arriving(copy, places[used]))
                given.append(arriving[-1])
                used, mark = used + 1, mark + 1
        for ref, item in zip(out_refs, outs, strict=True):
            if isinstance(item, Near):
                given += [Staying(ref.at[at]) for at in item.slices] or [Staying(ref)]
                continue
            for at in item[1]:
                copies = []
                for first in at[0] if isinstance(at[0], tuple) else (at[0],):
                    copies.append(
                        pltpu.make_async_copy(
                            places[used], ref.at[(first, *at[1:])], marks.at[mark]
                        )
                    )
                    mark += 1
                leaving.append(Leaving(copies, places[used]))
                given.append(leaving[-1])
                used += 1
        body(*given)
        for item in leaving:
            item.send()
        for item in arriving:
            item.wait()
        for item in leaving:
            for copy in item.copies:
                copy.wait()

    arrays = [item.array if isinstance(item, Near) else item[0] for item in ins]
    shapes = [item.array if isinstance(item, Near) else item[0] for item in outs]
    size = sum(x.size * x.dtype.itemsize for x in (*arrays, *shapes))
    return pl.pallas_call(
        run,
        out_shape=[
            result if isinstance(item, Near) else pltpu.HBM(result.shape, result.dtype)
            for result, item in zip(shapes, outs, strict=True)
        ],
        in_specs=[vmem if isinstance(item, Near) else hbm for item in ins],
        out_specs=[vmem if isinstance(item, Near) else hbm for item in outs],
        scratch_shapes=[*scratch, pltpu.SemaphoreType.DMA((max(marks_needed, 1),))],
        input_output_aliases={} if alias is None else {alias: 0},
        compiler_params=pltpu.CompilerParams(vmem_limit_bytes=VMEM_LIMIT),
        cost_estimate=pl.CostEstimate(flops=int(flops), bytes_accessed=size, transcendentals=0),
    )(
        *(
            array
            if isinstance(item, Near)
            else pltpu.with_memory_space_constraint(array, pltpu.HBM)
            for array, item in zip(arrays, ins, strict=True)
        )
    )


def whole(value):
    return (value, [(ALL,) * len(value.shape)])


def read_down(ref):
    return ref[...].reshape(-1, 128)


def read_up(ref):
    count, length, _ = ref.shape
    rows = 128 // count
    columns = []
    for pair in range(length // (2 * rows)):
        slab = ref[:, pair * 2 * rows : (pair + 1) * 2 * rows, :].astype(F32)
        for half in range(2):
            columns.append(
                slab[:, half * rows : (half + 1) * rows, :].reshape(128, 128).astype(BF16)
            )
    return jnp.concatenate(columns, axis=1)


def write_down(ref, value):
    value = value.astype(BF16)
    size = ref.shape[2] * ref.shape[1] // 128
    for place in range(ref.shape[0]):
        for part in range(size // 128):
            at = place * size + part * 128
            ref[place, part * 128 : (part + 1) * 128, :] = value[:, at : at + 128]


def write_up(ref, value):
    count, length, _ = ref.shape
    rows = 128 // count
    for pair in range(length // (2 * rows)):
        halves = [
            value[:, (2 * pair + half) * 128 : (2 * pair + half + 1) * 128].reshape(
                count, rows, 128
            )
            for half in range(2)
        ]
        ref[:, pair * 2 * rows : (pair + 1) * 2 * rows, :] = jnp.concatenate(
            halves, axis=1
        ).astype(BF16)


def pack_body(*refs):
    downs, ups, targets = refs[:4], refs[4:8], refs[8:16]
    for ref, target in zip(downs, targets[:4], strict=True):
        target[...] = ref[...]
    for ref, target in zip(ups, targets[4:], strict=True):
        rows, width = ref.shape
        value = ref[...].astype(F32)
        for pair in range(width // 256):
            halves = [
                value[:, (2 * pair + half) * 128 : (2 * pair + half + 1) * 128]
                for half in range(2)
            ]
            target[pair * 2 * rows : (pair + 1) * 2 * rows, :] = jnp.concatenate(
                halves, axis=0
            ).astype(BF16)


def unpack_body(*refs):
    for place, (came, ref) in enumerate(zip(refs[:8], refs[8:], strict=True)):
        value = came[...].astype(F32)
        if place % 4 < 2:
            for part in range(value.shape[0] // 128):
                at = slice(part * 128, (part + 1) * 128)
                ref[at, :] = jnp.transpose(value[at])
        else:
            rows, width = ref.shape
            for tile in range(width // 128):
                ref[:, tile * 128 : (tile + 1) * 128] = value[tile * rows : (tile + 1) * rows]
        ref.send()


def first_body(
    parent_ref, hidden_ref, cot_ref, gain0_ref, gain1_ref, down0_ref, down1_ref, up0_ref, up1_ref,
    sent_ref, bias_ref,
):
    lane = lax.broadcasted_iota(jnp.int32, (128, 128), 1)
    line = lax.broadcasted_iota(jnp.int32, (128, 128), 0)
    linked = (lane == line) | (jnp.broadcast_to(parent_ref[...], (128, 128)) == line)
    reached = jnp.where(linked, 1.0, 0.0).astype(BF16)
    for _ in range(7):
        reached = jnp.minimum(dot(reached, reached), 1.0).astype(BF16)
    bias_ref[...] = jnp.where(jnp.transpose(reached.astype(F32)) > 0.5, 0.0, -1e30)
    def send(start, value):
        value = value.astype(BF16)
        for peer in range(sent_ref.shape[0]):
            sent_ref[peer, start : start + value.shape[0], :] = value

    hidden, gain1 = hidden_ref[...], gain1_ref[...]
    wide = hidden.astype(F32)
    down1, up0, cot = read_down(down1_ref), read_up(up0_ref), cot_ref[...]
    send(PROJECTED0, dot((wide * gain0_ref[...]).astype(BF16), read_down(down0_ref)))
    send(PROJECTED1, dot((wide * gain1).astype(BF16), down1))
    send(CROSS, dot((up0.astype(F32) * gain1).astype(BF16), down1))
    send(BACK_OUTPUT1, dot_cols(cot, read_up(up1_ref)))
    send(HIDDEN_UP, dot_cols(hidden, up0))
    send(GRAM, dot_cols(up0, up0))
    send(BACK_OUTPUT0, dot_cols(cot, up0))
    squares = lax.dot_general(
        jnp.ones((16, hidden.shape[1]), F32),
        wide * wide,
        (((1,), (1,)), ((), ())),
        preferred_element_type=F32,
        precision=lax.Precision.HIGHEST,
    )
    high = squares.astype(BF16)
    rest = squares - high.astype(F32)
    middle = rest.astype(BF16)
    send(SQUARES, high)
    send(SQUARES + 16, middle)
    send(SQUARES + 32, rest - middle.astype(F32))


def to_column(row):
    lane = lax.broadcasted_iota(jnp.int32, (128, 128), 1)
    line = lax.broadcasted_iota(jnp.int32, (128, 128), 0)
    return row_sum(jnp.where(lane == line, jnp.broadcast_to(row, (128, 128)), 0.0))


def total(ref, start=0, rows=128):
    value = ref[0, start : start + rows, :].astype(F32)
    for peer in range(1, ref.shape[0]):
        value = value + ref[peer, start : start + rows, :].astype(F32)
    return value


def head_blocks(query_ref, key_ref):
    heads = query_ref.shape[-1] // HEAD_DIM
    groups = key_ref.shape[-1] // HEAD_DIM
    share = heads // groups
    return [
        (head, slice((head // share) * HEAD_DIM, (head // share + 1) * HEAD_DIM))
        for head in range(0, heads, HEADS_AT_ONCE)
    ]


def stacked(value, head):
    return jnp.concatenate(
        [
            value[:, (head + k) * HEAD_DIM : (head + k + 1) * HEAD_DIM]
            for k in range(HEADS_AT_ONCE)
        ],
        axis=0,
    )


def spread(ref, head, value):
    for k in range(HEADS_AT_ONCE):
        ref[:, (head + k) * HEAD_DIM : (head + k + 1) * HEAD_DIM] = value[k * 128 : (k + 1) * 128]


def softmax_of(queries, keys, bias):
    scores = dot_cols(queries, keys) * HEAD_DIM ** (-0.5) + bias
    weights = jnp.exp(scores - jnp.max(scores, axis=1, keepdims=True))
    return weights * (1.0 / row_sum(weights))


def score_back(back_attended, probability, keys, values):
    back_probability = dot_cols(back_attended, values)
    back_scores = probability * (back_probability - row_sum(probability * back_probability))
    return (dot(back_scores.astype(BF16), keys) * HEAD_DIM ** (-0.5)).astype(BF16)


def layer0_body(
    came_ref, query_ref, up_query_ref, key_ref, value_ref, bias_ref, down_output_ref,
    sent_ref, attended_ref, probability_ref, rank_ref, small_ref, far_small_ref,
):
    projected = total(came_ref, PROJECTED0)
    squares = to_column(
        (
            total(came_ref, SQUARES, 16)
            + total(came_ref, SQUARES + 16, 16)
            + total(came_ref, SQUARES + 32, 16)
        )[:1]
    )
    scale = lax.rsqrt(squares / D + EPSILON)
    rank_query = (scale * projected).astype(BF16)
    rank_ref[...] = rank_query
    small_ref[0] = projected
    small_ref[1] = jnp.broadcast_to(scale, (128, 128))
    small_ref[2] = jnp.broadcast_to(squares, (128, 128))
    far_small_ref[0] = projected
    far_small_ref[1] = jnp.broadcast_to(scale, (128, 128))
    rank_ref.send()
    far_small_ref.send()
    bias = jnp.concatenate([bias_ref[...]] * HEADS_AT_ONCE, axis=0)
    queries = (query_ref[...].astype(F32) + dot(rank_query, read_up(up_query_ref))).astype(BF16)
    for head, shared in head_blocks(query_ref, key_ref):
        probability = softmax_of(stacked(queries, head), key_ref[:, shared], bias)
        probability_ref[head * 128 : (head + HEADS_AT_ONCE) * 128, :] = probability
        spread(
            attended_ref, head, dot(probability.astype(BF16), value_ref[:, shared]).astype(BF16)
        )
    probability_ref.send()
    attended_ref.send()
    rank_output = dot(attended_ref[...], read_down(down_output_ref)).astype(BF16)
    for peer in range(sent_ref.shape[0]):
        sent_ref[peer] = rank_output


def layer1_body(
    came_ref, first_ref, small0_ref, query_ref, up_ref, key_ref, value_ref, bias_ref, down_ref,
    sent_ref, attended_ref, back_query_ref, ranks_ref, small_ref, scale_ref,
):
    rank_output0 = total(came_ref).astype(BF16)
    cross = total(first_ref, CROSS)
    projected = total(first_ref, PROJECTED1) + dot(rank_output0, cross.astype(BF16))
    back_rank_output = total(first_ref, BACK_OUTPUT1).astype(BF16)
    hidden_up = total(first_ref, HIDDEN_UP)
    gram = total(first_ref, GRAM)
    gram_high = gram.astype(BF16)
    gram_low = (gram - gram_high.astype(F32)).astype(BF16)
    output_gram = dot(rank_output0, gram_high) + dot(rank_output0, gram_low)
    squares = small0_ref[2, :, :1] + row_sum(
        rank_output0.astype(F32) * (2.0 * hidden_up + output_gram)
    )
    scale = lax.rsqrt(jnp.maximum(squares, 0.0) / D + EPSILON)
    rank_query = (scale * projected).astype(BF16)
    ranks_ref[0] = rank_output0
    ranks_ref[1] = rank_query
    ranks_ref[2] = back_rank_output
    ranks_ref.send()
    small_ref[0] = projected
    small_ref[1] = jnp.broadcast_to(scale, (128, 128))
    small_ref[2] = cross
    small_ref[3] = hidden_up + output_gram
    scale_ref[...] = jnp.broadcast_to(scale, (128, 128))
    scale_ref.send()
    bias = jnp.concatenate([bias_ref[...]] * HEADS_AT_ONCE, axis=0)
    up_query = read_up(up_ref)
    queries = (query_ref[...].astype(F32) + dot(rank_query, up_query)).astype(BF16)
    down_output = read_down(down_ref)
    back_attended = dot_cols(back_rank_output, down_output).astype(BF16)
    for head, shared in head_blocks(query_ref, key_ref):
        keys, values = key_ref[:, shared], value_ref[:, shared]
        probability = softmax_of(stacked(queries, head), keys, bias)
        spread(attended_ref, head, dot(probability.astype(BF16), values).astype(BF16))
        spread(
            back_query_ref, head, score_back(stacked(back_attended, head), probability, keys, values)
        )
    attended_ref.send()
    back_query_ref.send()
    rank_output = dot(attended_ref[...], down_output).astype(BF16)
    back_rank = dot_cols(back_query_ref[...], up_query).astype(BF16)
    for peer in range(sent_ref.shape[0]):
        sent_ref[peer, :128, :] = rank_output
        sent_ref[peer, 128:, :] = back_rank


def backward0_body(
    came_ref, first_ref, small_ref, down_ref, key_ref, value_ref, probability_ref, up_ref,
    sent_ref, back_query_ref, ranks_ref, pull_ref,
):
    back_rank1 = total(came_ref, 128).astype(BF16)
    scale = small_ref[1, :, :1]
    along = row_sum(back_rank1.astype(F32) * small_ref[0]) / D
    pull = scale * scale * scale * along
    back_output = (
        total(first_ref, BACK_OUTPUT0)
        + scale * dot_cols(back_rank1, small_ref[2].astype(BF16))
        - pull * small_ref[3]
    ).astype(BF16)
    ranks_ref[0] = total(came_ref).astype(BF16)
    ranks_ref[1] = back_rank1
    ranks_ref[2] = back_output
    ranks_ref.send()
    pull_ref[...] = jnp.broadcast_to(pull, (128, 128))
    pull_ref.send()
    back_attended = dot_cols(back_output, read_down(down_ref)).astype(BF16)
    for head, shared in head_blocks(back_query_ref, key_ref):
        spread(
            back_query_ref,
            head,
            score_back(
                stacked(back_attended, head),
                probability_ref[head * 128 : (head + HEADS_AT_ONCE) * 128, :],
                key_ref[:, shared],
                value_ref[:, shared],
            ),
        )
    back_query_ref.send()
    back_rank = dot_cols(back_query_ref[...], read_up(up_ref)).astype(BF16)
    sent_ref[...] = back_rank


def terms_body(
    ranks1_ref, ranks2_ref, scale_ref, pull_ref, gain_ref, cot_ref, hidden_ref, up0_ref, down1_ref,
    attended0_ref, attended1_ref, rank0_ref, back_query0_ref, back_query1_ref, small0_ref,
    gain0_ref, a_query1, b_query0, b_query1, a_out0, a_out1, b_out0, b_out1, normed0_ref,
):
    rank_output0, rank_query1, back_output1 = ranks1_ref[0], ranks1_ref[1], ranks1_ref[2]
    rank_output1, back_rank1, back_output0 = ranks2_ref[0], ranks2_ref[1], ranks2_ref[2]
    cot = cot_ref[...]
    write_up(b_out1, dot_rows(rank_output1, cot))
    b_out1.send()
    gain, scale, pull = gain_ref[...], scale_ref[:, :1], pull_ref[:, :1]
    hidden = hidden_ref[...].astype(F32)
    normed0_ref[...] = (hidden * small0_ref[1, :, :1] * gain0_ref[...]).astype(BF16)
    hidden = hidden + dot(rank_output0, read_up(up0_ref))
    write_down(a_query1, dot_rows(back_rank1, (hidden * scale * gain).astype(BF16)))
    a_query1.send()
    gained = gain * dot_cols(back_rank1, read_down(down1_ref))
    gradient = cot.astype(F32) + scale * gained - hidden * pull
    write_up(b_out0, dot_rows(rank_output0, gradient.astype(BF16)))
    b_out0.send()
    write_down(a_out0, dot_rows(back_output0, attended0_ref[...]))
    a_out0.send()
    write_down(a_out1, dot_rows(back_output1, attended1_ref[...]))
    a_out1.send()
    write_up(b_query1, dot_rows(rank_query1, back_query1_ref[...]))
    b_query1.send()
    write_up(b_query0, dot_rows(rank0_ref[...], back_query0_ref[...]))


def last_term_body(came_ref, normed_ref, a_query0, back_rank_ref):
    back_rank = total(came_ref).astype(BF16)
    back_rank_ref[...] = back_rank
    back_rank_ref.send()
    write_down(a_query0, dot_rows(back_rank, normed_ref[...]))


def rows_body(
    back_rank_ref, small_ref, gain0_ref, down0_ref, hidden_ref, cot_ref, gain1_ref, scale_ref,
    pull_ref, ranks1_ref, ranks2_ref, up0_ref, down1_ref, up1_ref, out_ref, cot_send_ref,
):
    hidden0 = hidden_ref[...].astype(F32)
    hidden1 = hidden0 + dot(ranks1_ref[0], read_up(up0_ref))
    out_ref[...] = (hidden1 + dot(ranks2_ref[0], read_up(up1_ref))).astype(BF16)
    out_ref.send()
    gained = gain1_ref[...] * dot_cols(ranks2_ref[1], read_down(down1_ref))
    gradient = (
        cot_ref[...].astype(F32) + scale_ref[:, :1] * gained - hidden1 * pull_ref[:, :1]
    )
    back_rank = back_rank_ref[...]
    scale = small_ref[1, :, :1]
    along = row_sum(back_rank.astype(F32) * small_ref[0]) / D
    gained = gain0_ref[...] * dot_cols(back_rank, read_down(down0_ref))
    cot_send_ref[...] = (
        gradient + scale * gained - hidden0 * (scale * scale * scale * along)
    ).astype(BF16)


def swap(value, axis):
    return lax.all_to_all(value, axis, 0, 0, tiled=True)


def on_device(
    arrived, cot_later, q_base, k_base, v_base, gains, parents, a_query, b_query, a_out, b_out
):
    ways = lax.axis_size("tensor")
    count = lax.axis_size("dp")
    rows, width = b_query.shape[1], arrived.shape[1]
    length = rows * width // 128
    heads = width // HEAD_DIM
    block = whole(shape((128, width), BF16))
    layer0, layer1 = [(0,)], [(1,)]
    gain0, gain1 = (gains, [(slice(0, 1),)]), (gains, [(slice(1, 2),)])
    peers = [(tuple(range(ways)),)]

    (shard,) = kernel_call(
        pack_body,
        [(array, [(0,), (1,)]) for array in (a_query, a_out, b_query, b_out)],
        [Near(shape((8, length, 128), BF16), *[(member,) for member in range(8)])],
        0,
    )
    shard = (shard.astype(F32) * SCALE_UP).astype(jnp.float16)
    stack = lax.all_gather(shard, "dp", axis=0, tiled=False)
    stack = (stack.astype(F32) * (1.0 / SCALE_UP)).astype(BF16)

    def factor(*members):
        return (stack, [(ALL, member) for member in members])

    def near_factor(*members):
        return Near(stack, *[(ALL, member) for member in members])

    hidden = from_behind(arrived, "section", 1)
    cot = from_behind(cot_later, "section", -1)
    near_gain0, near_gain1 = Near(gains, (slice(0, 1),)), Near(gains, (slice(1, 2),))
    sent, bias = kernel_call(
        first_body,
        [
            Near(parents.reshape(1, 128)), Near(hidden), Near(cot), near_gain0, near_gain1,
            near_factor(A_QUERY0, A_QUERY1, B_OUT0, B_OUT1),
        ],
        [Near(shape((ways, SQUARES + 48, 128), BF16)), Near(shape((128, 128), F32))],
        6e8,
    )
    first = swap(sent, "tensor")
    sent, attended0, probability, rank_query0, small0, far_small0 = kernel_call(
        layer0_body,
        [
            Near(first), Near(q_base, (0,)), near_factor(B_QUERY0), Near(k_base, (0,)),
            Near(v_base, (0,)), Near(bias), near_factor(A_OUT0),
        ],
        [
            Near(shape((ways, 128, 128), BF16)),
            block,
            Near(shape((heads * 128, 128), F32)),
            whole(shape((128, 128), BF16)),
            Near(shape((3, 128, 128), F32)),
            whole(shape((2, 128, 128), F32)),
        ],
        9e8,
    )
    came = swap(sent, "tensor")
    sent, attended1, back_query1, ranks1, small1, scale1 = kernel_call(
        layer1_body,
        [
            Near(came), Near(first), Near(small0), Near(q_base, (1,)), near_factor(B_QUERY1),
            Near(k_base, (1,)), Near(v_base, (1,)), Near(bias), near_factor(A_OUT1),
        ],
        [
            Near(shape((ways, 256, 128), BF16)),
            block,
            block,
            whole(shape((3, 128, 128), BF16)),
            Near(shape((4, 128, 128), F32)),
            whole(shape((128, 128), F32)),
        ],
        8e8,
    )
    came = swap(sent, "tensor")
    sent, back_query0, ranks2, pull = kernel_call(
        backward0_body,
        [
            Near(came), Near(first), Near(small1), near_factor(A_OUT0), Near(k_base, (0,)),
            Near(v_base, (0,)), Near(probability), near_factor(B_QUERY0),
        ],
        [
            (shape((ways, 128, 128), BF16), peers),
            block,
            whole(shape((3, 128, 128), BF16)),
            whole(shape((128, 128), F32)),
        ],
        4e8,
    )
    came = swap(sent, "tensor")
    term_shape = shape((count, 8, length, 128), BF16)
    made_first = (
        TERM_A_QUERY + 1, TERM_B_QUERY, TERM_B_QUERY + 1, TERM_A_OUT, TERM_A_OUT + 1,
        TERM_B_OUT, TERM_B_OUT + 1,
    )
    terms, normed0 = kernel_call(
        terms_body,
        [
            whole(ranks1), whole(ranks2), whole(scale1), whole(pull), gain1, whole(cot),
            whole(hidden), factor(B_OUT0, A_QUERY1), whole(attended0), whole(attended1),
            whole(rank_query0), whole(back_query0), whole(back_query1), whole(far_small0), gain0,
        ],
        [
            (term_shape, [(ALL, member) for member in made_first]),
            Near(block[0]),
        ],
        1e9,
    )
    terms, back_rank0 = kernel_call(
        last_term_body,
        [Near(came), Near(normed0), whole(terms)],
        [(term_shape, [(ALL, TERM_A_QUERY)]), whole(shape((128, 128), BF16))],
        1e8,
        alias=2,
    )
    reduced = lax.psum_scatter(terms, "dp", scatter_dimension=0, tiled=False)
    section_out, cot_send = kernel_call(
        rows_body,
        [
            whole(back_rank0), whole(far_small0), gain0, factor(A_QUERY0), whole(hidden),
            whole(cot), gain1, whole(scale1), whole(pull), whole(ranks1), whole(ranks2),
            factor(B_OUT0, A_QUERY1, B_OUT1),
        ],
        [block, block],
        4e8,
    )
    down, up = shape((2, length, 128), F32), shape((2, rows, width), F32)
    grads = kernel_call(
        unpack_body,
        [(reduced, [(member,) for member in range(8)])],
        [(result, [(0,), (1,)]) for result in (down, up, down, up)],
        0,
    )
    return (section_out, cot_send, *grads)


def solution(mesh):
    in_specs = (
        P(("section", "dp"), "tensor"),
        P(("section", "dp"), "tensor"),
        P(None, ("section", "dp"), "tensor"),
        P(None, ("section", "dp"), "tensor"),
        P(None, ("section", "dp"), "tensor"),
        P("section", "tensor"),
        P(("section", "dp")),
        P("section", ("tensor", "dp"), None),
        P("section", "dp", "tensor"),
        P("section", ("tensor", "dp"), None),
        P("section", "dp", "tensor"),
    )
    out_specs = (
        P(("section", "dp"), "tensor"),
        P(("section", "dp"), "tensor"),
        P("section", ("tensor", "dp"), None),
        P("section", "dp", "tensor"),
        P("section", ("tensor", "dp"), None),
        P("section", "dp", "tensor"),
    )
    return jax.shard_map(
        on_device, mesh=mesh, in_specs=in_specs, out_specs=out_specs, check_vma=False
    )
```

```python
import jax
import jax.numpy as jnp
from jax import lax
from jax.experimental import pallas as pl
from jax.experimental.pallas import tpu as pltpu
from jax.sharding import PartitionSpec as P

D = 8192
HEAD_DIM = 128
HEADS_AT_ONCE = 4
EPSILON = 1e-05
F32 = jnp.float32
BF16 = jnp.bfloat16
VMEM_LIMIT = 20 << 20
ALL = slice(None)
(A_QUERY0, A_QUERY1, A_OUT0, A_OUT1, B_QUERY0, B_QUERY1, B_OUT0, B_OUT1) = range(8)
PROJECTED0, PROJECTED1, CROSS, BACK_OUTPUT1, HIDDEN_UP, GRAM, BACK_OUTPUT0, SQUARES = range(
    0, 1024, 128
)
SCALE_UP = 65536.0
TERM_A_QUERY, TERM_B_QUERY, TERM_A_OUT, TERM_B_OUT = 0, 2, 4, 6


def from_behind(value, axis, steps):
    count = lax.axis_size(axis)
    pairs = [(source, (source + steps) % count) for source in range(count)]
    return lax.ppermute(value, axis, pairs)


def dot(left, right):
    return jnp.dot(left, right, preferred_element_type=F32)


def dot_rows(left, right):
    return lax.dot_general(left, right, (((0,), (0,)), ((), ())), preferred_element_type=F32)


def dot_cols(left, right):
    return lax.dot_general(left, right, (((1,), (1,)), ((), ())), preferred_element_type=F32)


def row_sum(value):
    return jnp.sum(value, axis=1, keepdims=True)


def shape(dims, dtype):
    return jax.ShapeDtypeStruct(dims, dtype)


class Arriving:
    def __init__(self, copy, ref):
        self.copy, self.ref, self.waited = copy, ref, False
        self.shape = ref.shape

    def wait(self):
        if not self.waited:
            self.copy.wait()
            self.waited = True

    def __getitem__(self, at):
        self.wait()
        return self.ref[at]


class Leaving:
    def __init__(self, copies, ref):
        self.copies, self.ref, self.sent = copies, ref, False
        self.shape = ref.shape

    def send(self):
        if not self.sent:
            for copy in self.copies:
                copy.start()
            self.sent = True

    def __setitem__(self, at, value):
        self.ref[at] = value

    def __getitem__(self, at):
        return self.ref[at]


class Staying:
    def __init__(self, ref):
        self.ref = ref
        self.shape = ref.shape

    def send(self):
        pass

    def __setitem__(self, at, value):
        self.ref[at] = value

    def __getitem__(self, at):
        return self.ref[at]


def sliced(dims, at):
    at = at + (ALL,) * (len(dims) - len(at))
    result = []
    for size, entry in zip(dims, at, strict=True):
        if isinstance(entry, slice):
            result.append(len(range(*entry.indices(size))))
    return tuple(result)


class Near:
    def __init__(self, array, *slices):
        self.array, self.slices = array, slices


def kernel_call(body, ins, outs, flops, alias=None):
    hbm, vmem = pl.BlockSpec(memory_space=pltpu.HBM), pl.BlockSpec(memory_space=pltpu.VMEM)
    scratch, marks_needed, in_count, out_count = [], 0, len(ins), len(outs)
    for index, item in enumerate(ins):
        if index != alias and not isinstance(item, Near):
            scratch += [pltpu.VMEM(sliced(item[0].shape, at), item[0].dtype) for at in item[1]]
            marks_needed += len(item[1])
    for item in outs:
        if not isinstance(item, Near):
            for at in item[1]:
                copies = at[0] if isinstance(at[0], tuple) else (at[0],)
                marks_needed += len(copies)
                scratch.append(
                    pltpu.VMEM(sliced(item[0].shape, (copies[0], *at[1:])), item[0].dtype)
                )

    def run(*refs):
        in_refs, out_refs = refs[:in_count], refs[in_count : in_count + out_count]
        places, marks = refs[in_count + out_count : -1], refs[-1]
        used, mark, given, arriving, leaving = 0, 0, [], [], []
        for index, (ref, item) in enumerate(zip(in_refs, ins, strict=True)):
            if index == alias:
                continue
            if isinstance(item, Near):
                given += [ref.at[at] for at in item.slices] if item.slices else [ref]
                continue
            for at in item[1]:
                copy = pltpu.make_async_copy(ref.at[at], places[used], marks.at[mark])
                copy.start()
                arriving.append(Arriving(copy, places[used]))
                given.append(arriving[-1])
                used, mark = used + 1, mark + 1
        for ref, item in zip(out_refs, outs, strict=True):
            if isinstance(item, Near):
                given += [Staying(ref.at[at]) for at in item.slices] or [Staying(ref)]
                continue
            for at in item[1]:
                copies = []
                for first in at[0] if isinstance(at[0], tuple) else (at[0],):
                    copies.append(
                        pltpu.make_async_copy(
                            places[used], ref.at[(first, *at[1:])], marks.at[mark]
                        )
                    )
                    mark += 1
                leaving.append(Leaving(copies, places[used]))
                given.append(leaving[-1])
                used += 1
        body(*given)
        for item in leaving:
            item.send()
        for item in arriving:
            item.wait()
        for item in leaving:
            for copy in item.copies:
                copy.wait()

    arrays = [item.array if isinstance(item, Near) else item[0] for item in ins]
    shapes = [item.array if isinstance(item, Near) else item[0] for item in outs]
    size = sum(x.size * x.dtype.itemsize for x in (*arrays, *shapes))
    return pl.pallas_call(
        run,
        out_shape=[
            result if isinstance(item, Near) else pltpu.HBM(result.shape, result.dtype)
            for result, item in zip(shapes, outs, strict=True)
        ],
        in_specs=[vmem if isinstance(item, Near) else hbm for item in ins],
        out_specs=[vmem if isinstance(item, Near) else hbm for item in outs],
        scratch_shapes=[*scratch, pltpu.SemaphoreType.DMA((max(marks_needed, 1),))],
        input_output_aliases={} if alias is None else {alias: 0},
        compiler_params=pltpu.CompilerParams(vmem_limit_bytes=VMEM_LIMIT),
        cost_estimate=pl.CostEstimate(flops=int(flops), bytes_accessed=size, transcendentals=0),
    )(
        *(
            array
            if isinstance(item, Near)
            else pltpu.with_memory_space_constraint(array, pltpu.HBM)
            for array, item in zip(arrays, ins, strict=True)
        )
    )


def whole(value):
    return (value, [(ALL,) * len(value.shape)])


def read_down(ref):
    return ref[...].reshape(-1, 128)


def read_up(ref):
    count, length, _ = ref.shape
    rows = 128 // count
    columns = []
    for pair in range(length // (2 * rows)):
        slab = ref[:, pair * 2 * rows : (pair + 1) * 2 * rows, :].astype(F32)
        for half in range(2):
            columns.append(
                slab[:, half * rows : (half + 1) * rows, :].reshape(128, 128).astype(BF16)
            )
    return jnp.concatenate(columns, axis=1)


def write_down(ref, value):
    value = value.astype(BF16)
    size = ref.shape[2] * ref.shape[1] // 128
    for place in range(ref.shape[0]):
        for part in range(size // 128):
            at = place * size + part * 128
            ref[place, part * 128 : (part + 1) * 128, :] = value[:, at : at + 128]


def write_up(ref, value):
    count, length, _ = ref.shape
    rows = 128 // count
    for pair in range(length // (2 * rows)):
        halves = [
            value[:, (2 * pair + half) * 128 : (2 * pair + half + 1) * 128].reshape(
                count, rows, 128
            )
            for half in range(2)
        ]
        ref[:, pair * 2 * rows : (pair + 1) * 2 * rows, :] = jnp.concatenate(
            halves, axis=1
        ).astype(BF16)


def pack_body(*refs):
    downs, ups, targets = refs[:4], refs[4:8], refs[8:16]
    for ref, target in zip(downs, targets[:4], strict=True):
        target[...] = ref[...]
    for ref, target in zip(ups, targets[4:], strict=True):
        rows, width = ref.shape
        value = ref[...].astype(F32)
        for pair in range(width // 256):
            halves = [
                value[:, (2 * pair + half) * 128 : (2 * pair + half + 1) * 128]
                for half in range(2)
            ]
            target[pair * 2 * rows : (pair + 1) * 2 * rows, :] = jnp.concatenate(
                halves, axis=0
            ).astype(BF16)


def unpack_body(came, a_query_ref, b_query_ref, a_out_ref, b_out_ref):
    for layer in range(2):
        for ref, place in ((a_query_ref, TERM_A_QUERY), (a_out_ref, TERM_A_OUT)):
            value = came[place + layer].astype(F32)
            for part in range(value.shape[0] // 128):
                at = slice(part * 128, (part + 1) * 128)
                ref[layer, at, :] = jnp.transpose(value[at])
        for ref, place in ((b_query_ref, TERM_B_QUERY), (b_out_ref, TERM_B_OUT)):
            rows, width = ref.shape[1:]
            value = came[place + layer].astype(F32)
            for tile in range(width // 128):
                ref[layer, :, tile * 128 : (tile + 1) * 128] = value[
                    tile * rows : (tile + 1) * rows
                ]


def first_body(
    parent_ref, hidden_ref, cot_ref, gain0_ref, gain1_ref, down0_ref, down1_ref, up0_ref, up1_ref,
    sent_ref, bias_ref,
):
    lane = lax.broadcasted_iota(jnp.int32, (128, 128), 1)
    line = lax.broadcasted_iota(jnp.int32, (128, 128), 0)
    linked = (lane == line) | (jnp.broadcast_to(parent_ref[...], (128, 128)) == line)
    reached = jnp.where(linked, 1.0, 0.0).astype(BF16)
    for _ in range(7):
        reached = jnp.minimum(dot(reached, reached), 1.0).astype(BF16)
    bias_ref[...] = jnp.where(jnp.transpose(reached.astype(F32)) > 0.5, 0.0, -1e30)
    def send(start, value):
        value = value.astype(BF16)
        for peer in range(sent_ref.shape[0]):
            sent_ref[peer, start : start + value.shape[0], :] = value

    hidden, gain1 = hidden_ref[...], gain1_ref[...]
    wide = hidden.astype(F32)
    down1, up0, cot = read_down(down1_ref), read_up(up0_ref), cot_ref[...]
    send(PROJECTED0, dot((wide * gain0_ref[...]).astype(BF16), read_down(down0_ref)))
    send(PROJECTED1, dot((wide * gain1).astype(BF16), down1))
    send(CROSS, dot((up0.astype(F32) * gain1).astype(BF16), down1))
    send(BACK_OUTPUT1, dot_cols(cot, read_up(up1_ref)))
    send(HIDDEN_UP, dot_cols(hidden, up0))
    send(GRAM, dot_cols(up0, up0))
    send(BACK_OUTPUT0, dot_cols(cot, up0))
    squares = lax.dot_general(
        jnp.ones((16, hidden.shape[1]), F32),
        wide * wide,
        (((1,), (1,)), ((), ())),
        preferred_element_type=F32,
        precision=lax.Precision.HIGHEST,
    )
    high = squares.astype(BF16)
    rest = squares - high.astype(F32)
    middle = rest.astype(BF16)
    send(SQUARES, high)
    send(SQUARES + 16, middle)
    send(SQUARES + 32, rest - middle.astype(F32))


def to_column(row):
    lane = lax.broadcasted_iota(jnp.int32, (128, 128), 1)
    line = lax.broadcasted_iota(jnp.int32, (128, 128), 0)
    return row_sum(jnp.where(lane == line, jnp.broadcast_to(row, (128, 128)), 0.0))


def total(ref, start=0, rows=128):
    value = ref[0, start : start + rows, :].astype(F32)
    for peer in range(1, ref.shape[0]):
        value = value + ref[peer, start : start + rows, :].astype(F32)
    return value


def head_blocks(query_ref, key_ref):
    heads = query_ref.shape[-1] // HEAD_DIM
    groups = key_ref.shape[-1] // HEAD_DIM
    share = heads // groups
    return [
        (head, slice((head // share) * HEAD_DIM, (head // share + 1) * HEAD_DIM))
        for head in range(0, heads, HEADS_AT_ONCE)
    ]


def stacked(value, head):
    return jnp.concatenate(
        [
            value[:, (head + k) * HEAD_DIM : (head + k + 1) * HEAD_DIM]
            for k in range(HEADS_AT_ONCE)
        ],
        axis=0,
    )


def spread(ref, head, value):
    for k in range(HEADS_AT_ONCE):
        ref[:, (head + k) * HEAD_DIM : (head + k + 1) * HEAD_DIM] = value[k * 128 : (k + 1) * 128]


def softmax_of(queries, keys, bias):
    scores = dot_cols(queries, keys) * HEAD_DIM ** (-0.5) + bias
    weights = jnp.exp(scores - jnp.max(scores, axis=1, keepdims=True))
    return weights * (1.0 / row_sum(weights))


def score_back(back_attended, probability, keys, values):
    back_probability = dot_cols(back_attended, values)
    back_scores = probability * (back_probability - row_sum(probability * back_probability))
    return (dot(back_scores.astype(BF16), keys) * HEAD_DIM ** (-0.5)).astype(BF16)


def layer0_body(
    came_ref, query_ref, up_query_ref, key_ref, value_ref, bias_ref, down_output_ref,
    sent_ref, attended_ref, probability_ref, rank_ref, small_ref, far_small_ref,
):
    projected = total(came_ref, PROJECTED0)
    squares = to_column(
        (
            total(came_ref, SQUARES, 16)
            + total(came_ref, SQUARES + 16, 16)
            + total(came_ref, SQUARES + 32, 16)
        )[:1]
    )
    scale = lax.rsqrt(squares / D + EPSILON)
    rank_query = (scale * projected).astype(BF16)
    rank_ref[...] = rank_query
    small_ref[0] = projected
    small_ref[1] = jnp.broadcast_to(scale, (128, 128))
    small_ref[2] = jnp.broadcast_to(squares, (128, 128))
    far_small_ref[0] = projected
    far_small_ref[1] = jnp.broadcast_to(scale, (128, 128))
    rank_ref.send()
    far_small_ref.send()
    bias = jnp.concatenate([bias_ref[...]] * HEADS_AT_ONCE, axis=0)
    queries = (query_ref[...].astype(F32) + dot(rank_query, read_up(up_query_ref))).astype(BF16)
    for head, shared in head_blocks(query_ref, key_ref):
        probability = softmax_of(stacked(queries, head), key_ref[:, shared], bias)
        probability_ref[head * 128 : (head + HEADS_AT_ONCE) * 128, :] = probability
        spread(
            attended_ref, head, dot(probability.astype(BF16), value_ref[:, shared]).astype(BF16)
        )
    probability_ref.send()
    attended_ref.send()
    rank_output = dot(attended_ref[...], read_down(down_output_ref)).astype(BF16)
    for peer in range(sent_ref.shape[0]):
        sent_ref[peer] = rank_output


def layer1_body(
    came_ref, first_ref, small0_ref, query_ref, up_ref, key_ref, value_ref, bias_ref, down_ref,
    sent_ref, attended_ref, back_query_ref, ranks_ref, small_ref, scale_ref,
):
    rank_output0 = total(came_ref).astype(BF16)
    cross = total(first_ref, CROSS)
    projected = total(first_ref, PROJECTED1) + dot(rank_output0, cross.astype(BF16))
    back_rank_output = total(first_ref, BACK_OUTPUT1).astype(BF16)
    hidden_up = total(first_ref, HIDDEN_UP)
    gram = total(first_ref, GRAM)
    gram_high = gram.astype(BF16)
    gram_low = (gram - gram_high.astype(F32)).astype(BF16)
    output_gram = dot(rank_output0, gram_high) + dot(rank_output0, gram_low)
    squares = small0_ref[2, :, :1] + row_sum(
        rank_output0.astype(F32) * (2.0 * hidden_up + output_gram)
    )
    scale = lax.rsqrt(jnp.maximum(squares, 0.0) / D + EPSILON)
    rank_query = (scale * projected).astype(BF16)
    ranks_ref[0] = rank_output0
    ranks_ref[1] = rank_query
    ranks_ref[2] = back_rank_output
    ranks_ref.send()
    small_ref[0] = projected
    small_ref[1] = jnp.broadcast_to(scale, (128, 128))
    small_ref[2] = cross
    small_ref[3] = hidden_up + output_gram
    scale_ref[...] = jnp.broadcast_to(scale, (128, 128))
    scale_ref.send()
    bias = jnp.concatenate([bias_ref[...]] * HEADS_AT_ONCE, axis=0)
    up_query = read_up(up_ref)
    queries = (query_ref[...].astype(F32) + dot(rank_query, up_query)).astype(BF16)
    down_output = read_down(down_ref)
    back_attended = dot_cols(back_rank_output, down_output).astype(BF16)
    for head, shared in head_blocks(query_ref, key_ref):
        keys, values = key_ref[:, shared], value_ref[:, shared]
        probability = softmax_of(stacked(queries, head), keys, bias)
        spread(attended_ref, head, dot(probability.astype(BF16), values).astype(BF16))
        spread(
            back_query_ref, head, score_back(stacked(back_attended, head), probability, keys, values)
        )
    attended_ref.send()
    back_query_ref.send()
    rank_output = dot(attended_ref[...], down_output).astype(BF16)
    back_rank = dot_cols(back_query_ref[...], up_query).astype(BF16)
    for peer in range(sent_ref.shape[0]):
        sent_ref[peer, :128, :] = rank_output
        sent_ref[peer, 128:, :] = back_rank


def backward0_body(
    came_ref, first_ref, small_ref, down_ref, key_ref, value_ref, probability_ref, up_ref,
    sent_ref, back_query_ref, ranks_ref, pull_ref,
):
    back_rank1 = total(came_ref, 128).astype(BF16)
    scale = small_ref[1, :, :1]
    along = row_sum(back_rank1.astype(F32) * small_ref[0]) / D
    pull = scale * scale * scale * along
    back_output = (
        total(first_ref, BACK_OUTPUT0)
        + scale * dot_cols(back_rank1, small_ref[2].astype(BF16))
        - pull * small_ref[3]
    ).astype(BF16)
    ranks_ref[0] = total(came_ref).astype(BF16)
    ranks_ref[1] = back_rank1
    ranks_ref[2] = back_output
    ranks_ref.send()
    pull_ref[...] = jnp.broadcast_to(pull, (128, 128))
    pull_ref.send()
    back_attended = dot_cols(back_output, read_down(down_ref)).astype(BF16)
    for head, shared in head_blocks(back_query_ref, key_ref):
        spread(
            back_query_ref,
            head,
            score_back(
                stacked(back_attended, head),
                probability_ref[head * 128 : (head + HEADS_AT_ONCE) * 128, :],
                key_ref[:, shared],
                value_ref[:, shared],
            ),
        )
    back_query_ref.send()
    back_rank = dot_cols(back_query_ref[...], read_up(up_ref)).astype(BF16)
    sent_ref[...] = back_rank


def terms_body(
    ranks2_ref, ranks1_ref, scale_ref, pull_ref, small0_ref, rank0_ref, gain0_ref, gain_ref, cot_ref,
    up0_ref, hidden_ref, down1_ref, back_query1_ref, attended1_ref, attended0_ref, back_query0_ref,
    a_query1, b_query0, b_query1, a_out0, a_out1, b_out0, b_out1, normed0_ref,
):
    rank_output1, back_rank1, back_output0 = ranks2_ref[0], ranks2_ref[1], ranks2_ref[2]
    rank_output0, rank_query1, back_output1 = ranks1_ref[0], ranks1_ref[1], ranks1_ref[2]
    cot = cot_ref[...]
    write_up(b_out1, dot_rows(rank_output1, cot))
    b_out1.send()
    write_up(b_query1, dot_rows(rank_query1, back_query1_ref[...]))
    b_query1.send()
    write_down(a_out1, dot_rows(back_output1, attended1_ref[...]))
    a_out1.send()
    write_down(a_out0, dot_rows(back_output0, attended0_ref[...]))
    a_out0.send()
    change = dot(rank_output0, read_up(up0_ref))
    gain, scale, pull = gain_ref[...], scale_ref[:, :1], pull_ref[:, :1]
    hidden = hidden_ref[...].astype(F32)
    normed0_ref[...] = (hidden * small0_ref[1, :, :1] * gain0_ref[...]).astype(BF16)
    hidden = hidden + change
    write_down(a_query1, dot_rows(back_rank1, (hidden * scale * gain).astype(BF16)))
    a_query1.send()
    gained = gain * dot_cols(back_rank1, read_down(down1_ref))
    gradient = cot.astype(F32) + scale * gained - hidden * pull
    write_up(b_out0, dot_rows(rank_output0, gradient.astype(BF16)))
    b_out0.send()
    write_up(b_query0, dot_rows(rank0_ref[...], back_query0_ref[...]))


def last_term_body(came_ref, normed_ref, a_query0, back_rank_ref):
    back_rank = total(came_ref).astype(BF16)
    back_rank_ref[...] = back_rank
    back_rank_ref.send()
    write_down(a_query0, dot_rows(back_rank, normed_ref[...]))


def rows_body(
    back_rank_ref, small_ref, gain0_ref, down0_ref, hidden_ref, cot_ref, gain1_ref, scale_ref,
    pull_ref, ranks1_ref, ranks2_ref, up0_ref, down1_ref, up1_ref, out_ref, cot_send_ref,
):
    hidden0 = hidden_ref[...].astype(F32)
    hidden1 = hidden0 + dot(ranks1_ref[0], read_up(up0_ref))
    out_ref[...] = (hidden1 + dot(ranks2_ref[0], read_up(up1_ref))).astype(BF16)
    out_ref.send()
    gained = gain1_ref[...] * dot_cols(ranks2_ref[1], read_down(down1_ref))
    gradient = (
        cot_ref[...].astype(F32) + scale_ref[:, :1] * gained - hidden1 * pull_ref[:, :1]
    )
    back_rank = back_rank_ref[...]
    scale = small_ref[1, :, :1]
    along = row_sum(back_rank.astype(F32) * small_ref[0]) / D
    gained = gain0_ref[...] * dot_cols(back_rank, read_down(down0_ref))
    cot_send_ref[...] = (
        gradient + scale * gained - hidden0 * (scale * scale * scale * along)
    ).astype(BF16)


def swap(value, axis):
    return lax.all_to_all(value, axis, 0, 0, tiled=True)


def on_device(
    arrived, cot_later, q_base, k_base, v_base, gains, parents, a_query, b_query, a_out, b_out
):
    ways = lax.axis_size("tensor")
    count = lax.axis_size("dp")
    rows, width = b_query.shape[1], arrived.shape[1]
    length = rows * width // 128
    heads = width // HEAD_DIM
    block = whole(shape((128, width), BF16))
    layer0, layer1 = [(0,)], [(1,)]
    gain0, gain1 = (gains, [(slice(0, 1),)]), (gains, [(slice(1, 2),)])
    peers = [(tuple(range(ways)),)]

    (shard,) = kernel_call(
        pack_body,
        [(array, [(0,), (1,)]) for array in (a_query, a_out, b_query, b_out)],
        [Near(shape((8, length, 128), BF16), *[(member,) for member in range(8)])],
        0,
    )
    shard = (shard.astype(F32) * SCALE_UP).astype(jnp.float16)
    stack = lax.all_gather(shard, "dp", axis=0, tiled=False)
    stack = (stack.astype(F32) * (1.0 / SCALE_UP)).astype(BF16)

    def factor(*members):
        return (stack, [(ALL, member) for member in members])

    def near_factor(*members):
        return Near(stack, *[(ALL, member) for member in members])

    hidden = from_behind(arrived, "section", 1)
    cot = from_behind(cot_later, "section", -1)
    near_gain0, near_gain1 = Near(gains, (slice(0, 1),)), Near(gains, (slice(1, 2),))
    sent, bias = kernel_call(
        first_body,
        [
            Near(parents.reshape(1, 128)), Near(hidden), Near(cot), near_gain0, near_gain1,
            near_factor(A_QUERY0, A_QUERY1, B_OUT0, B_OUT1),
        ],
        [Near(shape((ways, SQUARES + 48, 128), BF16)), Near(shape((128, 128), F32))],
        6e8,
    )
    first = swap(sent, "tensor")
    sent, attended0, probability, rank_query0, small0, far_small0 = kernel_call(
        layer0_body,
        [
            Near(first), Near(q_base, (0,)), near_factor(B_QUERY0), Near(k_base, (0,)),
            Near(v_base, (0,)), Near(bias), near_factor(A_OUT0),
        ],
        [
            Near(shape((ways, 128, 128), BF16)),
            Near(block[0]),
            Near(shape((heads * 128, 128), F32)),
            whole(shape((128, 128), BF16)),
            Near(shape((3, 128, 128), F32)),
            whole(shape((2, 128, 128), F32)),
        ],
        9e8,
    )
    came = swap(sent, "tensor")
    sent, attended1, back_query1, ranks1, small1, scale1 = kernel_call(
        layer1_body,
        [
            Near(came), Near(first), Near(small0), Near(q_base, (1,)), near_factor(B_QUERY1),
            Near(k_base, (1,)), Near(v_base, (1,)), Near(bias), near_factor(A_OUT1),
        ],
        [
            Near(shape((ways, 256, 128), BF16)),
            Near(block[0]),
            Near(block[0]),
            whole(shape((3, 128, 128), BF16)),
            Near(shape((4, 128, 128), F32)),
            whole(shape((128, 128), F32)),
        ],
        8e8,
    )
    came = swap(sent, "tensor")
    sent, back_query0, ranks2, pull = kernel_call(
        backward0_body,
        [
            Near(came), Near(first), Near(small1), near_factor(A_OUT0), Near(k_base, (0,)),
            Near(v_base, (0,)), Near(probability), near_factor(B_QUERY0),
        ],
        [
            (shape((ways, 128, 128), BF16), peers),
            block,
            whole(shape((3, 128, 128), BF16)),
            whole(shape((128, 128), F32)),
        ],
        4e8,
    )
    came = swap(sent, "tensor")
    term_shape = shape((count, 8, length, 128), BF16)
    made_first = (
        TERM_A_QUERY + 1, TERM_B_QUERY, TERM_B_QUERY + 1, TERM_A_OUT, TERM_A_OUT + 1,
        TERM_B_OUT, TERM_B_OUT + 1,
    )
    terms, normed0 = kernel_call(
        terms_body,
        [
            whole(ranks2), whole(ranks1), whole(scale1), whole(pull), whole(far_small0),
            whole(rank_query0), gain0, gain1, Near(cot), factor(B_OUT0), Near(hidden),
            factor(A_QUERY1), Near(back_query1), Near(attended1), Near(attended0),
            whole(back_query0),
        ],
        [
            (term_shape, [(ALL, member) for member in made_first]),
            Near(block[0]),
        ],
        1e9,
    )
    terms, back_rank0 = kernel_call(
        last_term_body,
        [Near(came), Near(normed0), whole(terms)],
        [(term_shape, [(ALL, TERM_A_QUERY)]), whole(shape((128, 128), BF16))],
        1e8,
        alias=2,
    )
    reduced = lax.psum_scatter(terms, "dp", scatter_dimension=0, tiled=False)
    section_out, cot_send = kernel_call(
        rows_body,
        [
            whole(back_rank0), whole(far_small0), gain0, factor(A_QUERY0), whole(hidden),
            whole(cot), gain1, whole(scale1), whole(pull), whole(ranks1), whole(ranks2),
            factor(B_OUT0, A_QUERY1, B_OUT1),
        ],
        [block, block],
        4e8,
    )
    grads = kernel_call(
        unpack_body,
        [whole(reduced)],
        [
            whole(shape((2, length, 128), F32)),
            whole(shape((2, rows, width), F32)),
            whole(shape((2, length, 128), F32)),
            whole(shape((2, rows, width), F32)),
        ],
        0,
    )
    return (section_out, cot_send, *grads)


def solution(mesh):
    in_specs = (
        P(("section", "dp"), "tensor"),
        P(("section", "dp"), "tensor"),
        P(None, ("section", "dp"), "tensor"),
        P(None, ("section", "dp"), "tensor"),
        P(None, ("section", "dp"), "tensor"),
        P("section", "tensor"),
        P(("section", "dp")),
        P("section", ("tensor", "dp"), None),
        P("section", "dp", "tensor"),
        P("section", ("tensor", "dp"), None),
        P("section", "dp", "tensor"),
    )
    out_specs = (
        P(("section", "dp"), "tensor"),
        P(("section", "dp"), "tensor"),
        P("section", ("tensor", "dp"), None),
        P("section", "dp", "tensor"),
        P("section", ("tensor", "dp"), None),
        P("section", "dp", "tensor"),
    )
    return jax.shard_map(
        on_device, mesh=mesh, in_specs=in_specs, out_specs=out_specs, check_vma=False
    )
```

```python
import jax
import jax.numpy as jnp
from jax import lax
from jax.experimental import pallas as pl
from jax.experimental.pallas import tpu as pltpu
from jax.sharding import PartitionSpec as P

D = 8192
HEAD_DIM = 128
HEADS_AT_ONCE = 8
EPSILON = 1e-05
F32 = jnp.float32
BF16 = jnp.bfloat16
VMEM_LIMIT = 20 << 20
ALL = slice(None)
(A_QUERY0, A_QUERY1, A_OUT0, A_OUT1, B_QUERY0, B_QUERY1, B_OUT0, B_OUT1) = range(8)
PROJECTED0, PROJECTED1, CROSS, BACK_OUTPUT1, HIDDEN_UP, GRAM, BACK_OUTPUT0, SQUARES = range(
    0, 1024, 128
)
SCALE_UP = 65536.0
TERM_A_QUERY, TERM_B_QUERY, TERM_A_OUT, TERM_B_OUT = 0, 2, 4, 6


def from_behind(value, axis, steps):
    count = lax.axis_size(axis)
    pairs = [(source, (source + steps) % count) for source in range(count)]
    return lax.ppermute(value, axis, pairs)


def dot(left, right):
    return jnp.dot(left, right, preferred_element_type=F32)


def dot_rows(left, right):
    return lax.dot_general(left, right, (((0,), (0,)), ((), ())), preferred_element_type=F32)


def dot_cols(left, right):
    return lax.dot_general(left, right, (((1,), (1,)), ((), ())), preferred_element_type=F32)


def row_sum(value):
    return jnp.sum(value, axis=1, keepdims=True)


def shape(dims, dtype):
    return jax.ShapeDtypeStruct(dims, dtype)


class Arriving:
    def __init__(self, copy, ref):
        self.copy, self.ref, self.waited = copy, ref, False
        self.shape = ref.shape

    def wait(self):
        if not self.waited:
            self.copy.wait()
            self.waited = True

    def __getitem__(self, at):
        self.wait()
        return self.ref[at]


class Leaving:
    def __init__(self, copies, ref):
        self.copies, self.ref, self.sent = copies, ref, False
        self.shape = ref.shape

    def send(self):
        if not self.sent:
            for copy in self.copies:
                copy.start()
            self.sent = True

    def __setitem__(self, at, value):
        self.ref[at] = value

    def __getitem__(self, at):
        return self.ref[at]


class Staying:
    def __init__(self, ref):
        self.ref = ref
        self.shape = ref.shape

    def send(self):
        pass

    def __setitem__(self, at, value):
        self.ref[at] = value

    def __getitem__(self, at):
        return self.ref[at]


def sliced(dims, at):
    at = at + (ALL,) * (len(dims) - len(at))
    result = []
    for size, entry in zip(dims, at, strict=True):
        if isinstance(entry, slice):
            result.append(len(range(*entry.indices(size))))
    return tuple(result)


class Near:
    def __init__(self, array, *slices):
        self.array, self.slices = array, slices


def kernel_call(body, ins, outs, flops, alias=None):
    hbm, vmem = pl.BlockSpec(memory_space=pltpu.HBM), pl.BlockSpec(memory_space=pltpu.VMEM)
    scratch, marks_needed, in_count, out_count = [], 0, len(ins), len(outs)
    for index, item in enumerate(ins):
        if index != alias and not isinstance(item, Near):
            scratch += [pltpu.VMEM(sliced(item[0].shape, at), item[0].dtype) for at in item[1]]
            marks_needed += len(item[1])
    for item in outs:
        if not isinstance(item, Near):
            for at in item[1]:
                copies = at[0] if isinstance(at[0], tuple) else (at[0],)
                marks_needed += len(copies)
                scratch.append(
                    pltpu.VMEM(sliced(item[0].shape, (copies[0], *at[1:])), item[0].dtype)
                )

    def run(*refs):
        in_refs, out_refs = refs[:in_count], refs[in_count : in_count + out_count]
        places, marks = refs[in_count + out_count : -1], refs[-1]
        used, mark, given, arriving, leaving = 0, 0, [], [], []
        for index, (ref, item) in enumerate(zip(in_refs, ins, strict=True)):
            if index == alias:
                continue
            if isinstance(item, Near):
                given += [ref.at[at] for at in item.slices] if item.slices else [ref]
                continue
            for at in item[1]:
                copy = pltpu.make_async_copy(ref.at[at], places[used], marks.at[mark])
                copy.start()
                arriving.append(Arriving(copy, places[used]))
                given.append(arriving[-1])
                used, mark = used + 1, mark + 1
        for ref, item in zip(out_refs, outs, strict=True):
            if isinstance(item, Near):
                given += [Staying(ref.at[at]) for at in item.slices] or [Staying(ref)]
                continue
            for at in item[1]:
                copies = []
                for first in at[0] if isinstance(at[0], tuple) else (at[0],):
                    copies.append(
                        pltpu.make_async_copy(
                            places[used], ref.at[(first, *at[1:])], marks.at[mark]
                        )
                    )
                    mark += 1
                leaving.append(Leaving(copies, places[used]))
                given.append(leaving[-1])
                used += 1
        body(*given)
        for item in leaving:
            item.send()
        for item in arriving:
            item.wait()
        for item in leaving:
            for copy in item.copies:
                copy.wait()

    arrays = [item.array if isinstance(item, Near) else item[0] for item in ins]
    shapes = [item.array if isinstance(item, Near) else item[0] for item in outs]
    size = sum(x.size * x.dtype.itemsize for x in (*arrays, *shapes))
    return pl.pallas_call(
        run,
        out_shape=[
            result if isinstance(item, Near) else pltpu.HBM(result.shape, result.dtype)
            for result, item in zip(shapes, outs, strict=True)
        ],
        in_specs=[vmem if isinstance(item, Near) else hbm for item in ins],
        out_specs=[vmem if isinstance(item, Near) else hbm for item in outs],
        scratch_shapes=[*scratch, pltpu.SemaphoreType.DMA((max(marks_needed, 1),))],
        input_output_aliases={} if alias is None else {alias: 0},
        compiler_params=pltpu.CompilerParams(vmem_limit_bytes=VMEM_LIMIT),
        cost_estimate=pl.CostEstimate(flops=int(flops), bytes_accessed=size, transcendentals=0),
    )(
        *(
            array
            if isinstance(item, Near)
            else pltpu.with_memory_space_constraint(array, pltpu.HBM)
            for array, item in zip(arrays, ins, strict=True)
        )
    )


def whole(value):
    return (value, [(ALL,) * len(value.shape)])


def read_down(ref):
    return ref[...].reshape(-1, 128)


def read_up(ref):
    count, length, _ = ref.shape
    rows = 128 // count
    columns = []
    for pair in range(length // (2 * rows)):
        slab = ref[:, pair * 2 * rows : (pair + 1) * 2 * rows, :].astype(F32)
        for half in range(2):
            columns.append(
                slab[:, half * rows : (half + 1) * rows, :].reshape(128, 128).astype(BF16)
            )
    return jnp.concatenate(columns, axis=1)


def write_down(ref, value):
    value = value.astype(BF16)
    size = ref.shape[2] * ref.shape[1] // 128
    for place in range(ref.shape[0]):
        for part in range(size // 128):
            at = place * size + part * 128
            ref[place, part * 128 : (part + 1) * 128, :] = value[:, at : at + 128]


def write_up(ref, value):
    count, length, _ = ref.shape
    rows = 128 // count
    for pair in range(length // (2 * rows)):
        halves = [
            value[:, (2 * pair + half) * 128 : (2 * pair + half + 1) * 128].reshape(
                count, rows, 128
            )
            for half in range(2)
        ]
        ref[:, pair * 2 * rows : (pair + 1) * 2 * rows, :] = jnp.concatenate(
            halves, axis=1
        ).astype(BF16)


def pack_body(*refs):
    downs, ups, targets = refs[:4], refs[4:8], refs[8:16]
    for ref, target in zip(downs, targets[:4], strict=True):
        target[...] = ref[...]
    for ref, target in zip(ups, targets[4:], strict=True):
        rows, width = ref.shape
        value = ref[...].astype(F32)
        for pair in range(width // 256):
            halves = [
                value[:, (2 * pair + half) * 128 : (2 * pair + half + 1) * 128]
                for half in range(2)
            ]
            target[pair * 2 * rows : (pair + 1) * 2 * rows, :] = jnp.concatenate(
                halves, axis=0
            ).astype(BF16)


def unpack_body(came, a_query_ref, b_query_ref, a_out_ref, b_out_ref):
    for layer in range(2):
        for ref, place in ((a_query_ref, TERM_A_QUERY), (a_out_ref, TERM_A_OUT)):
            value = came[place + layer].astype(F32)
            for part in range(value.shape[0] // 128):
                at = slice(part * 128, (part + 1) * 128)
                ref[layer, at, :] = jnp.transpose(value[at])
        for ref, place in ((b_query_ref, TERM_B_QUERY), (b_out_ref, TERM_B_OUT)):
            rows, width = ref.shape[1:]
            value = came[place + layer].astype(F32)
            for tile in range(width // 128):
                ref[layer, :, tile * 128 : (tile + 1) * 128] = value[
                    tile * rows : (tile + 1) * rows
                ]


def first_body(
    parent_ref, hidden_ref, cot_ref, gain0_ref, gain1_ref, down0_ref, down1_ref, up0_ref, up1_ref,
    sent_ref, bias_ref,
):
    lane = lax.broadcasted_iota(jnp.int32, (128, 128), 1)
    line = lax.broadcasted_iota(jnp.int32, (128, 128), 0)
    linked = (lane == line) | (jnp.broadcast_to(parent_ref[...], (128, 128)) == line)
    reached = jnp.where(linked, 1.0, 0.0).astype(BF16)
    for _ in range(7):
        reached = jnp.minimum(dot(reached, reached), 1.0).astype(BF16)
    bias_ref[...] = jnp.where(jnp.transpose(reached.astype(F32)) > 0.5, 0.0, -1e30)
    def send(start, value):
        value = value.astype(BF16)
        for peer in range(sent_ref.shape[0]):
            sent_ref[peer, start : start + value.shape[0], :] = value

    hidden, gain1 = hidden_ref[...], gain1_ref[...]
    wide = hidden.astype(F32)
    down1, up0, cot = read_down(down1_ref), read_up(up0_ref), cot_ref[...]
    send(PROJECTED0, dot((wide * gain0_ref[...]).astype(BF16), read_down(down0_ref)))
    send(PROJECTED1, dot((wide * gain1).astype(BF16), down1))
    send(CROSS, dot((up0.astype(F32) * gain1).astype(BF16), down1))
    send(BACK_OUTPUT1, dot_cols(cot, read_up(up1_ref)))
    send(HIDDEN_UP, dot_cols(hidden, up0))
    send(GRAM, dot_cols(up0, up0))
    send(BACK_OUTPUT0, dot_cols(cot, up0))
    squares = lax.dot_general(
        jnp.ones((16, hidden.shape[1]), F32),
        wide * wide,
        (((1,), (1,)), ((), ())),
        preferred_element_type=F32,
        precision=lax.Precision.HIGHEST,
    )
    high = squares.astype(BF16)
    rest = squares - high.astype(F32)
    middle = rest.astype(BF16)
    send(SQUARES, high)
    send(SQUARES + 16, middle)
    send(SQUARES + 32, rest - middle.astype(F32))


def to_column(row):
    lane = lax.broadcasted_iota(jnp.int32, (128, 128), 1)
    line = lax.broadcasted_iota(jnp.int32, (128, 128), 0)
    return row_sum(jnp.where(lane == line, jnp.broadcast_to(row, (128, 128)), 0.0))


def total(ref, start=0, rows=128):
    value = ref[0, start : start + rows, :].astype(F32)
    for peer in range(1, ref.shape[0]):
        value = value + ref[peer, start : start + rows, :].astype(F32)
    return value


def head_blocks(query_ref, key_ref):
    heads = query_ref.shape[-1] // HEAD_DIM
    groups = key_ref.shape[-1] // HEAD_DIM
    share = heads // groups
    return [
        (head, slice((head // share) * HEAD_DIM, (head // share + 1) * HEAD_DIM))
        for head in range(0, heads, HEADS_AT_ONCE)
    ]


def stacked(value, head):
    return jnp.concatenate(
        [
            value[:, (head + k) * HEAD_DIM : (head + k + 1) * HEAD_DIM]
            for k in range(HEADS_AT_ONCE)
        ],
        axis=0,
    )


def spread(ref, head, value):
    for k in range(HEADS_AT_ONCE):
        ref[:, (head + k) * HEAD_DIM : (head + k + 1) * HEAD_DIM] = value[k * 128 : (k + 1) * 128]


def softmax_of(queries, keys, bias):
    scores = dot_cols(queries, keys) * HEAD_DIM ** (-0.5) + bias
    weights = jnp.exp(scores - jnp.max(scores, axis=1, keepdims=True))
    return weights * (1.0 / row_sum(weights))


def score_back(back_attended, probability, keys, values):
    back_probability = dot_cols(back_attended, values)
    back_scores = probability * (back_probability - row_sum(probability * back_probability))
    return (dot(back_scores.astype(BF16), keys) * HEAD_DIM ** (-0.5)).astype(BF16)


def layer0_body(
    came_ref, query_ref, up_query_ref, key_ref, value_ref, bias_ref, down_output_ref,
    sent_ref, attended_ref, probability_ref, rank_ref, small_ref, far_small_ref,
):
    projected = total(came_ref, PROJECTED0)
    squares = to_column(
        (
            total(came_ref, SQUARES, 16)
            + total(came_ref, SQUARES + 16, 16)
            + total(came_ref, SQUARES + 32, 16)
        )[:1]
    )
    scale = lax.rsqrt(squares / D + EPSILON)
    rank_query = (scale * projected).astype(BF16)
    rank_ref[...] = rank_query
    small_ref[0] = projected
    small_ref[1] = jnp.broadcast_to(scale, (128, 128))
    small_ref[2] = jnp.broadcast_to(squares, (128, 128))
    far_small_ref[0] = projected
    far_small_ref[1] = jnp.broadcast_to(scale, (128, 128))
    rank_ref.send()
    far_small_ref.send()
    bias = jnp.concatenate([bias_ref[...]] * HEADS_AT_ONCE, axis=0)
    queries = (query_ref[...].astype(F32) + dot(rank_query, read_up(up_query_ref))).astype(BF16)
    for head, shared in head_blocks(query_ref, key_ref):
        probability = softmax_of(stacked(queries, head), key_ref[:, shared], bias)
        probability_ref[head * 128 : (head + HEADS_AT_ONCE) * 128, :] = probability
        spread(
            attended_ref, head, dot(probability.astype(BF16), value_ref[:, shared]).astype(BF16)
        )
    probability_ref.send()
    attended_ref.send()
    rank_output = dot(attended_ref[...], read_down(down_output_ref)).astype(BF16)
    for peer in range(sent_ref.shape[0]):
        sent_ref[peer] = rank_output


def layer1_body(
    came_ref, first_ref, small0_ref, query_ref, up_ref, key_ref, value_ref, bias_ref, down_ref,
    sent_ref, attended_ref, back_query_ref, ranks_ref, small_ref, scale_ref,
):
    rank_output0 = total(came_ref).astype(BF16)
    cross = total(first_ref, CROSS)
    projected = total(first_ref, PROJECTED1) + dot(rank_output0, cross.astype(BF16))
    back_rank_output = total(first_ref, BACK_OUTPUT1).astype(BF16)
    hidden_up = total(first_ref, HIDDEN_UP)
    gram = total(first_ref, GRAM)
    gram_high = gram.astype(BF16)
    gram_low = (gram - gram_high.astype(F32)).astype(BF16)
    output_gram = dot(rank_output0, gram_high) + dot(rank_output0, gram_low)
    squares = small0_ref[2, :, :1] + row_sum(
        rank_output0.astype(F32) * (2.0 * hidden_up + output_gram)
    )
    scale = lax.rsqrt(jnp.maximum(squares, 0.0) / D + EPSILON)
    rank_query = (scale * projected).astype(BF16)
    ranks_ref[0] = rank_output0
    ranks_ref[1] = rank_query
    ranks_ref[2] = back_rank_output
    ranks_ref.send()
    small_ref[0] = projected
    small_ref[1] = jnp.broadcast_to(scale, (128, 128))
    small_ref[2] = cross
    small_ref[3] = hidden_up + output_gram
    scale_ref[...] = jnp.broadcast_to(scale, (128, 128))
    scale_ref.send()
    bias = jnp.concatenate([bias_ref[...]] * HEADS_AT_ONCE, axis=0)
    up_query = read_up(up_ref)
    queries = (query_ref[...].astype(F32) + dot(rank_query, up_query)).astype(BF16)
    down_output = read_down(down_ref)
    back_attended = dot_cols(back_rank_output, down_output).astype(BF16)
    for head, shared in head_blocks(query_ref, key_ref):
        keys, values = key_ref[:, shared], value_ref[:, shared]
        probability = softmax_of(stacked(queries, head), keys, bias)
        spread(attended_ref, head, dot(probability.astype(BF16), values).astype(BF16))
        spread(
            back_query_ref, head, score_back(stacked(back_attended, head), probability, keys, values)
        )
    attended_ref.send()
    back_query_ref.send()
    rank_output = dot(attended_ref[...], down_output).astype(BF16)
    back_rank = dot_cols(back_query_ref[...], up_query).astype(BF16)
    for peer in range(sent_ref.shape[0]):
        sent_ref[peer, :128, :] = rank_output
        sent_ref[peer, 128:, :] = back_rank


def backward0_body(
    came_ref, first_ref, small_ref, down_ref, key_ref, value_ref, probability_ref, up_ref,
    sent_ref, back_query_ref, ranks_ref, pull_ref,
):
    back_rank1 = total(came_ref, 128).astype(BF16)
    scale = small_ref[1, :, :1]
    along = row_sum(back_rank1.astype(F32) * small_ref[0]) / D
    pull = scale * scale * scale * along
    back_output = (
        total(first_ref, BACK_OUTPUT0)
        + scale * dot_cols(back_rank1, small_ref[2].astype(BF16))
        - pull * small_ref[3]
    ).astype(BF16)
    ranks_ref[0] = total(came_ref).astype(BF16)
    ranks_ref[1] = back_rank1
    ranks_ref[2] = back_output
    ranks_ref.send()
    pull_ref[...] = jnp.broadcast_to(pull, (128, 128))
    pull_ref.send()
    back_attended = dot_cols(back_output, read_down(down_ref)).astype(BF16)
    for head, shared in head_blocks(back_query_ref, key_ref):
        spread(
            back_query_ref,
            head,
            score_back(
                stacked(back_attended, head),
                probability_ref[head * 128 : (head + HEADS_AT_ONCE) * 128, :],
                key_ref[:, shared],
                value_ref[:, shared],
            ),
        )
    back_query_ref.send()
    back_rank = dot_cols(back_query_ref[...], read_up(up_ref)).astype(BF16)
    sent_ref[...] = back_rank


def terms_body(
    ranks2_ref, ranks1_ref, scale_ref, pull_ref, small0_ref, rank0_ref, gain0_ref, gain_ref, cot_ref,
    up0_ref, hidden_ref, down1_ref, back_query1_ref, attended1_ref, attended0_ref, back_query0_ref,
    a_query1, b_query0, b_query1, a_out0, a_out1, b_out0, b_out1, normed0_ref,
):
    rank_output1, back_rank1, back_output0 = ranks2_ref[0], ranks2_ref[1], ranks2_ref[2]
    rank_output0, rank_query1, back_output1 = ranks1_ref[0], ranks1_ref[1], ranks1_ref[2]
    cot = cot_ref[...]
    write_up(b_out1, dot_rows(rank_output1, cot))
    b_out1.send()
    write_up(b_query1, dot_rows(rank_query1, back_query1_ref[...]))
    b_query1.send()
    write_down(a_out1, dot_rows(back_output1, attended1_ref[...]))
    a_out1.send()
    write_down(a_out0, dot_rows(back_output0, attended0_ref[...]))
    a_out0.send()
    change = dot(rank_output0, read_up(up0_ref))
    gain, scale, pull = gain_ref[...], scale_ref[:, :1], pull_ref[:, :1]
    hidden = hidden_ref[...].astype(F32)
    normed0_ref[...] = (hidden * small0_ref[1, :, :1] * gain0_ref[...]).astype(BF16)
    hidden = hidden + change
    write_down(a_query1, dot_rows(back_rank1, (hidden * scale * gain).astype(BF16)))
    a_query1.send()
    gained = gain * dot_cols(back_rank1, read_down(down1_ref))
    gradient = cot.astype(F32) + scale * gained - hidden * pull
    write_up(b_out0, dot_rows(rank_output0, gradient.astype(BF16)))
    b_out0.send()
    write_up(b_query0, dot_rows(rank0_ref[...], back_query0_ref[...]))


def last_term_body(came_ref, normed_ref, a_query0, back_rank_ref):
    back_rank = total(came_ref).astype(BF16)
    back_rank_ref[...] = back_rank
    back_rank_ref.send()
    write_down(a_query0, dot_rows(back_rank, normed_ref[...]))


def rows_body(
    back_rank_ref, small_ref, gain0_ref, down0_ref, hidden_ref, cot_ref, gain1_ref, scale_ref,
    pull_ref, ranks1_ref, ranks2_ref, up0_ref, down1_ref, up1_ref, out_ref, cot_send_ref,
):
    hidden0 = hidden_ref[...].astype(F32)
    hidden1 = hidden0 + dot(ranks1_ref[0], read_up(up0_ref))
    out_ref[...] = (hidden1 + dot(ranks2_ref[0], read_up(up1_ref))).astype(BF16)
    out_ref.send()
    gained = gain1_ref[...] * dot_cols(ranks2_ref[1], read_down(down1_ref))
    gradient = (
        cot_ref[...].astype(F32) + scale_ref[:, :1] * gained - hidden1 * pull_ref[:, :1]
    )
    back_rank = back_rank_ref[...]
    scale = small_ref[1, :, :1]
    along = row_sum(back_rank.astype(F32) * small_ref[0]) / D
    gained = gain0_ref[...] * dot_cols(back_rank, read_down(down0_ref))
    cot_send_ref[...] = (
        gradient + scale * gained - hidden0 * (scale * scale * scale * along)
    ).astype(BF16)


def swap(value, axis):
    return lax.all_to_all(value, axis, 0, 0, tiled=True)


def on_device(
    arrived, cot_later, q_base, k_base, v_base, gains, parents, a_query, b_query, a_out, b_out
):
    ways = lax.axis_size("tensor")
    count = lax.axis_size("dp")
    rows, width = b_query.shape[1], arrived.shape[1]
    length = rows * width // 128
    heads = width // HEAD_DIM
    block = whole(shape((128, width), BF16))
    layer0, layer1 = [(0,)], [(1,)]
    gain0, gain1 = (gains, [(slice(0, 1),)]), (gains, [(slice(1, 2),)])
    peers = [(tuple(range(ways)),)]

    (shard,) = kernel_call(
        pack_body,
        [(array, [(0,), (1,)]) for array in (a_query, a_out, b_query, b_out)],
        [Near(shape((8, length, 128), BF16), *[(member,) for member in range(8)])],
        0,
    )
    shard = (shard.astype(F32) * SCALE_UP).astype(jnp.float16)
    stack = lax.all_gather(shard, "dp", axis=0, tiled=False)
    stack = (stack.astype(F32) * (1.0 / SCALE_UP)).astype(BF16)

    def factor(*members):
        return (stack, [(ALL, member) for member in members])

    def near_factor(*members):
        return Near(stack, *[(ALL, member) for member in members])

    hidden = from_behind(arrived, "section", 1)
    cot = from_behind(cot_later, "section", -1)
    near_gain0, near_gain1 = Near(gains, (slice(0, 1),)), Near(gains, (slice(1, 2),))
    sent, bias = kernel_call(
        first_body,
        [
            Near(parents.reshape(1, 128)), Near(hidden), Near(cot), near_gain0, near_gain1,
            near_factor(A_QUERY0, A_QUERY1, B_OUT0, B_OUT1),
        ],
        [Near(shape((ways, SQUARES + 48, 128), BF16)), Near(shape((128, 128), F32))],
        6e8,
    )
    first = swap(sent, "tensor")
    sent, attended0, probability, rank_query0, small0, far_small0 = kernel_call(
        layer0_body,
        [
            Near(first), Near(q_base, (0,)), near_factor(B_QUERY0), Near(k_base, (0,)),
            Near(v_base, (0,)), Near(bias), near_factor(A_OUT0),
        ],
        [
            Near(shape((ways, 128, 128), BF16)),
            Near(block[0]),
            Near(shape((heads * 128, 128), F32)),
            whole(shape((128, 128), BF16)),
            Near(shape((3, 128, 128), F32)),
            whole(shape((2, 128, 128), F32)),
        ],
        9e8,
    )
    came = swap(sent, "tensor")
    sent, attended1, back_query1, ranks1, small1, scale1 = kernel_call(
        layer1_body,
        [
            Near(came), Near(first), Near(small0), Near(q_base, (1,)), near_factor(B_QUERY1),
            Near(k_base, (1,)), Near(v_base, (1,)), Near(bias), near_factor(A_OUT1),
        ],
        [
            Near(shape((ways, 256, 128), BF16)),
            Near(block[0]),
            Near(block[0]),
            whole(shape((3, 128, 128), BF16)),
            Near(shape((4, 128, 128), F32)),
            whole(shape((128, 128), F32)),
        ],
        8e8,
    )
    came = swap(sent, "tensor")
    sent, back_query0, ranks2, pull = kernel_call(
        backward0_body,
        [
            Near(came), Near(first), Near(small1), near_factor(A_OUT0), Near(k_base, (0,)),
            Near(v_base, (0,)), Near(probability), near_factor(B_QUERY0),
        ],
        [
            (shape((ways, 128, 128), BF16), peers),
            block,
            whole(shape((3, 128, 128), BF16)),
            whole(shape((128, 128), F32)),
        ],
        4e8,
    )
    came = swap(sent, "tensor")
    term_shape = shape((count, 8, length, 128), BF16)
    made_first = (
        TERM_A_QUERY + 1, TERM_B_QUERY, TERM_B_QUERY + 1, TERM_A_OUT, TERM_A_OUT + 1,
        TERM_B_OUT, TERM_B_OUT + 1,
    )
    terms, normed0 = kernel_call(
        terms_body,
        [
            whole(ranks2), whole(ranks1), whole(scale1), whole(pull), whole(far_small0),
            whole(rank_query0), gain0, gain1, Near(cot), factor(B_OUT0), Near(hidden),
            factor(A_QUERY1), Near(back_query1), Near(attended1), Near(attended0),
            whole(back_query0),
        ],
        [
            (term_shape, [(ALL, member) for member in made_first]),
            Near(block[0]),
        ],
        1e9,
    )
    terms, back_rank0 = kernel_call(
        last_term_body,
        [Near(came), Near(normed0), whole(terms)],
        [(term_shape, [(ALL, TERM_A_QUERY)]), whole(shape((128, 128), BF16))],
        1e8,
        alias=2,
    )
    reduced = lax.psum_scatter(terms, "dp", scatter_dimension=0, tiled=False)
    section_out, cot_send = kernel_call(
        rows_body,
        [
            whole(back_rank0), whole(far_small0), gain0, factor(A_QUERY0), whole(hidden),
            whole(cot), gain1, whole(scale1), whole(pull), whole(ranks1), whole(ranks2),
            factor(B_OUT0, A_QUERY1, B_OUT1),
        ],
        [block, block],
        4e8,
    )
    grads = kernel_call(
        unpack_body,
        [whole(reduced)],
        [
            whole(shape((2, length, 128), F32)),
            whole(shape((2, rows, width), F32)),
            whole(shape((2, length, 128), F32)),
            whole(shape((2, rows, width), F32)),
        ],
        0,
    )
    return (section_out, cot_send, *grads)


def solution(mesh):
    in_specs = (
        P(("section", "dp"), "tensor"),
        P(("section", "dp"), "tensor"),
        P(None, ("section", "dp"), "tensor"),
        P(None, ("section", "dp"), "tensor"),
        P(None, ("section", "dp"), "tensor"),
        P("section", "tensor"),
        P(("section", "dp")),
        P("section", ("tensor", "dp"), None),
        P("section", "dp", "tensor"),
        P("section", ("tensor", "dp"), None),
        P("section", "dp", "tensor"),
    )
    out_specs = (
        P(("section", "dp"), "tensor"),
        P(("section", "dp"), "tensor"),
        P("section", ("tensor", "dp"), None),
        P("section", "dp", "tensor"),
        P("section", ("tensor", "dp"), None),
        P("section", "dp", "tensor"),
    )
    return jax.shard_map(
        on_device, mesh=mesh, in_specs=in_specs, out_specs=out_specs, check_vma=False
    )
```
